32 devices in a mesh: dp: 4 (over y, x), wide: 8 (over z, core).
Axes of the slice: x: 2, y: 2, z: 4, core: 2. Of those that a mesh axis runs over, the one named last changes fastest.
Arguments:
- tokens: bfloat16 [36864, 768], P(('dp', 'wide')), may hold values from -6 to 6
- pos_index: int32 [36864, 2], P(('dp', 'wide')), may hold values from 0 to 196
- size_group: int32 [224], P(('dp', 'wide')), may hold values from 0 to 3, as said below
- pos_table: bfloat16 [197, 768], replicated, may hold values from -3 to 3
- prompts: float32 [50, 768], replicated, may hold values from -6 to 6
- norm_gains: float32 [2, 768], replicated, may hold values from 0.5 to 1.5
- w_qkv: bfloat16 [768, 2304], P('wide'), may hold values from -0.21875 to 0.21875
- w_out: bfloat16 [768, 768], P('wide'), may hold values from -1.75 to 1.75
- w_up: bfloat16 [768, 3072], P('wide'), may hold values from -0.21875 to 0.21875
- w_down: bfloat16 [3072, 768], P('wide'), may hold values from -0.109375 to 0.109375
- cotangent: bfloat16 [36864, 768], P(('dp', 'wide')), may hold values from -6 to 6
Outputs:
- outputs: bfloat16 [36864, 768], P(('dp', 'wide'))
- input_grad: bfloat16 [36864, 768], P(('dp', 'wide'))
- prompt_grad: float32 [50, 768], replicated
- penalty: float32 [], replicated
The draws below stay inside these ranges and needn't reach their ends.
Inputs may be any that keep to these rules, and one draw needn't show every extreme that they name: `size_group`: 0, 1, 2 name images of 100, 196, 576 patches, 3 an empty slot; the images of one device's 7 slots take at most 1139 of its 1152 rows, and the last device's take exactly that.
All inputs are finite; a program needn't handle non-finite values.
Results may differ from the reference program's by a relative error of at most 0.013.
Values may be sent and summed in bfloat16 or wider, within the bound.
A program may use at most 192 MiB of HBM per device.

```python
import jax
import jax.numpy as jnp
import numpy as np
from jax import lax

D = 768
HEADS = 12
HEAD_DIM = 64
FF = 3072
PROMPTS = 50
PATCH_S = 100
PATCH_M = 196
PATCH_L = 576
POSN = 197
TOK_DEV = 1152
IMG_DEV = 7
TOKENS = 36864
IMAGES = 224


menu_table = np.array([[[0, 3, 3, 3, 3, 3, 3], [1, 3, 3, 3, 3, 3, 3], [0, 0, 3, 3, 3, 3, 3], [1, 0, 3, 3, 3, 3, 3]], [[2, 3, 3, 3, 3, 3, 3], [1, 1, 3, 3, 3, 3, 3], [2, 0, 3, 3, 3, 3, 3], [1, 1, 0, 3, 3, 3, 3]], [[2, 1, 3, 3, 3, 3, 3], [2, 0, 0, 3, 3, 3, 3], [1, 1, 1, 3, 3, 3, 3], [1, 1, 0, 0, 3, 3, 3]], [[2, 1, 1, 3, 3, 3, 3], [2, 1, 0, 3, 3, 3, 3], [0, 0, 0, 0, 0, 0, 0], [1, 1, 1, 0, 0, 3, 3]]], dtype=np.int32)


fullest_row = np.array([1, 1, 1, 1, 0, 3, 3], dtype=np.int32)


def draw_size_group(key, part):
    device_total = IMAGES // IMG_DEV
    first, second = jax.random.split(jax.random.fold_in(key, 11))
    tiers = jnp.arange(device_total, dtype=jnp.int32) * 4 // device_total
    combos = jax.random.randint(first, (device_total,), 0, 4)
    picked = jnp.asarray(menu_table)[tiers, combos]
    picked = picked.at[device_total - 1].set(jnp.asarray(fullest_row))
    orders = jax.vmap(lambda k: jax.random.permutation(k, IMG_DEV))(jax.random.split(second, device_total))
    return jnp.take_along_axis(picked, orders, axis=1).reshape(-1).astype(jnp.int32)


def place_ends(result, key, least, largest):
    spot = [jax.random.randint(jax.random.fold_in(key, axis), (), 0, length) for axis, length in enumerate(result.shape)]
    longest = result.shape.index(max(result.shape))
    beside = spot[:longest] + [(spot[longest] + 1) % result.shape[longest]] + spot[longest + 1:]
    return result.at[tuple(spot)].set(least).at[tuple(beside)].set(largest)


def level_of(own_key, dims, cuts, smallest, largest):
    level = 1.0
    for dim, parts in cuts:
        steps = jax.random.uniform(jax.random.fold_in(jax.random.fold_in(own_key, 6), dim), (parts,), jnp.float32, smallest / len(cuts), largest / len(cuts))
        level = level * jnp.repeat(jnp.exp(steps), dims[dim] // parts).reshape((-1,) + (1,) * (len(dims) - 1 - dim))
    return level


def centred(stream_key, dims, scale, reach, cuts=(), held_as=jnp.bfloat16):
    level = level_of(stream_key, dims, cuts, -0.22, 0.18) if cuts else 1.0
    values = jax.random.normal(stream_key, dims, jnp.float32) * scale * level
    return jnp.minimum(jnp.maximum(values, -reach), reach).astype(held_as)


def setup_inputs(seed: int = 0) -> dict:
    key_list = jax.random.split(jax.random.key(seed), 12)
    return {
        "tokens": centred(key_list[0], (TOKENS, D), 1.0, 6.0, ((0, 32),)),
        "pos_index": place_ends(jax.random.randint(key_list[1], (TOKENS, 2), 0, POSN), jax.random.fold_in(key_list[1], 1), 0, POSN - 1).astype(jnp.int32),
        "size_group": draw_size_group(jax.random.fold_in(key_list[11], 71), 0),
        "pos_table": centred(key_list[3], (POSN, D), 0.5, 3.0),
        "prompts": centred(key_list[4], (PROMPTS, D), 1.0, 6.0, (), jnp.float32),
        "norm_gains": jnp.clip(1.0 + 0.1 * jax.random.normal(key_list[5], (2, D), jnp.float32), 0.5, 1.5),
        "w_qkv": centred(key_list[6], (D, 3 * D), D ** -0.5, 0.21875, ((0, 8),)),
        "w_out": centred(key_list[7], (D, D), (D // 64) ** -0.5, 1.75, ((0, 8),)),
        "w_up": centred(key_list[8], (D, FF), D ** -0.5, 0.21875, ((0, 8),)),
        "w_down": centred(key_list[9], (FF, D), FF ** -0.5, 0.109375, ((0, 8),)),
        "cotangent": centred(key_list[10], (TOKENS, D), 1.0, 6.0, ((0, 32),)),
    }


@jax.custom_vjp
def low(v):
    return lax.optimization_barrier(v.astype(jnp.bfloat16)).astype(jnp.float32)

@jax.custom_vjp
def low_back(v):
    return v

def low_keep(v):
    return (low(v), None)

def low_pass(kept, grad):
    return (grad,)

def back_keep(v):
    return (v, None)

def back_low(kept, grad):
    return (low(grad),)
low.defvjp(low_keep, low_pass)
low_back.defvjp(back_keep, back_low)
EPSILON = 1e-06
PENALTY_RATE = 3e-05

def layout(groups):
    patches = jnp.where(groups == 0, PATCH_S, jnp.where(groups == 1, PATCH_M, PATCH_L))
    lengths = jnp.where(groups == 3, 0, 1 + PROMPTS + patches).astype(jnp.int32)
    starts = (jnp.cumsum(lengths) - lengths).astype(jnp.int32)
    row_ids = jnp.arange(TOK_DEV, dtype=jnp.int32)
    inside = (row_ids[None, :] >= starts[:, None]) & (row_ids[None, :] < (starts + lengths)[:, None])
    slot_number = jnp.arange(IMG_DEV, dtype=jnp.int32)
    segment = (lax.optimization_barrier(jnp.sum(jnp.where(inside, slot_number[:, None] + 1, 0), axis=0)) - 1).astype(jnp.int32)
    position = (row_ids - lax.optimization_barrier(jnp.sum(jnp.where(inside, starts[:, None], 0), axis=0))).astype(jnp.int32)
    live_rows = segment >= 0
    prompt_slot = jnp.where(live_rows & (position >= 1) & (position <= PROMPTS), position - 1, -1).astype(jnp.int32)
    return (segment, prompt_slot, live_rows, lengths)

def layer_norm(values, gain):
    centered = values - lax.optimization_barrier(jnp.mean(values, axis=-1, keepdims=True))
    return centered * lax.rsqrt(lax.optimization_barrier(jnp.mean(centered * centered, axis=-1, keepdims=True)) + EPSILON) * gain

def forward_buffer(field_in, indices, segment, prompt_slot, live_rows, prompts, pos_rows, norm_gains, w_qkv, w_out, w_up, w_down):
    highest = lax.Precision.HIGHEST
    pos_shift = 0.5 * (jnp.take(pos_rows, indices[:, 0], axis=0) + jnp.take(pos_rows, indices[:, 1], axis=0))
    chosen = jnp.take(prompts, jnp.maximum(prompt_slot, 0), axis=0)
    hidden_in = jnp.where((prompt_slot >= 0)[:, None], chosen, field_in + pos_shift)
    normed = low(layer_norm(hidden_in, norm_gains[0]))
    joint_qkv = low(low_back(jnp.dot(normed, w_qkv, precision=highest)))
    joint_qkv = joint_qkv.reshape(TOK_DEV, 3, HEADS, HEAD_DIM)
    scores = low_back(jnp.einsum('qhd,khd->hqk', joint_qkv[:, 0], joint_qkv[:, 1], precision=highest) * HEAD_DIM ** (-0.5))
    same_image = segment[:, None] == segment[None, :]
    scores = jnp.where(same_image[None], scores, -1e+30)
    attn_probs = jax.nn.softmax(scores, axis=-1)
    mixed_heads = jnp.einsum('hqk,khd->qhd', low(attn_probs), joint_qkv[:, 2], precision=highest).reshape(TOK_DEV, D)
    mixed_heads = low(low_back(mixed_heads))
    middle = hidden_in + low_back(jnp.dot(mixed_heads, w_out, precision=highest))
    second = low(layer_norm(middle, norm_gains[1]))
    inner_act = low_back(jnp.dot(second, w_up, precision=highest))
    activated = low(jax.nn.gelu(inner_act, approximate=False))
    return (middle + jnp.dot(activated, w_down, precision=highest)) * live_rows[:, None].astype(jnp.float32)

def reference(tokens, pos_index, size_group, pos_table, prompts, norm_gains, w_qkv, w_out, w_up, w_down, cotangent):
    buffers = TOKENS // TOK_DEV
    groups = size_group.reshape(buffers, IMG_DEV)
    segment, prompt_slot, live_rows, lengths = jax.vmap(layout)(groups)
    token_count = jnp.sum(lengths).astype(jnp.float32)
    field_in = tokens.astype(jnp.float32).reshape(buffers, TOK_DEV, D)
    indices = pos_index.reshape(buffers, TOK_DEV, 2)
    pos_rows = pos_table.astype(jnp.float32)
    qkv_full = w_qkv.astype(jnp.float32)
    out_full = w_out.astype(jnp.float32)
    up_full = w_up.astype(jnp.float32)
    down_full = w_down.astype(jnp.float32)

    def full_pass(field_all, prompt_rows):

        def per_buffer(pieces):
            return jax.checkpoint(forward_buffer)(pieces[0], pieces[1], pieces[2], pieces[3], pieces[4], prompt_rows, pos_rows, norm_gains, qkv_full, out_full, up_full, down_full)
        results = lax.map(per_buffer, (field_all, indices, segment, prompt_slot, live_rows))
        penalty = PENALTY_RATE * token_count * jnp.mean(prompt_rows * prompt_rows)
        return (results, penalty)
    (results, penalty), pullback = jax.vjp(full_pass, field_in, prompts)
    field_grad, prompt_grad = pullback((cotangent.astype(jnp.float32).reshape(buffers, TOK_DEV, D), jnp.ones_like(penalty)))
    return (results.reshape(TOKENS, D).astype(jnp.bfloat16), field_grad.reshape(TOKENS, D).astype(jnp.bfloat16), prompt_grad, penalty)
```

```python
import functools

import jax
import jax.numpy as jnp
from jax import lax
from jax.experimental import pallas as pl
from jax.experimental.pallas import tpu as pltpu
from jax.sharding import PartitionSpec as P

HEADS = 12
HEAD_DIM = 64
PROMPTS = 50
PATCH_S = 100
PATCH_M = 196
PATCH_L = 576

EPSILON = 1e-06
PENALTY_RATE = 3e-05
SCALE = HEAD_DIM**-0.5
LOG2E = 1.4426950408889634
SCORE = SCALE * LOG2E

BF = jnp.bfloat16
F32 = jnp.float32
NN = (((1,), (0,)), ((), ()))
NT = (((1,), (1,)), ((), ()))
MESH = pl.DeviceIdType.MESH

LANES = 128
HEAD_COLS = 256
PAIRS = HEAD_COLS // LANES
GROUP_HEADS = HEAD_COLS // HEAD_DIM
SMALL = 256
LARGE = 640
CHUNKS = {SMAL: c for SMAL, c in ((SMALL, ((0, 256),)), (LARGE, ((0, 256), (256, 256), (512, 128))))}
POS_ROWS = 256
SLOT_ROWS = 64


def dot(a, b, dims=NN):
    return lax.dot_general(a, b, dims, preferred_element_type=F32)


def image_length(group):
    patches = jnp.where(group == 0, PATCH_S, jnp.where(group == 1, PATCH_M, PATCH_L))
    return jnp.where(group == 3, 0, 1 + PROMPTS + patches).astype(jnp.int32)


def total_length(groups, slots):
    total = jnp.int32(0)
    for slot in range(slots):
        total = total + image_length(groups[slot])
    return total


def row_places(groups, slots, first_row, count):
    rows = first_row + lax.broadcasted_iota(jnp.int32, (count, 1), 0)
    place = rows
    start = jnp.int32(0)
    for slot in range(slots):
        length = image_length(groups[slot])
        place = jnp.where((rows >= start) & (length > 0), rows - start, place)
        start = start + length
    live = rows < start
    prompt_slot = jnp.where(live & (place >= 1) & (place <= PROMPTS), place - 1, -1)
    return prompt_slot, live


def norm_parts(values):
    centered = values - jnp.mean(values, axis=-1, keepdims=True)
    rstd = lax.rsqrt(jnp.mean(centered * centered, axis=-1, keepdims=True) + EPSILON)
    return centered * rstd, rstd


def norm_back(normal, rstd, gain, grad):
    scaled = grad * gain
    return (
        scaled
        - jnp.mean(scaled, axis=-1, keepdims=True)
        - normal * jnp.mean(scaled * normal, axis=-1, keepdims=True)
    ) * rstd


def embed_kernel(
    slots, groups, tokens, pos_index, pos_table, prompts, gains, w_qkv, hidden_out, qkv_out, table
):
    tile = tokens.shape[0]
    step = pl.program_id(0)

    @pl.when(step == 0)
    def _():
        table[...] = jnp.zeros_like(table)
        table[: pos_table.shape[0]] = pos_table[...]
        rest = prompts[...]
        for piece in range(3):
            part = rest.astype(BF)
            first = POS_ROWS + piece * SLOT_ROWS
            table[first : first + PROMPTS] = part
            rest = rest - part.astype(F32)

    prompt_slot, _ = row_places(groups, slots, step * tile, tile)
    is_prompt = prompt_slot >= 0
    lane = lax.broadcasted_iota(jnp.int32, (1, POS_ROWS), 1)
    left = jnp.where(is_prompt, -1, pos_index[:, 0:1])
    right = jnp.where(is_prompt, -1, pos_index[:, 1:2])
    half_hot = jnp.where(lane == left, 0.5, 0.0) + jnp.where(lane == right, 0.5, 0.0)
    slot_lane = lax.broadcasted_iota(jnp.int32, (1, 3 * SLOT_ROWS), 1)
    slot_lane = lax.rem(slot_lane, SLOT_ROWS)
    slot_hot = jnp.where(slot_lane == prompt_slot, 1.0, 0.0)
    picked = dot(half_hot.astype(BF), table[:POS_ROWS]) + dot(
        slot_hot.astype(BF), table[POS_ROWS:]
    )
    hidden = jnp.where(is_prompt, 0.0, tokens[...].astype(F32)) + picked
    hidden_out[...] = hidden
    normal, _ = norm_parts(hidden)
    normed = (normal * gains[0:1]).astype(BF)
    qkv_out[...] = dot(normed, w_qkv[...]).astype(BF)


def embed(size_group, tokens, pos_index, pos_table, prompts, gains, w_qkv):
    rows, width = tokens.shape
    tile = 384
    keep = lambda i, g: (0, 0)
    whole = lambda a: pl.BlockSpec(a.shape, keep, pipeline_mode=pl.Buffered(1))
    by_row = lambda columns: pl.BlockSpec((tile, columns), lambda i, g: (i, 0))
    return pl.pallas_call(
        functools.partial(embed_kernel, size_group.shape[0]),
        grid_spec=pltpu.PrefetchScalarGridSpec(
            num_scalar_prefetch=1,
            grid=(rows // tile,),
            in_specs=[
                by_row(width),
                by_row(2),
                whole(pos_table),
                whole(prompts),
                whole(gains),
                whole(w_qkv),
            ],
            out_specs=[by_row(width), by_row(3 * width)],
            scratch_shapes=[pltpu.VMEM((POS_ROWS + 3 * SLOT_ROWS, width), BF)],
        ),
        out_shape=[
            jax.ShapeDtypeStruct((rows, width), F32),
            jax.ShapeDtypeStruct((rows, 3 * width), BF),
        ],
        compiler_params=pltpu.CompilerParams(vmem_limit_bytes=40 << 20),
        name="embed",
    )(size_group, tokens, pos_index, pos_table, prompts, gains, w_qkv)


def half(values, which):
    lane = lax.broadcasted_iota(jnp.int32, values.shape, 1)
    inside = (lane < HEAD_DIM) if which == 0 else (lane >= HEAD_DIM)
    return jnp.where(inside, values, jnp.zeros_like(values))


def each_image(groups, slots, image):
    def body(slot, start):
        group = groups[slot]
        length = image_length(group)
        pl.when(group == 2)(functools.partial(image, LARGE, start, length, slot))
        pl.when(group < 2)(functools.partial(image, SMALL, start, length, slot))
        return start + length

    lax.fori_loop(0, slots, body, jnp.int32(0))


def spread(pairs):
    for spaced, block in pairs:
        for pair in range(PAIRS):
            columns = slice(LANES * pair, LANES * (pair + 1))
            spaced[pair, : block.shape[0]] = block[:, columns].astype(F32)


def collect(block, spaced):
    for pair in range(PAIRS):
        columns = slice(LANES * pair, LANES * (pair + 1))
        block[:, columns] = spaced[pair, : block.shape[0]].astype(BF)


def take(spaced, rows):
    return [spaced[pair, rows, :] for pair in range(PAIRS)]


def low(parts):
    return [part.astype(BF) for part in parts]


def head_rows(parts, head):
    return parts[head // 2][HEAD_DIM * (head % 2) : HEAD_DIM * (head % 2 + 1)]


def clear_first(*refs):
    @pl.when(pl.program_id(0) == 0)
    def _():
        for ref in refs:
            ref[...] = jnp.zeros_like(ref)


def attend_kernel(slots, groups, q_ref, k_ref, v_ref, out_ref, total_ref, qs, ks, vs, outs):
    clear_first(qs, ks, vs, outs)
    spread(((qs, q_ref), (ks, k_ref), (vs, v_ref)))
    heads = range(GROUP_HEADS)

    def image(span, start, length, slot):
        rows = pl.ds(start, span)
        query = low(take(qs, rows))
        key = low(take(ks, rows))
        value_t = low([x.T for x in take(vs, rows)])
        last = span - LANES
        tail = lax.broadcasted_iota(jnp.int32, (LANES, 1), 0) + last < length
        for first, count in CHUNKS[span]:
            scores = [
                dot(key[h // 2], half(query[h // 2][first : first + count], h % 2), NT)
                for h in heads
            ]
            scores = [
                jnp.concatenate([s[:last], jnp.where(tail, s[last:], -1e30)], 0) for s in scores
            ]
            peaks = [jnp.max(s, axis=0, keepdims=True) for s in scores]
            powers = [jnp.exp2((s - m) * SCORE) for s, m in zip(scores, peaks)]
            totals = [jnp.sum(e, axis=0, keepdims=True) for e in powers]
            mixed = [dot(head_rows(value_t, h), powers[h].astype(BF)) for h in heads]
            mixed = [o / t for o, t in zip(mixed, totals)]
            for h in heads:
                total_ref[0, GROUP_HEADS * slot + h, :, first : first + count] = peaks[
                    h
                ] * SCORE + jnp.log2(totals[h])
            for pair in range(PAIRS):
                outs[pair, pl.ds(start + first, count), :] = jnp.concatenate(
                    mixed[2 * pair : 2 * pair + 2], 0
                ).T

    each_image(groups, slots, image)
    collect(out_ref, outs)


def attend(size_group, qkv):
    rows = qkv.shape[0]
    width = qkv.shape[1] // 3
    steps = width // HEAD_COLS
    slots = size_group.shape[0]
    block = lambda shift: pl.BlockSpec((rows, HEAD_COLS), lambda i, g: (0, shift * steps + i))
    spaced = pltpu.VMEM((PAIRS, rows + LANES, LANES), F32)
    return pl.pallas_call(
        functools.partial(attend_kernel, slots),
        grid_spec=pltpu.PrefetchScalarGridSpec(
            num_scalar_prefetch=1,
            grid=(steps,),
            in_specs=[block(0), block(1), block(2)],
            out_specs=[
                block(0),
                pl.BlockSpec((1, GROUP_HEADS * slots, 1, LARGE), lambda i, g: (i, 0, 0, 0)),
            ],
            scratch_shapes=[spaced] * 4,
        ),
        out_shape=[
            jax.ShapeDtypeStruct((rows, width), BF),
            jax.ShapeDtypeStruct((steps, GROUP_HEADS * slots, 1, LARGE), F32),
        ],
        compiler_params=pltpu.CompilerParams(vmem_limit_bytes=50 << 20),
        name="attend",
    )(size_group, qkv, qkv, qkv)


def attend_back_kernel(
    slots,
    groups,
    q_ref,
    k_ref,
    v_ref,
    grad_ref,
    mixed_ref,
    total_ref,
    dq_ref,
    dk_ref,
    dv_ref,
    qs,
    ks,
    vs,
    grads,
    mixes,
    dqs,
    dks,
    dvs,
):
    clear_first(qs, ks, vs, grads, mixes, dqs, dks, dvs)
    spread(((qs, q_ref), (ks, k_ref), (vs, v_ref), (grads, grad_ref), (mixes, mixed_ref)))
    heads = range(GROUP_HEADS)

    def image(span, start, length, slot):
        rows = pl.ds(start, span)
        query = low(take(qs, rows))
        key = low(take(ks, rows))
        key_t = low([x.T for x in take(ks, rows)])
        value = low(take(vs, rows))
        inside = lax.broadcasted_iota(jnp.int32, (span, 1), 0) < length
        grad32 = [jnp.where(inside, x, 0.0) for x in take(grads, rows)]
        products = [(x * y).T for x, y in zip(grad32, take(mixes, rows))]
        grad = low(grad32)
        last = span - LANES
        tail = inside[last:]
        dk = [jnp.zeros((span, LANES), F32)] * PAIRS
        dv = [jnp.zeros((span, LANES), F32)] * PAIRS
        for first, count in CHUNKS[span]:
            part = slice(first, first + count)
            query_h = [half(query[h // 2][part], h % 2) for h in heads]
            grad_h = [half(grad[h // 2][part], h % 2) for h in heads]
            scores = [dot(key[h // 2], query_h[h], NT) for h in heads]
            prob_grads = [dot(value[h // 2], grad_h[h], NT) for h in heads]
            probs = [
                jnp.exp2(scores[h] * SCORE - total_ref[0, GROUP_HEADS * slot + h, :, part])
                for h in heads
            ]
            probs = [
                jnp.concatenate([p[:last], jnp.where(tail, p[last:], 0.0)], 0) for p in probs
            ]
            deltas = [
                jnp.sum(head_rows(products, h)[:, part], axis=0, keepdims=True) for h in heads
            ]
            score_grads = [(probs[h] * (prob_grads[h] - deltas[h])).astype(BF) for h in heads]
            for h in heads:
                dv[h // 2] += dot(probs[h].astype(BF), grad_h[h])
                dk[h // 2] += dot(score_grads[h], query_h[h])
            dq = [dot(head_rows(key_t, h), score_grads[h]) for h in heads]
            for pair in range(PAIRS):
                dqs[pair, pl.ds(start + first, count), :] = (
                    jnp.concatenate(dq[2 * pair : 2 * pair + 2], 0).T * SCALE
                )
        for pair in range(PAIRS):
            dks[pair, rows, :] = dk[pair] * SCALE
            dvs[pair, rows, :] = dv[pair]

    each_image(groups, slots, image)
    collect(dq_ref, dqs)
    collect(dk_ref, dks)
    collect(dv_ref, dvs)


def attend_back(size_group, qkv, mixed_grad, mixed, totals):
    rows = qkv.shape[0]
    width = qkv.shape[1] // 3
    steps = width // HEAD_COLS
    slots = size_group.shape[0]
    block = lambda shift: pl.BlockSpec((rows, HEAD_COLS), lambda i, g: (0, shift * steps + i))
    spaced = pltpu.VMEM((PAIRS, rows + LANES, LANES), F32)
    return pl.pallas_call(
        functools.partial(attend_back_kernel, slots),
        grid_spec=pltpu.PrefetchScalarGridSpec(
            num_scalar_prefetch=1,
            grid=(steps,),
            in_specs=[
                block(0),
                block(1),
                block(2),
                block(0),
                block(0),
                pl.BlockSpec((1, GROUP_HEADS * slots, 1, LARGE), lambda i, g: (i, 0, 0, 0)),
            ],
            out_specs=[block(0)] * 3,
            scratch_shapes=[spaced] * 8,
        ),
        out_shape=[jax.ShapeDtypeStruct((rows, width), BF)] * 3,
        compiler_params=pltpu.CompilerParams(vmem_limit_bytes=56 << 20),
        name="attend_back",
    )(size_group, qkv, qkv, qkv, mixed_grad, mixed, totals)


def feed_kernel(
    slots,
    chunk,
    groups,
    hidden,
    mixed,
    cotangent,
    gains,
    w_out,
    w_up,
    w_down,
    out_ref,
    middle_grad_ref,
    mixed_grad_ref,
):
    tile = hidden.shape[0]
    inner_width = w_up.shape[1]
    rows = pl.program_id(0) * tile + lax.broadcasted_iota(jnp.int32, (tile, 1), 0)
    live = rows < total_length(groups, slots)
    out_grad = jnp.where(live, cotangent[...].astype(F32), 0.0)
    out_grad_low = out_grad.astype(BF)
    middle = hidden[...] + dot(mixed[...], w_out[...])
    normal, rstd = norm_parts(middle)
    gain = gains[1:2]
    second = (normal * gain).astype(BF)
    forward = middle
    back = jnp.zeros_like(middle)
    for first in range(0, inner_width, chunk):
        part = slice(first, first + chunk)
        inner = dot(second, w_up[:, part])
        act_grad = dot(out_grad_low, w_down[part], NT)
        phi = 0.5 + 0.5 * lax.erf(inner * (0.5**0.5))
        density = jnp.exp2(inner * inner * (-0.5 * LOG2E)) * 0.3989422804014327
        activated = (inner * phi).astype(BF)
        inner_grad = (act_grad * (phi + inner * density)).astype(BF)
        forward = forward + dot(activated, w_down[part])
        back = back + dot(inner_grad, w_up[:, part], NT)
    out_ref[...] = jnp.where(live, forward, 0.0).astype(BF)
    middle_grad = out_grad + norm_back(normal, rstd, gain, back)
    middle_grad_ref[...] = middle_grad
    mixed_grad_ref[...] = dot(middle_grad.astype(BF), w_out[...], NT).astype(BF)


def feed(size_group, hidden, mixed, cotangent, gains, w_out, w_up, w_down):
    rows, width = hidden.shape
    tile = 384
    chunk = 512
    keep = lambda i, g: (0, 0)
    whole = lambda a: pl.BlockSpec(a.shape, keep, pipeline_mode=pl.Buffered(1))
    by_row = pl.BlockSpec((tile, width), lambda i, g: (i, 0))
    return pl.pallas_call(
        functools.partial(feed_kernel, size_group.shape[0], chunk),
        grid_spec=pltpu.PrefetchScalarGridSpec(
            num_scalar_prefetch=1,
            grid=(rows // tile,),
            in_specs=[by_row, by_row, by_row, whole(gains), whole(w_out), whole(w_up), whole(w_down)],
            out_specs=[by_row, by_row, by_row],
        ),
        out_shape=[
            jax.ShapeDtypeStruct((rows, width), BF),
            jax.ShapeDtypeStruct((rows, width), F32),
            jax.ShapeDtypeStruct((rows, width), BF),
        ],
        compiler_params=pltpu.CompilerParams(vmem_limit_bytes=56 << 20),
        name="feed",
    )(size_group, hidden, mixed, cotangent, gains, w_out, w_up, w_down)


def finish_kernel(
    slots, groups, hidden, middle_grad, dq, dk, dv, gains, w_qkv, grad_ref, sums_ref, kept
):
    tile, width = hidden.shape
    step = pl.program_id(0)
    normed_grad = (
        dot(dq[...], w_qkv[:, :width], NT)
        + dot(dk[...], w_qkv[:, width : 2 * width], NT)
        + dot(dv[...], w_qkv[:, 2 * width :], NT)
    )
    normal, rstd = norm_parts(hidden[...])
    hidden_grad = middle_grad[...] + norm_back(normal, rstd, gains[0:1], normed_grad)
    prompt_slot, live = row_places(groups, slots, step * tile, tile)
    grad_ref[...] = jnp.where(live & (prompt_slot < 0), hidden_grad, 0.0).astype(BF)
    for column in range(width // LANES):
        kept[column, pl.ds(pl.multiple_of(step * tile, tile), tile), :] = hidden_grad[
            :, LANES * column : LANES * (column + 1)
        ]

    @pl.when(step == pl.num_programs(0) - 1)
    def _():
        total = total_length(groups, slots).astype(F32)
        slot_row = lax.broadcasted_iota(jnp.int32, (SLOT_ROWS, LANES), 0)
        for column in range(width // LANES):
            start = jnp.int32(0)
            sums = jnp.zeros((SLOT_ROWS, LANES), F32)
            for slot in range(slots):
                length = image_length(groups[slot])
                first = jnp.where(length > 0, start + 1, 0)
                taken = kept[column, pl.ds(first, SLOT_ROWS), :]
                sums = sums + jnp.where(length > 0, taken, 0.0)
                start = start + length
            sums_ref[:, LANES * column : LANES * (column + 1)] = jnp.where(
                slot_row < PROMPTS, sums, jnp.where(slot_row == PROMPTS, total, 0.0)
            )


def finish(size_group, hidden, middle_grad, dq, dk, dv, gains, w_qkv):
    rows, width = hidden.shape
    tile = 384
    keep = lambda i, g: (0, 0)
    whole = lambda a: pl.BlockSpec(a.shape, keep, pipeline_mode=pl.Buffered(1))
    by_row = pl.BlockSpec((tile, width), lambda i, g: (i, 0))
    return pl.pallas_call(
        functools.partial(finish_kernel, size_group.shape[0]),
        grid_spec=pltpu.PrefetchScalarGridSpec(
            num_scalar_prefetch=1,
            grid=(rows // tile,),
            in_specs=[by_row] * 5 + [whole(gains), whole(w_qkv)],
            out_specs=[by_row, pl.BlockSpec((SLOT_ROWS, width), keep)],
            scratch_shapes=[pltpu.VMEM((width // LANES, rows, LANES), F32)],
        ),
        out_shape=[
            jax.ShapeDtypeStruct((rows, width), BF),
            jax.ShapeDtypeStruct((SLOT_ROWS, width), F32),
        ],
        compiler_params=pltpu.CompilerParams(vmem_limit_bytes=50 << 20),
        name="finish",
    )(size_group, hidden, middle_grad, dq, dk, dv, gains, w_qkv)


def shards(
    axes,
    tokens,
    pos_index,
    size_group,
    pos_table,
    prompts,
    norm_gains,
    w_qkv,
    w_out,
    w_up,
    w_down,
    cotangent,
):
    full_qkv = lax.all_gather(w_qkv, "wide", axis=0, tiled=True)
    full_out = lax.all_gather(w_out, "wide", axis=0, tiled=True)
    full_up = lax.all_gather(w_up, "wide", axis=0, tiled=True)
    full_down = lax.all_gather(w_down, "wide", axis=0, tiled=True)
    hidden, qkv = embed(size_group, tokens, pos_index, pos_table, prompts, norm_gains, full_qkv)
    mixed, totals = attend(size_group, qkv)
    outputs, middle_grad, mixed_grad = feed(
        size_group, hidden, mixed, cotangent, norm_gains, full_out, full_up, full_down
    )
    dq, dk, dv = attend_back(size_group, qkv, mixed_grad, mixed, totals)
    input_grad, sums = finish(size_group, hidden, middle_grad, dq, dk, dv, norm_gains, full_qkv)
    sums = lax.psum(sums, ("dp", "wide"))
    token_total = sums[PROMPTS, 0]
    prompt_grad = sums[:PROMPTS] + (2.0 * PENALTY_RATE / prompts.size) * token_total * prompts
    penalty = PENALTY_RATE * token_total * jnp.mean(prompts * prompts)
    return (outputs, input_grad, prompt_grad, penalty)


def solution(mesh):
    return jax.shard_map(
        functools.partial(shards, tuple(mesh.shape.items())),
        mesh=mesh,
        in_specs=(
            P(("dp", "wide"), None),
            P(("dp", "wide"), None),
            P(("dp", "wide")),
            P(),
            P(),
            P(),
            P("wide", None),
            P("wide", None),
            P("wide", None),
            P("wide", None),
            P(("dp", "wide"), None),
        ),
        out_specs=(P(("dp", "wide"), None), P(("dp", "wide"), None), P(), P()),
        check_vma=False,
    )
```

```python
import functools

import jax
import jax.numpy as jnp
from jax import lax
from jax.experimental import pallas as pl
from jax.experimental.pallas import tpu as pltpu
from jax.sharding import PartitionSpec as P

HEADS = 12
HEAD_DIM = 64
PROMPTS = 50
PATCH_S = 100
PATCH_M = 196
PATCH_L = 576

EPSILON = 1e-06
PENALTY_RATE = 3e-05
SCALE = HEAD_DIM**-0.5
LOG2E = 1.4426950408889634
SCORE = SCALE * LOG2E

BF = jnp.bfloat16
F32 = jnp.float32
NN = (((1,), (0,)), ((), ()))
NT = (((1,), (1,)), ((), ()))
MESH = pl.DeviceIdType.MESH

LANES = 128
HEAD_COLS = 256
PAIRS = HEAD_COLS // LANES
GROUP_HEADS = HEAD_COLS // HEAD_DIM
SMALL = 256
LARGE = 640
CHUNKS = {SMAL: c for SMAL, c in ((SMALL, ((0, 256),)), (LARGE, ((0, 256), (256, 256), (512, 128))))}
POS_ROWS = 256
SLOT_ROWS = 64


def dot(a, b, dims=NN):
    return lax.dot_general(a, b, dims, preferred_element_type=F32)


def image_length(group):
    patches = jnp.where(group == 0, PATCH_S, jnp.where(group == 1, PATCH_M, PATCH_L))
    return jnp.where(group == 3, 0, 1 + PROMPTS + patches).astype(jnp.int32)


def total_length(groups, slots):
    total = jnp.int32(0)
    for slot in range(slots):
        total = total + image_length(groups[slot])
    return total


def row_places(groups, slots, first_row, count):
    rows = first_row + lax.broadcasted_iota(jnp.int32, (count, 1), 0)
    place = rows
    start = jnp.int32(0)
    for slot in range(slots):
        length = image_length(groups[slot])
        place = jnp.where((rows >= start) & (length > 0), rows - start, place)
        start = start + length
    live = rows < start
    prompt_slot = jnp.where(live & (place >= 1) & (place <= PROMPTS), place - 1, -1)
    return prompt_slot, live


def norm_parts(values):
    centered = values - jnp.mean(values, axis=-1, keepdims=True)
    rstd = lax.rsqrt(jnp.mean(centered * centered, axis=-1, keepdims=True) + EPSILON)
    return centered * rstd, rstd


def norm_back(normal, rstd, gain, grad):
    scaled = grad * gain
    return (
        scaled
        - jnp.mean(scaled, axis=-1, keepdims=True)
        - normal * jnp.mean(scaled * normal, axis=-1, keepdims=True)
    ) * rstd


def embed_kernel(
    slots, groups, tokens, pos_index, pos_table, prompts, gains, w_qkv, hidden_out, qkv_out, table
):
    tile = tokens.shape[0]
    step = pl.program_id(0)

    @pl.when(step == 0)
    def _():
        table[...] = jnp.zeros_like(table)
        table[: pos_table.shape[0]] = pos_table[...]
        rest = prompts[...]
        for piece in range(3):
            part = rest.astype(BF)
            first = POS_ROWS + piece * SLOT_ROWS
            table[first : first + PROMPTS] = part
            rest = rest - part.astype(F32)

    prompt_slot, _ = row_places(groups, slots, step * tile, tile)
    is_prompt = prompt_slot >= 0
    lane = lax.broadcasted_iota(jnp.int32, (1, POS_ROWS), 1)
    left = jnp.where(is_prompt, -1, pos_index[:, 0:1])
    right = jnp.where(is_prompt, -1, pos_index[:, 1:2])
    half_hot = jnp.where(lane == left, 0.5, 0.0) + jnp.where(lane == right, 0.5, 0.0)
    slot_lane = lax.broadcasted_iota(jnp.int32, (1, 3 * SLOT_ROWS), 1)
    slot_lane = lax.rem(slot_lane, SLOT_ROWS)
    slot_hot = jnp.where(slot_lane == prompt_slot, 1.0, 0.0)
    picked = dot(half_hot.astype(BF), table[:POS_ROWS]) + dot(
        slot_hot.astype(BF), table[POS_ROWS:]
    )
    hidden = jnp.where(is_prompt, 0.0, tokens[...].astype(F32)) + picked
    hidden_out[...] = hidden
    normal, _ = norm_parts(hidden)
    normed = (normal * gains[0:1]).astype(BF)
    qkv_out[...] = dot(normed, w_qkv[...]).astype(BF)


def embed(size_group, tokens, pos_index, pos_table, prompts, gains, w_qkv):
    rows, width = tokens.shape
    tile = 384
    keep = lambda i, g: (0, 0)
    whole = lambda a: pl.BlockSpec(a.shape, keep, pipeline_mode=pl.Buffered(1))
    by_row = lambda columns: pl.BlockSpec((tile, columns), lambda i, g: (i, 0))
    return pl.pallas_call(
        functools.partial(embed_kernel, size_group.shape[0]),
        grid_spec=pltpu.PrefetchScalarGridSpec(
            num_scalar_prefetch=1,
            grid=(rows // tile,),
            in_specs=[
                by_row(width),
                by_row(2),
                whole(pos_table),
                whole(prompts),
                whole(gains),
                whole(w_qkv),
            ],
            out_specs=[by_row(width), by_row(3 * width)],
            scratch_shapes=[pltpu.VMEM((POS_ROWS + 3 * SLOT_ROWS, width), BF)],
        ),
        out_shape=[
            jax.ShapeDtypeStruct((rows, width), F32),
            jax.ShapeDtypeStruct((rows, 3 * width), BF),
        ],
        compiler_params=pltpu.CompilerParams(vmem_limit_bytes=40 << 20),
        name="embed",
    )(size_group, tokens, pos_index, pos_table, prompts, gains, w_qkv)


def half(values, which):
    lane = lax.broadcasted_iota(jnp.int32, values.shape, 1)
    inside = (lane < HEAD_DIM) if which == 0 else (lane >= HEAD_DIM)
    return jnp.where(inside, values, jnp.zeros_like(values))


def each_image(groups, slots, image):
    def body(slot, start):
        group = groups[slot]
        length = image_length(group)
        pl.when(group == 2)(functools.partial(image, LARGE, start, length, slot))
        pl.when(group < 2)(functools.partial(image, SMALL, start, length, slot))
        return start + length

    lax.fori_loop(0, slots, body, jnp.int32(0))


def spread(pairs):
    for spaced, block in pairs:
        for pair in range(PAIRS):
            columns = slice(LANES * pair, LANES * (pair + 1))
            spaced[pair, : block.shape[0]] = block[:, columns].astype(F32)


def collect(block, spaced):
    for pair in range(PAIRS):
        columns = slice(LANES * pair, LANES * (pair + 1))
        block[:, columns] = spaced[pair, : block.shape[0]].astype(BF)


def take(spaced, rows):
    return [spaced[pair, rows, :] for pair in range(PAIRS)]


def low(parts):
    return [part.astype(BF) for part in parts]


def head_rows(parts, head):
    return parts[head // 2][HEAD_DIM * (head % 2) : HEAD_DIM * (head % 2 + 1)]


def clear_first(*refs):
    @pl.when(pl.program_id(0) == 0)
    def _():
        for ref in refs:
            ref[...] = jnp.zeros_like(ref)


def attend_kernel(slots, groups, q_ref, k_ref, v_ref, out_ref, total_ref, qs, ks, vs, outs):
    clear_first(qs, ks, vs, outs)
    spread(((qs, q_ref), (ks, k_ref), (vs, v_ref)))
    heads = range(GROUP_HEADS)

    def image(span, start, length, slot):
        rows = pl.ds(start, span)
        query = low(take(qs, rows))
        key = low(take(ks, rows))
        value_t = low([x.T for x in take(vs, rows)])
        last = span - LANES
        tail = lax.broadcasted_iota(jnp.int32, (LANES, 1), 0) + last < length
        for first, count in CHUNKS[span]:
            scores = [
                dot(key[h // 2], half(query[h // 2][first : first + count], h % 2), NT)
                for h in heads
            ]
            scores = [
                jnp.concatenate([s[:last], jnp.where(tail, s[last:], -1e30)], 0) for s in scores
            ]
            peaks = [jnp.max(s, axis=0, keepdims=True) for s in scores]
            powers = [jnp.exp2((s - m) * SCORE) for s, m in zip(scores, peaks)]
            totals = [jnp.sum(e, axis=0, keepdims=True) for e in powers]
            mixed = [dot(head_rows(value_t, h), powers[h].astype(BF)) for h in heads]
            mixed = [o / t for o, t in zip(mixed, totals)]
            for h in heads:
                total_ref[0, GROUP_HEADS * slot + h, :, first : first + count] = peaks[
                    h
                ] * SCORE + jnp.log2(totals[h])
            for pair in range(PAIRS):
                outs[pair, pl.ds(start + first, count), :] = jnp.concatenate(
                    mixed[2 * pair : 2 * pair + 2], 0
                ).T

    each_image(groups, slots, image)
    collect(out_ref, outs)


def attend(size_group, qkv):
    rows = qkv.shape[0]
    width = qkv.shape[1] // 3
    steps = width // HEAD_COLS
    slots = size_group.shape[0]
    block = lambda shift: pl.BlockSpec((rows, HEAD_COLS), lambda i, g: (0, shift * steps + i))
    spaced = pltpu.VMEM((PAIRS, rows + LANES, LANES), F32)
    return pl.pallas_call(
        functools.partial(attend_kernel, slots),
        grid_spec=pltpu.PrefetchScalarGridSpec(
            num_scalar_prefetch=1,
            grid=(steps,),
            in_specs=[block(0), block(1), block(2)],
            out_specs=[
                block(0),
                pl.BlockSpec((1, GROUP_HEADS * slots, 1, LARGE), lambda i, g: (i, 0, 0, 0)),
            ],
            scratch_shapes=[spaced] * 4,
        ),
        out_shape=[
            jax.ShapeDtypeStruct((rows, width), BF),
            jax.ShapeDtypeStruct((steps, GROUP_HEADS * slots, 1, LARGE), F32),
        ],
        compiler_params=pltpu.CompilerParams(vmem_limit_bytes=50 << 20),
        name="attend",
    )(size_group, qkv, qkv, qkv)


def attend_back_kernel(
    slots,
    groups,
    q_ref,
    k_ref,
    v_ref,
    grad_ref,
    mixed_ref,
    total_ref,
    dq_ref,
    dk_ref,
    dv_ref,
    qs,
    ks,
    vs,
    grads,
    mixes,
    dqs,
    dks,
    dvs,
):
    clear_first(qs, ks, vs, grads, mixes, dqs, dks, dvs)
    spread(((qs, q_ref), (ks, k_ref), (vs, v_ref), (grads, grad_ref), (mixes, mixed_ref)))
    heads = range(GROUP_HEADS)

    def image(span, start, length, slot):
        rows = pl.ds(start, span)
        query = low(take(qs, rows))
        key = low(take(ks, rows))
        key_t = low([x.T for x in take(ks, rows)])
        value = low(take(vs, rows))
        inside = lax.broadcasted_iota(jnp.int32, (span, 1), 0) < length
        grad32 = [jnp.where(inside, x, 0.0) for x in take(grads, rows)]
        products = [(x * y).T for x, y in zip(grad32, take(mixes, rows))]
        grad = low(grad32)
        last = span - LANES
        tail = inside[last:]
        dk = [jnp.zeros((span, LANES), F32)] * PAIRS
        dv = [jnp.zeros((span, LANES), F32)] * PAIRS
        for first, count in CHUNKS[span]:
            part = slice(first, first + count)
            query_h = [half(query[h // 2][part], h % 2) for h in heads]
            grad_h = [half(grad[h // 2][part], h % 2) for h in heads]
            scores = [dot(key[h // 2], query_h[h], NT) for h in heads]
            prob_grads = [dot(value[h // 2], grad_h[h], NT) for h in heads]
            probs = [
                jnp.exp2(scores[h] * SCORE - total_ref[0, GROUP_HEADS * slot + h, :, part])
                for h in heads
            ]
            probs = [
                jnp.concatenate([p[:last], jnp.where(tail, p[last:], 0.0)], 0) for p in probs
            ]
            deltas = [
                jnp.sum(head_rows(products, h)[:, part], axis=0, keepdims=True) for h in heads
            ]
            score_grads = [(probs[h] * (prob_grads[h] - deltas[h])).astype(BF) for h in heads]
            for h in heads:
                dv[h // 2] += dot(probs[h].astype(BF), grad_h[h])
                dk[h // 2] += dot(score_grads[h], query_h[h])
            dq = [dot(head_rows(key_t, h), score_grads[h]) for h in heads]
            for pair in range(PAIRS):
                dqs[pair, pl.ds(start + first, count), :] = (
                    jnp.concatenate(dq[2 * pair : 2 * pair + 2], 0).T * SCALE
                )
        for pair in range(PAIRS):
            dks[pair, rows, :] = dk[pair] * SCALE
            dvs[pair, rows, :] = dv[pair]

    each_image(groups, slots, image)
    collect(dq_ref, dqs)
    collect(dk_ref, dks)
    collect(dv_ref, dvs)


def attend_back(size_group, qkv, mixed_grad, mixed, totals):
    rows = qkv.shape[0]
    width = qkv.shape[1] // 3
    steps = width // HEAD_COLS
    slots = size_group.shape[0]
    block = lambda shift: pl.BlockSpec((rows, HEAD_COLS), lambda i, g: (0, shift * steps + i))
    spaced = pltpu.VMEM((PAIRS, rows + LANES, LANES), F32)
    return pl.pallas_call(
        functools.partial(attend_back_kernel, slots),
        grid_spec=pltpu.PrefetchScalarGridSpec(
            num_scalar_prefetch=1,
            grid=(steps,),
            in_specs=[
                block(0),
                block(1),
                block(2),
                block(0),
                block(0),
                pl.BlockSpec((1, GROUP_HEADS * slots, 1, LARGE), lambda i, g: (i, 0, 0, 0)),
            ],
            out_specs=[block(0)] * 3,
            scratch_shapes=[spaced] * 8,
        ),
        out_shape=[jax.ShapeDtypeStruct((rows, width), BF)] * 3,
        compiler_params=pltpu.CompilerParams(vmem_limit_bytes=56 << 20),
        name="attend_back",
    )(size_group, qkv, qkv, qkv, mixed_grad, mixed, totals)


def feed_kernel(
    slots,
    chunk,
    groups,
    hidden,
    mixed,
    cotangent,
    gains,
    w_out,
    w_up,
    w_down,
    out_ref,
    middle_grad_ref,
    mixed_grad_ref,
):
    tile = hidden.shape[0]
    inner_width = w_up.shape[1]
    rows = pl.program_id(0) * tile + lax.broadcasted_iota(jnp.int32, (tile, 1), 0)
    live = rows < total_length(groups, slots)
    out_grad = jnp.where(live, cotangent[...].astype(F32), 0.0)
    out_grad_low = out_grad.astype(BF)
    middle = hidden[...] + dot(mixed[...], w_out[...])
    normal, rstd = norm_parts(middle)
    gain = gains[1:2]
    second = (normal * gain).astype(BF)
    forward = middle
    back = jnp.zeros_like(middle)
    for first in range(0, inner_width, chunk):
        part = slice(first, first + chunk)
        inner = dot(second, w_up[:, part])
        act_grad = dot(out_grad_low, w_down[part], NT)
        phi = 0.5 + 0.5 * lax.erf(inner * (0.5**0.5))
        density = jnp.exp2(inner * inner * (-0.5 * LOG2E)) * 0.3989422804014327
        activated = (inner * phi).astype(BF)
        inner_grad = (act_grad * (phi + inner * density)).astype(BF)
        forward = forward + dot(activated, w_down[part])
        back = back + dot(inner_grad, w_up[:, part], NT)
    out_ref[...] = jnp.where(live, forward, 0.0).astype(BF)
    middle_grad = out_grad + norm_back(normal, rstd, gain, back)
    middle_grad_ref[...] = middle_grad
    mixed_grad_ref[...] = dot(middle_grad.astype(BF), w_out[...], NT).astype(BF)


def feed(size_group, hidden, mixed, cotangent, gains, w_out, w_up, w_down):
    rows, width = hidden.shape
    tile = 384
    chunk = 512
    keep = lambda i, g: (0, 0)
    whole = lambda a: pl.BlockSpec(a.shape, keep, pipeline_mode=pl.Buffered(1))
    by_row = pl.BlockSpec((tile, width), lambda i, g: (i, 0))
    return pl.pallas_call(
        functools.partial(feed_kernel, size_group.shape[0], chunk),
        grid_spec=pltpu.PrefetchScalarGridSpec(
            num_scalar_prefetch=1,
            grid=(rows // tile,),
            in_specs=[by_row, by_row, by_row, whole(gains), whole(w_out), whole(w_up), whole(w_down)],
            out_specs=[by_row, by_row, by_row],
        ),
        out_shape=[
            jax.ShapeDtypeStruct((rows, width), BF),
            jax.ShapeDtypeStruct((rows, width), F32),
            jax.ShapeDtypeStruct((rows, width), BF),
        ],
        compiler_params=pltpu.CompilerParams(vmem_limit_bytes=56 << 20),
        name="feed",
    )(size_group, hidden, mixed, cotangent, gains, w_out, w_up, w_down)


def finish_kernel(
    slots, groups, hidden, middle_grad, dq, dk, dv, gains, w_qkv, grad_ref, sums_ref, kept
):
    tile, width = hidden.shape
    step = pl.program_id(0)
    normed_grad = (
        dot(dq[...], w_qkv[:, :width], NT)
        + dot(dk[...], w_qkv[:, width : 2 * width], NT)
        + dot(dv[...], w_qkv[:, 2 * width :], NT)
    )
    normal, rstd = norm_parts(hidden[...])
    hidden_grad = middle_grad[...] + norm_back(normal, rstd, gains[0:1], normed_grad)
    prompt_slot, live = row_places(groups, slots, step * tile, tile)
    grad_ref[...] = jnp.where(live & (prompt_slot < 0), hidden_grad, 0.0).astype(BF)
    for column in range(width // LANES):
        kept[column, pl.ds(pl.multiple_of(step * tile, tile), tile), :] = hidden_grad[
            :, LANES * column : LANES * (column + 1)
        ]

    @pl.when(step == pl.num_programs(0) - 1)
    def _():
        total = total_length(groups, slots).astype(F32)
        slot_row = lax.broadcasted_iota(jnp.int32, (SLOT_ROWS, LANES), 0)
        for column in range(width // LANES):
            start = jnp.int32(0)
            sums = jnp.zeros((SLOT_ROWS, LANES), F32)
            for slot in range(slots):
                length = image_length(groups[slot])
                first = jnp.where(length > 0, start + 1, 0)
                taken = kept[column, pl.ds(first, SLOT_ROWS), :]
                sums = sums + jnp.where(length > 0, taken, 0.0)
                start = start + length
            sums_ref[:, LANES * column : LANES * (column + 1)] = jnp.where(
                slot_row < PROMPTS, sums, jnp.where(slot_row == PROMPTS, total, 0.0)
            )


def finish(size_group, hidden, middle_grad, dq, dk, dv, gains, w_qkv):
    rows, width = hidden.shape
    tile = 384
    keep = lambda i, g: (0, 0)
    whole = lambda a: pl.BlockSpec(a.shape, keep, pipeline_mode=pl.Buffered(1))
    by_row = pl.BlockSpec((tile, width), lambda i, g: (i, 0))
    return pl.pallas_call(
        functools.partial(finish_kernel, size_group.shape[0]),
        grid_spec=pltpu.PrefetchScalarGridSpec(
            num_scalar_prefetch=1,
            grid=(rows // tile,),
            in_specs=[by_row] * 5 + [whole(gains), whole(w_qkv)],
            out_specs=[by_row, pl.BlockSpec((SLOT_ROWS, width), keep)],
            scratch_shapes=[pltpu.VMEM((width // LANES, rows, LANES), F32)],
        ),
        out_shape=[
            jax.ShapeDtypeStruct((rows, width), BF),
            jax.ShapeDtypeStruct((SLOT_ROWS, width), F32),
        ],
        compiler_params=pltpu.CompilerParams(vmem_limit_bytes=50 << 20),
        name="finish",
    )(size_group, hidden, middle_grad, dq, dk, dv, gains, w_qkv)


def share_kernel(
    dp, wide, sums, prompts, grad_ref, penalty_ref, near, far, result, send, near_in, far_in, last_in
):
    members = 2 * dp
    planes = wide // 2
    slice_rows = SLOT_ROWS // members
    d = lax.axis_index("dp")
    w = lax.axis_index("wide")
    plane = w // 2
    member = d * 2 + lax.rem(w, 2)

    def peer(step):
        other = lax.rem(member + step, members)
        return other, (other // 2, plane * 2 + lax.rem(other, 2))

    def plane_peer(step):
        other = lax.rem(plane + step, planes)
        return other, (d, other * 2 + lax.rem(w, 2))

    barrier = pltpu.get_barrier_semaphore()
    for step in range(1, members):
        pl.semaphore_signal(barrier, inc=1, device_id=peer(step)[1], device_id_type=MESH)
    for step in range(1, planes):
        pl.semaphore_signal(barrier, inc=1, device_id=plane_peer(step)[1], device_id_type=MESH)
    pl.semaphore_wait(barrier, members + planes - 2)

    def part(ref, index):
        return ref.at[pl.ds(pl.multiple_of(index * slice_rows, slice_rows), slice_rows)]

    first = []
    for step in range(1, members):
        other, device = peer(step)
        first.append(
            pltpu.make_async_remote_copy(
                part(sums, other),
                near.at[step],
                send.at[0, step],
                near_in.at[step],
                device_id=device,
                device_id_type=MESH,
            )
        )
        first[-1].start()
    near[0] = part(sums, member)[...]
    for copy in first:
        copy.wait_recv()
    total = jnp.zeros(near.shape[1:], F32)
    for index in range(members):
        total = total + near[lax.rem(member - index + members, members)]
    far[plane] = total
    second = []
    for step in range(1, planes):
        other, device = plane_peer(step)
        second.append(
            pltpu.make_async_remote_copy(
                far.at[plane],
                far.at[plane],
                send.at[1, step],
                far_in.at[step],
                device_id=device,
                device_id_type=MESH,
            )
        )
        second[-1].start()
    for copy in second:
        copy.wait_recv()
    total = jnp.zeros(near.shape[1:], F32)
    for index in range(planes):
        total = total + far[index]
    part(result, member)[...] = total
    third = []
    for step in range(1, members):
        other, device = peer(step)
        third.append(
            pltpu.make_async_remote_copy(
                part(result, member),
                part(result, member),
                send.at[2, step],
                last_in.at[step],
                device_id=device,
                device_id_type=MESH,
            )
        )
        third[-1].start()
    for copy in third:
        copy.wait_recv()
    for copy in first + second + third:
        copy.wait_send()
    known = prompts[...]
    count = result[PROMPTS : PROMPTS + 1]
    size = known.shape[0] * known.shape[1]
    grad_ref[...] = result[:PROMPTS] + (2.0 * PENALTY_RATE / size) * count * known
    square = jnp.sum(jnp.sum(known * known, axis=1, keepdims=True), axis=0, keepdims=True)
    penalty_ref[...] = PENALTY_RATE * count[:, :1] * (square / size)


def share(axes, sums, prompts):
    dp, wide = axes["dp"], axes["wide"]
    members, planes = 2 * dp, wide // 2
    rows, width = sums.shape
    dma = pltpu.SemaphoreType.DMA
    grad, penalty = pl.pallas_call(
        functools.partial(share_kernel, dp, wide),
        in_specs=[pl.BlockSpec(memory_space=pltpu.VMEM)] * 2,
        out_specs=[pl.BlockSpec(memory_space=pltpu.VMEM)] * 2,
        out_shape=[
            jax.ShapeDtypeStruct(prompts.shape, F32),
            jax.ShapeDtypeStruct((1, 1), F32),
        ],
        scratch_shapes=[
            pltpu.VMEM((members, rows // members, width), F32),
            pltpu.VMEM((planes, rows // members, width), F32),
            pltpu.VMEM((rows, width), F32),
            dma((3, max(members, planes))),
            dma((members,)),
            dma((planes,)),
            dma((members,)),
        ],
        compiler_params=pltpu.CompilerParams(collective_id=1, has_side_effects=True),
        name="share",
    )(sums, prompts)
    return grad, penalty[0, 0]


def shards(
    axes,
    tokens,
    pos_index,
    size_group,
    pos_table,
    prompts,
    norm_gains,
    w_qkv,
    w_out,
    w_up,
    w_down,
    cotangent,
):
    full_qkv = lax.all_gather(w_qkv, "wide", axis=0, tiled=True)
    full_out = lax.all_gather(w_out, "wide", axis=0, tiled=True)
    full_up = lax.all_gather(w_up, "wide", axis=0, tiled=True)
    full_down = lax.all_gather(w_down, "wide", axis=0, tiled=True)
    hidden, qkv = embed(size_group, tokens, pos_index, pos_table, prompts, norm_gains, full_qkv)
    mixed, totals = attend(size_group, qkv)
    outputs, middle_grad, mixed_grad = feed(
        size_group, hidden, mixed, cotangent, norm_gains, full_out, full_up, full_down
    )
    dq, dk, dv = attend_back(size_group, qkv, mixed_grad, mixed, totals)
    input_grad, sums = finish(size_group, hidden, middle_grad, dq, dk, dv, norm_gains, full_qkv)
    prompt_grad, penalty = share(axes, sums, prompts)
    return (outputs, input_grad, prompt_grad, penalty)


def solution(mesh):
    return jax.shard_map(
        functools.partial(shards, dict(mesh.shape)),
        mesh=mesh,
        in_specs=(
            P(("dp", "wide"), None),
            P(("dp", "wide"), None),
            P(("dp", "wide")),
            P(),
            P(),
            P(),
            P("wide", None),
            P("wide", None),
            P("wide", None),
            P("wide", None),
            P(("dp", "wide"), None),
        ),
        out_specs=(P(("dp", "wide"), None), P(("dp", "wide"), None), P(), P()),
        check_vma=False,
    )
```

```python
import functools

import jax
import jax.numpy as jnp
from jax import lax
from jax.experimental import pallas as pl
from jax.experimental.pallas import tpu as pltpu
from jax.sharding import PartitionSpec as P

HEADS = 12
HEAD_DIM = 64
PROMPTS = 50
PATCH_S = 100
PATCH_M = 196
PATCH_L = 576

EPSILON = 1e-06
PENALTY_RATE = 3e-05
SCALE = HEAD_DIM**-0.5
LOG2E = 1.4426950408889634
SCORE = SCALE * LOG2E

BF = jnp.bfloat16
F32 = jnp.float32
NN = (((1,), (0,)), ((), ()))
NT = (((1,), (1,)), ((), ()))
MESH = pl.DeviceIdType.MESH

LANES = 128
HEAD_COLS = 256
PAIRS = HEAD_COLS // LANES
GROUP_HEADS = HEAD_COLS // HEAD_DIM
SMALL = 256
LARGE = 640
CHUNKS = {SMAL: c for SMAL, c in ((SMALL, ((0, 256),)), (LARGE, ((0, 256), (256, 256), (512, 128))))}
POS_ROWS = 256
SLOT_ROWS = 64


def dot(a, b, dims=NN):
    return lax.dot_general(a, b, dims, preferred_element_type=F32)


def image_length(group):
    patches = jnp.where(group == 0, PATCH_S, jnp.where(group == 1, PATCH_M, PATCH_L))
    return jnp.where(group == 3, 0, 1 + PROMPTS + patches).astype(jnp.int32)


def total_length(groups, slots):
    total = jnp.int32(0)
    for slot in range(slots):
        total = total + image_length(groups[slot])
    return total


def row_places(groups, slots, first_row, count):
    rows = first_row + lax.broadcasted_iota(jnp.int32, (count, 1), 0)
    place = rows
    start = jnp.int32(0)
    for slot in range(slots):
        length = image_length(groups[slot])
        place = jnp.where((rows >= start) & (length > 0), rows - start, place)
        start = start + length
    live = rows < start
    prompt_slot = jnp.where(live & (place >= 1) & (place <= PROMPTS), place - 1, -1)
    return prompt_slot, live


def norm_parts(values):
    centered = values - jnp.mean(values, axis=-1, keepdims=True)
    rstd = lax.rsqrt(jnp.mean(centered * centered, axis=-1, keepdims=True) + EPSILON)
    return centered * rstd, rstd


def norm_back(normal, rstd, gain, grad):
    scaled = grad * gain
    return (
        scaled
        - jnp.mean(scaled, axis=-1, keepdims=True)
        - normal * jnp.mean(scaled * normal, axis=-1, keepdims=True)
    ) * rstd


def fill_table(table, pos_table, prompts):
    table[...] = jnp.zeros_like(table)
    table[: pos_table.shape[0]] = pos_table[...]
    rest = prompts[...]
    for piece in range(3):
        part = rest.astype(BF)
        first = POS_ROWS + piece * SLOT_ROWS
        table[first : first + PROMPTS] = part
        rest = rest - part.astype(F32)


def embedded(groups, slots, first_row, tokens, pos_index, table):
    prompt_slot, _ = row_places(groups, slots, first_row, tokens.shape[0])
    is_prompt = prompt_slot >= 0
    lane = lax.broadcasted_iota(jnp.int32, (1, POS_ROWS), 1)
    left = jnp.where(is_prompt, -1, pos_index[:, 0:1])
    right = jnp.where(is_prompt, -1, pos_index[:, 1:2])
    half_hot = jnp.where(lane == left, 0.5, 0.0) + jnp.where(lane == right, 0.5, 0.0)
    slot_lane = lax.broadcasted_iota(jnp.int32, (1, 3 * SLOT_ROWS), 1)
    slot_lane = lax.rem(slot_lane, SLOT_ROWS)
    slot_hot = jnp.where(slot_lane == prompt_slot, 1.0, 0.0)
    picked = dot(half_hot.astype(BF), table[:POS_ROWS]) + dot(
        slot_hot.astype(BF), table[POS_ROWS:]
    )
    return jnp.where(is_prompt, 0.0, tokens.astype(F32)) + picked


def embed_kernel(
    slots, groups, tokens, pos_index, pos_table, prompts, gains, w_qkv, hidden_out, qkv_out, table
):
    tile = tokens.shape[0]
    step = pl.program_id(0)

    @pl.when(step == 0)
    def _():
        fill_table(table, pos_table, prompts)

    hidden = embedded(groups, slots, step * tile, tokens[...], pos_index[...], table)
    hidden_out[...] = hidden
    normal, _ = norm_parts(hidden)
    normed = (normal * gains[0:1]).astype(BF)
    qkv_out[...] = dot(normed, w_qkv[...]).astype(BF)


def embed(size_group, tokens, pos_index, pos_table, prompts, gains, w_qkv):
    rows, width = tokens.shape
    tile = 384
    keep = lambda i, g: (0, 0)
    whole = lambda a: pl.BlockSpec(a.shape, keep, pipeline_mode=pl.Buffered(1))
    by_row = lambda columns: pl.BlockSpec((tile, columns), lambda i, g: (i, 0))
    return pl.pallas_call(
        functools.partial(embed_kernel, size_group.shape[0]),
        grid_spec=pltpu.PrefetchScalarGridSpec(
            num_scalar_prefetch=1,
            grid=(rows // tile,),
            in_specs=[
                by_row(width),
                by_row(2),
                whole(pos_table),
                whole(prompts),
                whole(gains),
                whole(w_qkv),
            ],
            out_specs=[by_row(width), by_row(3 * width)],
            scratch_shapes=[pltpu.VMEM((POS_ROWS + 3 * SLOT_ROWS, width), BF)],
        ),
        out_shape=[
            jax.ShapeDtypeStruct((rows, width), F32),
            jax.ShapeDtypeStruct((rows, 3 * width), BF),
        ],
        compiler_params=pltpu.CompilerParams(vmem_limit_bytes=40 << 20),
        name="embed",
    )(size_group, tokens, pos_index, pos_table, prompts, gains, w_qkv)


class Gather:
    def __init__(self, place, index, full, sems, by_rows=False):
        self.dp, self.wide, self.planes, self.plane, self.core = place
        self.index = index
        self.full = full
        self.send, self.recv = sems
        self.rows = full.shape[0] // (2 * self.planes)
        self.columns = full.shape[1] // 8
        self.by_rows = by_rows
        d = self.dp
        self.across = d + 1 - 2 * lax.rem(d, 2)
        self.beyond = lax.rem(d + 2, 4)

    def alpha(self, d):
        return d

    def beta(self, d):
        return 4 + 2 * lax.rem(d, 2) + d // 2

    def pair(self, slot):
        return slot - lax.rem(slot, 2)

    def shard(self, plane, core, slot=None, count=1, array=None):
        full = self.full if array is None else array
        first = pl.multiple_of((2 * plane + core) * self.rows, self.rows)
        if slot is None:
            return full.at[pl.ds(first, self.rows)]
        if self.by_rows:
            step = self.rows // 8
            return full.at[pl.ds(pl.multiple_of(first + slot * step, step), count * step)]
        column = pl.multiple_of(slot * self.columns, self.columns)
        return full.at[pl.ds(first, self.rows), pl.ds(column, count * self.columns)]

    def copy(self, ref, send, recv, device):
        return pltpu.make_async_remote_copy(
            ref,
            ref,
            self.send.at[self.index, send],
            self.recv.at[self.index, recv],
            device_id=device,
            device_id_type=MESH,
        )

    def device(self, plane):
        return (self.dp, 2 * plane + self.core)

    def nearest(self, k):
        n = self.planes
        low = 1 - self.plane // (n // 2)
        edge = low * self.plane + (1 - low) * (n - 1 - self.plane)
        other = k + 1 - (edge - k + n - 1) // n
        return low * other + (1 - low) * (n - 1 - other)

    def along_copies(self, plane):
        n = self.planes
        up = (plane <= self.plane) & (self.plane < n - 1)
        down = (plane >= self.plane) & (self.plane > 0)
        for part, slot in enumerate((self.alpha(self.dp), self.beta(self.dp))):
            ref = self.shard(plane, self.core, slot)
            sem = 2 * plane + part
            for go, sent, target in (
                (up, sem, lax.rem(self.plane + 1, n)),
                (down, 2 * n + sem, lax.rem(self.plane + n - 1, n)),
            ):
                yield go, self.copy(ref, sent, sem, self.device(target))

    def along(self, plane):
        for go, copy in self.along_copies(plane):
            pl.when(go)(copy.start)

    def wait_along(self, plane):
        for part, slot in enumerate((self.alpha(self.dp), self.beta(self.dp))):
            ref = self.shard(plane, self.core, slot)
            sem = 2 * plane + part
            self.copy(ref, sem, sem, self.device(plane)).wait_recv()

    def exchange_copies(self, plane):
        for part, (slot, d) in enumerate(
            ((self.alpha(self.dp), self.across), (self.beta(self.dp), self.beyond))
        ):
            sem = 4 * self.planes + 2 * plane + part
            yield self.copy(self.shard(plane, self.core, slot), sem, sem, (d, self.wide))

    def exchange(self, plane):
        for copy in self.exchange_copies(plane):
            copy.start()

    def wait_exchange(self, plane):
        for part, (slot, d) in enumerate(
            ((self.alpha(self.across), self.across), (self.beta(self.beyond), self.beyond))
        ):
            sem = 4 * self.planes + 2 * plane + part
            self.copy(self.shard(plane, self.core, slot), sem, sem, (d, self.wide)).wait_recv()

    def pair_copies(self, plane):
        for part, (slot, d) in enumerate(
            ((self.alpha(self.dp), self.beyond), (self.beta(self.dp), self.across))
        ):
            sem = 6 * self.planes + 2 * plane + part
            ref = self.shard(plane, self.core, self.pair(slot), 2)
            yield self.copy(ref, sem, sem, (d, self.wide))

    def exchange_pairs(self, plane):
        for copy in self.pair_copies(plane):
            copy.start()

    def wait_pairs(self, plane):
        for part, (slot, d) in enumerate(
            ((self.alpha(self.beyond), self.beyond), (self.beta(self.across), self.across))
        ):
            sem = 6 * self.planes + 2 * plane + part
            ref = self.shard(plane, self.core, self.pair(slot), 2)
            self.copy(ref, sem, sem, (d, self.wide)).wait_recv()

    def other_core(self):
        return (self.dp, 2 * self.plane + 1 - self.core)

    def give_copy(self, plane):
        sem = 8 * self.planes + plane
        return self.copy(self.shard(plane, self.core), sem, sem, self.other_core())

    def give(self, plane):
        self.give_copy(plane).start()

    def wait_all_given(self):
        for plane in range(self.planes):
            sem = 8 * self.planes + plane
            self.copy(self.shard(plane, 1 - self.core), sem, sem, self.other_core()).wait_recv()

    def begin(self):
        self.along(self.plane)
        self.give(self.plane)

    def fetch(self, k):
        plane = self.nearest(k)
        self.wait_along(plane)
        self.along(plane)

    def bring(self, k):
        self.fetch(k)
        self.exchange(self.nearest(k))

    def pass_on(self, k):
        plane = self.nearest(k)
        self.wait_exchange(plane)
        self.exchange_pairs(plane)

    def close(self, k):
        plane = self.nearest(k)
        self.wait_pairs(plane)
        self.give(plane)

    def wait_fetched(self):
        for k in range(self.planes):
            plane = self.plane if k == self.planes - 1 else self.nearest(k)
            for go, copy in self.along_copies(plane):
                pl.when(go)(copy.wait_send)

    def wait_passed(self):
        self.give_copy(self.plane).wait_send()
        for k in range(self.planes - 1):
            plane = self.nearest(k)
            for copy in self.exchange_copies(plane):
                copy.wait_send()
            for copy in self.pair_copies(plane):
                copy.wait_send()
            self.give_copy(plane).wait_send()

    def greet(self, planes=True):
        barrier = pltpu.get_barrier_semaphore()
        peers = [(self.across, self.wide), (self.beyond, self.wide), self.other_core()]
        if planes:
            peers += [
                self.device(lax.rem(self.plane + step, self.planes))
                for step in range(1, self.planes)
            ]
        for device in peers:
            pl.semaphore_signal(barrier, inc=1, device_id=device, device_id_type=MESH)
        return barrier, len(peers)

    def fetched(self, k, array=None):
        plane = self.nearest(k)
        slots = (self.alpha(self.dp), self.beta(self.dp))
        return [self.shard(plane, self.core, slot, 1, array) for slot in slots]

    @staticmethod
    def semaphores(planes):
        return 9 * planes


def gather_embed_kernel(
    planes,
    slots,
    groups,
    pos_table,
    prompts,
    gains,
    tokens_in,
    pos_index_in,
    own_qkv,
    own_out,
    own_up,
    own_down,
    hidden_out,
    qkv_out,
    full_qkv,
    full_out,
    full_up,
    part_down,
    table,
    tokens,
    pos_index,
    hidden,
    normed,
    qkv,
    first_full,
    second_full,
    third_full,
    send,
    recv,
    local,
):
    d = lax.axis_index("dp")
    w = lax.axis_index("wide")
    place = (d, w, planes, w // 2, lax.rem(w, 2))
    first = Gather(place, 0, first_full, (send, recv))
    second = Gather(place, 1, second_full, (send, recv))
    third = Gather(place, 2, third_full, (send, recv), by_rows=True)
    others = planes - 1
    qkv_columns = own_qkv.shape[1]
    barrier, greeted = first.greet()
    mine = pl.ds(pl.multiple_of(w * first.rows, first.rows), first.rows)
    loads = [
        pltpu.make_async_copy(own_qkv, first_full.at[mine, :qkv_columns], local.at[0]),
        pltpu.make_async_copy(own_out, first_full.at[mine, qkv_columns:], local.at[1]),
        pltpu.make_async_copy(own_up, second_full.at[mine], local.at[2]),
        pltpu.make_async_copy(own_down, third.shard(third.plane, third.core), local.at[3]),
        pltpu.make_async_copy(tokens_in, tokens, local.at[4]),
        pltpu.make_async_copy(pos_index_in, pos_index, local.at[5]),
    ]
    for copy in loads:
        copy.start()
    fill_table(table, pos_table, prompts)
    for copy in loads[:4]:
        copy.wait()
    pl.semaphore_wait(barrier, greeted)
    first.begin()
    second.begin()
    for copy in loads[4:]:
        copy.wait()

    rows = tokens.shape[0]
    tiles = 6
    tile = rows // tiles
    outgoing = []

    def leave(source, target):
        copy = pltpu.make_async_copy(source, target, local.at[6 + len(outgoing)])
        copy.start()
        outgoing.append(copy)

    def embed_tile(index):
        part = slice(index * tile, (index + 1) * tile)
        value = embedded(groups, slots, index * tile, tokens[part], pos_index[part], table)
        hidden[part] = value
        leave(hidden.at[part], hidden_out.at[part])
        normal, _ = norm_parts(value)
        normed[part] = (normal * gains[0:1]).astype(BF)

    def qkv_tile(index):
        part = slice(index * tile, (index + 1) * tile)
        qkv[part] = dot(normed[part], first_full[:, :qkv_columns]).astype(BF)
        leave(qkv.at[part], qkv_out.at[part])

    embed_tile(0)
    embed_tile(1)
    first.bring(0)
    embed_tile(2)
    first.bring(1)
    first.pass_on(0)
    embed_tile(3)
    first.bring(2)
    first.pass_on(1)
    embed_tile(4)
    third.along(third.plane)
    second.bring(0)
    first.pass_on(2)
    first.close(0)
    embed_tile(5)
    second.bring(1)
    second.pass_on(0)
    first.close(1)
    second.bring(2)
    second.pass_on(1)
    first.close(2)
    first.wait_all_given()
    leave(first_full.at[:, :qkv_columns], full_qkv)
    leave(first_full.at[:, qkv_columns:], full_out)
    qkv_tile(0)
    second.pass_on(2)
    second.close(0)
    qkv_tile(1)
    third.fetch(0)
    qkv_tile(2)
    second.close(1)
    third.fetch(1)
    qkv_tile(3)
    third.fetch(2)
    qkv_tile(4)
    for k in range(others):
        for source, target in zip(third.fetched(k), third.fetched(k, part_down)):
            leave(source, target)
    qkv_tile(5)
    second.close(2)
    second.wait_all_given()
    leave(second_full, full_up)
    first.wait_fetched()
    second.wait_fetched()
    third.wait_fetched()
    first.wait_passed()
    second.wait_passed()
    for copy in outgoing:
        copy.wait()


def can_gather(axes, w_qkv, w_out, w_up, w_down):
    return (
        axes["dp"] == 4
        and axes["wide"] % 4 == 0
        and w_qkv.shape[0] % 16 == 0
        and w_down.shape[0] % (8 * 16) == 0
        and w_up.shape[1] % (8 * LANES) == 0
        and (w_qkv.shape[1] + w_out.shape[1]) % (8 * LANES) == 0
    )


def gather_embed(
    axes, size_group, tokens, pos_index, pos_table, prompts, gains, w_qkv, w_out, w_up, w_down
):
    rows, width = tokens.shape
    wide = axes["wide"]
    planes = wide // 2
    depth = w_qkv.shape[0] * wide
    inner_width = w_up.shape[1]
    vmem = pl.BlockSpec(memory_space=pltpu.VMEM)
    hbm = pl.BlockSpec(memory_space=pltpu.HBM)
    dma = pltpu.SemaphoreType.DMA
    count = Gather.semaphores(planes)
    first_columns = w_qkv.shape[1] + w_out.shape[1]
    return pl.pallas_call(
        functools.partial(gather_embed_kernel, planes, size_group.shape[0]),
        in_specs=[pl.BlockSpec(memory_space=pltpu.SMEM)] + [vmem] * 3 + [hbm] * 6,
        out_specs=[hbm] * 6,
        out_shape=[
            jax.ShapeDtypeStruct((rows, width), F32),
            jax.ShapeDtypeStruct((rows, w_qkv.shape[1]), BF),
            jax.ShapeDtypeStruct((depth, w_qkv.shape[1]), BF),
            jax.ShapeDtypeStruct((depth, w_out.shape[1]), BF),
            jax.ShapeDtypeStruct((depth, inner_width), BF),
            jax.ShapeDtypeStruct((inner_width, width), BF),
        ],
        scratch_shapes=[
            pltpu.VMEM((POS_ROWS + 3 * SLOT_ROWS, width), BF),
            pltpu.VMEM((rows, width), BF),
            pltpu.VMEM((rows, 2), jnp.int32),
            pltpu.VMEM((rows, width), F32),
            pltpu.VMEM((rows, width), BF),
            pltpu.VMEM((rows, w_qkv.shape[1]), BF),
            pltpu.VMEM((depth, first_columns), BF),
            pltpu.VMEM((depth, inner_width), BF),
            pltpu.VMEM((inner_width, width), BF),
            dma((3, count)),
            dma((3, count)),
            dma((6 + 12 + 3 + 2 * (planes - 1),)),
        ],
        compiler_params=pltpu.CompilerParams(
            collective_id=0, has_side_effects=True, vmem_limit_bytes=56 << 20
        ),
        name="gather_embed",
    )(
        size_group, pos_table, prompts, gains, tokens, pos_index, w_qkv, w_out, w_up, w_down
    )


def half(values, which):
    lane = lax.broadcasted_iota(jnp.int32, values.shape, 1)
    inside = (lane < HEAD_DIM) if which == 0 else (lane >= HEAD_DIM)
    return jnp.where(inside, values, jnp.zeros_like(values))


def each_image(groups, slots, image):
    def body(slot, start):
        group = groups[slot]
        length = image_length(group)
        pl.when(group == 2)(functools.partial(image, LARGE, start, length, slot))
        pl.when(group < 2)(functools.partial(image, SMALL, start, length, slot))
        return start + length

    lax.fori_loop(0, slots, body, jnp.int32(0))


def spread(pairs):
    for spaced, block in pairs:
        for pair in range(PAIRS):
            columns = slice(LANES * pair, LANES * (pair + 1))
            spaced[pair, : block.shape[0]] = block[:, columns].astype(F32)


def collect(block, spaced):
    for pair in range(PAIRS):
        columns = slice(LANES * pair, LANES * (pair + 1))
        block[:, columns] = spaced[pair, : block.shape[0]].astype(BF)


def take(spaced, rows):
    return [spaced[pair, rows, :] for pair in range(PAIRS)]


def low(parts):
    return [part.astype(BF) for part in parts]


def head_rows(parts, head):
    return parts[head // 2][HEAD_DIM * (head % 2) : HEAD_DIM * (head % 2 + 1)]


def clear_first(*refs):
    @pl.when(pl.program_id(0) == 0)
    def _():
        for ref in refs:
            ref[...] = jnp.zeros_like(ref)


def attend_kernel(slots, groups, q_ref, k_ref, v_ref, out_ref, total_ref, qs, ks, vs, outs):
    clear_first(qs, ks, vs, outs)
    spread(((qs, q_ref), (ks, k_ref), (vs, v_ref)))
    heads = range(GROUP_HEADS)

    def image(span, start, length, slot):
        rows = pl.ds(start, span)
        query = low(take(qs, rows))
        key = low(take(ks, rows))
        value_t = low([x.T for x in take(vs, rows)])
        last = span - LANES
        tail = lax.broadcasted_iota(jnp.int32, (LANES, 1), 0) + last < length
        for first, count in CHUNKS[span]:
            scores = [
                dot(key[h // 2], half(query[h // 2][first : first + count], h % 2), NT)
                for h in heads
            ]
            scores = [
                jnp.concatenate([s[:last], jnp.where(tail, s[last:], -1e30)], 0) for s in scores
            ]
            peaks = [jnp.max(s, axis=0, keepdims=True) for s in scores]
            powers = [jnp.exp2((s - m) * SCORE) for s, m in zip(scores, peaks)]
            totals = [jnp.sum(e, axis=0, keepdims=True) for e in powers]
            mixed = [dot(head_rows(value_t, h), powers[h].astype(BF)) for h in heads]
            mixed = [o / t for o, t in zip(mixed, totals)]
            for h in heads:
                total_ref[0, GROUP_HEADS * slot + h, :, first : first + count] = peaks[
                    h
                ] * SCORE + jnp.log2(totals[h])
            for pair in range(PAIRS):
                outs[pair, pl.ds(start + first, count), :] = jnp.concatenate(
                    mixed[2 * pair : 2 * pair + 2], 0
                ).T

    each_image(groups, slots, image)
    collect(out_ref, outs)


def attend(size_group, qkv):
    rows = qkv.shape[0]
    width = qkv.shape[1] // 3
    steps = width // HEAD_COLS
    slots = size_group.shape[0]
    block = lambda shift: pl.BlockSpec((rows, HEAD_COLS), lambda i, g: (0, shift * steps + i))
    spaced = pltpu.VMEM((PAIRS, rows + LANES, LANES), F32)
    return pl.pallas_call(
        functools.partial(attend_kernel, slots),
        grid_spec=pltpu.PrefetchScalarGridSpec(
            num_scalar_prefetch=1,
            grid=(steps,),
            in_specs=[block(0), block(1), block(2)],
            out_specs=[
                block(0),
                pl.BlockSpec((1, GROUP_HEADS * slots, 1, LARGE), lambda i, g: (i, 0, 0, 0)),
            ],
            scratch_shapes=[spaced] * 4,
        ),
        out_shape=[
            jax.ShapeDtypeStruct((rows, width), BF),
            jax.ShapeDtypeStruct((steps, GROUP_HEADS * slots, 1, LARGE), F32),
        ],
        compiler_params=pltpu.CompilerParams(vmem_limit_bytes=50 << 20),
        name="attend",
    )(size_group, qkv, qkv, qkv)


def attend_back_kernel(
    slots,
    groups,
    q_ref,
    k_ref,
    v_ref,
    grad_ref,
    mixed_ref,
    total_ref,
    dq_ref,
    dk_ref,
    dv_ref,
    qs,
    ks,
    vs,
    grads,
    mixes,
    dqs,
    dks,
    dvs,
):
    clear_first(qs, ks, vs, grads, mixes, dqs, dks, dvs)
    spread(((qs, q_ref), (ks, k_ref), (vs, v_ref), (grads, grad_ref), (mixes, mixed_ref)))
    heads = range(GROUP_HEADS)

    def image(span, start, length, slot):
        rows = pl.ds(start, span)
        query = low(take(qs, rows))
        key = low(take(ks, rows))
        key_t = low([x.T for x in take(ks, rows)])
        value = low(take(vs, rows))
        inside = lax.broadcasted_iota(jnp.int32, (span, 1), 0) < length
        grad32 = [jnp.where(inside, x, 0.0) for x in take(grads, rows)]
        products = [(x * y).T for x, y in zip(grad32, take(mixes, rows))]
        grad = low(grad32)
        last = span - LANES
        tail = inside[last:]
        dk = [jnp.zeros((span, LANES), F32)] * PAIRS
        dv = [jnp.zeros((span, LANES), F32)] * PAIRS
        for first, count in CHUNKS[span]:
            part = slice(first, first + count)
            query_h = [half(query[h // 2][part], h % 2) for h in heads]
            grad_h = [half(grad[h // 2][part], h % 2) for h in heads]
            scores = [dot(key[h // 2], query_h[h], NT) for h in heads]
            prob_grads = [dot(value[h // 2], grad_h[h], NT) for h in heads]
            probs = [
                jnp.exp2(scores[h] * SCORE - total_ref[0, GROUP_HEADS * slot + h, :, part])
                for h in heads
            ]
            probs = [
                jnp.concatenate([p[:last], jnp.where(tail, p[last:], 0.0)], 0) for p in probs
            ]
            deltas = [
                jnp.sum(head_rows(products, h)[:, part], axis=0, keepdims=True) for h in heads
            ]
            score_grads = [(probs[h] * (prob_grads[h] - deltas[h])).astype(BF) for h in heads]
            for h in heads:
                dv[h // 2] += dot(probs[h].astype(BF), grad_h[h])
                dk[h // 2] += dot(score_grads[h], query_h[h])
            dq = [dot(head_rows(key_t, h), score_grads[h]) for h in heads]
            for pair in range(PAIRS):
                dqs[pair, pl.ds(start + first, count), :] = (
                    jnp.concatenate(dq[2 * pair : 2 * pair + 2], 0).T * SCALE
                )
        for pair in range(PAIRS):
            dks[pair, rows, :] = dk[pair] * SCALE
            dvs[pair, rows, :] = dv[pair]

    each_image(groups, slots, image)
    collect(dq_ref, dqs)
    collect(dk_ref, dks)
    collect(dv_ref, dvs)


def attend_back(size_group, qkv, mixed_grad, mixed, totals):
    rows = qkv.shape[0]
    width = qkv.shape[1] // 3
    steps = width // HEAD_COLS
    slots = size_group.shape[0]
    block = lambda shift: pl.BlockSpec((rows, HEAD_COLS), lambda i, g: (0, shift * steps + i))
    spaced = pltpu.VMEM((PAIRS, rows + LANES, LANES), F32)
    return pl.pallas_call(
        functools.partial(attend_back_kernel, slots),
        grid_spec=pltpu.PrefetchScalarGridSpec(
            num_scalar_prefetch=1,
            grid=(steps,),
            in_specs=[
                block(0),
                block(1),
                block(2),
                block(0),
                block(0),
                pl.BlockSpec((1, GROUP_HEADS * slots, 1, LARGE), lambda i, g: (i, 0, 0, 0)),
            ],
            out_specs=[block(0)] * 3,
            scratch_shapes=[spaced] * 8,
        ),
        out_shape=[jax.ShapeDtypeStruct((rows, width), BF)] * 3,
        compiler_params=pltpu.CompilerParams(vmem_limit_bytes=56 << 20),
        name="attend_back",
    )(size_group, qkv, qkv, qkv, mixed_grad, mixed, totals)


def feed_kernel(
    slots,
    chunk,
    groups,
    hidden,
    mixed,
    cotangent,
    gains,
    w_out,
    w_up,
    w_down,
    out_ref,
    middle_grad_ref,
    mixed_grad_ref,
):
    tile = hidden.shape[0]
    inner_width = w_up.shape[1]
    rows = pl.program_id(0) * tile + lax.broadcasted_iota(jnp.int32, (tile, 1), 0)
    live = rows < total_length(groups, slots)
    out_grad = jnp.where(live, cotangent[...].astype(F32), 0.0)
    out_grad_low = out_grad.astype(BF)
    middle = hidden[...] + dot(mixed[...], w_out[...])
    normal, rstd = norm_parts(middle)
    gain = gains[1:2]
    second = (normal * gain).astype(BF)
    forward = middle
    back = jnp.zeros_like(middle)
    for first in range(0, inner_width, chunk):
        part = slice(first, first + chunk)
        inner = dot(second, w_up[:, part])
        act_grad = dot(out_grad_low, w_down[part], NT)
        phi = 0.5 + 0.5 * lax.erf(inner * (0.5**0.5))
        density = jnp.exp2(inner * inner * (-0.5 * LOG2E)) * 0.3989422804014327
        activated = (inner * phi).astype(BF)
        inner_grad = (act_grad * (phi + inner * density)).astype(BF)
        forward = forward + dot(activated, w_down[part])
        back = back + dot(inner_grad, w_up[:, part], NT)
    out_ref[...] = jnp.where(live, forward, 0.0).astype(BF)
    middle_grad = out_grad + norm_back(normal, rstd, gain, back)
    middle_grad_ref[...] = middle_grad
    mixed_grad_ref[...] = dot(middle_grad.astype(BF), w_out[...], NT).astype(BF)


def feed(size_group, hidden, mixed, cotangent, gains, w_out, w_up, w_down):
    rows, width = hidden.shape
    tile = 384
    chunk = 512
    keep = lambda i, g: (0, 0)
    whole = lambda a: pl.BlockSpec(a.shape, keep, pipeline_mode=pl.Buffered(1))
    by_row = pl.BlockSpec((tile, width), lambda i, g: (i, 0))
    return pl.pallas_call(
        functools.partial(feed_kernel, size_group.shape[0], chunk),
        grid_spec=pltpu.PrefetchScalarGridSpec(
            num_scalar_prefetch=1,
            grid=(rows // tile,),
            in_specs=[by_row, by_row, by_row, whole(gains), whole(w_out), whole(w_up), whole(w_down)],
            out_specs=[by_row, by_row, by_row],
        ),
        out_shape=[
            jax.ShapeDtypeStruct((rows, width), BF),
            jax.ShapeDtypeStruct((rows, width), F32),
            jax.ShapeDtypeStruct((rows, width), BF),
        ],
        compiler_params=pltpu.CompilerParams(vmem_limit_bytes=56 << 20),
        name="feed",
    )(size_group, hidden, mixed, cotangent, gains, w_out, w_up, w_down)


def gather_feed_kernel(
    planes,
    slots,
    chunk,
    groups,
    gains,
    hidden_in,
    mixed_in,
    cotangent_in,
    full_out,
    full_up,
    own_down,
    part_down,
    out_ref,
    middle_grad_ref,
    mixed_grad_ref,
    middle,
    mixed,
    cotangent,
    w_out,
    w_up,
    w_down,
    active,
    slope,
    send,
    recv,
    weights_in,
    rows_in,
    rows_out,
):
    d = lax.axis_index("dp")
    w = lax.axis_index("wide")
    down = Gather((d, w, planes, w // 2, lax.rem(w, 2)), 0, w_down, (send, recv), by_rows=True)
    barrier, greeted = down.greet(planes=False)
    others = planes - 1
    tiles = rows_in.shape[0]
    tile = middle.shape[0] // tiles
    inner_width = w_up.shape[1]

    def tile_rows(index):
        return pl.ds(pl.multiple_of(index * tile, tile), tile)

    def loads(index):
        part = tile_rows(index)
        return [
            pltpu.make_async_copy(hidden_in.at[part], middle.at[part], rows_in.at[index, 0]),
            pltpu.make_async_copy(mixed_in.at[part], mixed.at[part], rows_in.at[index, 1]),
            pltpu.make_async_copy(cotangent_in.at[part], cotangent.at[part], rows_in.at[index, 2]),
        ]

    def stores(index):
        part = tile_rows(index)
        return [
            pltpu.make_async_copy(middle.at[part], middle_grad_ref.at[part], rows_out.at[index, 0]),
            pltpu.make_async_copy(mixed.at[part], mixed_grad_ref.at[part], rows_out.at[index, 1]),
            pltpu.make_async_copy(cotangent.at[part], out_ref.at[part], rows_out.at[index, 2]),
        ]

    down_loads = [(own_down, down.shard(down.plane, down.core))]
    for k in range(others):
        down_loads += list(zip(down.fetched(k, part_down), down.fetched(k)))
    down_loads = [
        pltpu.make_async_copy(source, target, weights_in.at[2 + index])
        for index, (source, target) in enumerate(down_loads)
    ]
    out_load = pltpu.make_async_copy(full_out, w_out, weights_in.at[0])
    up_load = pltpu.make_async_copy(full_up, w_up, weights_in.at[1])
    for copy in down_loads:
        copy.start()
    out_load.start()
    for copy in loads(0):
        copy.start()
    up_load.start()
    for index in range(1, tiles):
        for copy in loads(index):
            copy.start()
    for copy in down_loads:
        copy.wait()
    pl.semaphore_wait(barrier, greeted)
    for k in range(others):
        down.exchange(down.nearest(k))
    down.give(down.plane)
    out_load.wait()
    up_load.wait()
    gain = gains[1:2]

    def pump(step):
        @pl.when((step >= 0) & (step < others))
        def _():
            down.pass_on(step)

        @pl.when((step >= 2) & (step < others + 2))
        def _():
            down.close(step - 2)

    def up_tile(index, carry):
        for copy in loads(index):
            copy.wait()
        part = tile_rows(index)
        value = middle[part, :] + dot(mixed[part, :], w_out[...])
        middle[part, :] = value
        normal, _ = norm_parts(value)
        second = (normal * gain).astype(BF)
        for first in range(0, inner_width, chunk):
            columns = slice(first, first + chunk)
            inner = dot(second, w_up[:, columns])
            phi = 0.5 + 0.5 * lax.erf(inner * (0.5**0.5))
            density = jnp.exp2(inner * inner * (-0.5 * LOG2E)) * 0.3989422804014327
            active[part, columns] = (inner * phi).astype(BF)
            slope[part, columns] = phi + inner * density
            if first + chunk == inner_width // 2:
                pump(2 * index)
        pump(2 * index + 1)
        return carry

    lax.fori_loop(0, tiles, up_tile, 0)
    for step in range(2 * tiles, others + 2):
        pump(step)
    down.wait_all_given()
    total = total_length(groups, slots)

    def down_tile(index, carry):
        part = tile_rows(index)
        rows = index * tile + lax.broadcasted_iota(jnp.int32, (tile, 1), 0)
        live = rows < total
        out_grad = jnp.where(live, cotangent[part, :].astype(F32), 0.0)
        out_grad_low = out_grad.astype(BF)
        value = middle[part, :]
        back = jnp.zeros_like(value)
        for first in range(0, inner_width, chunk):
            columns = slice(first, first + chunk)
            act_grad = dot(out_grad_low, w_down[columns], NT)
            inner_grad = (act_grad * slope[part, columns]).astype(BF)
            back = back + dot(inner_grad, w_up[:, columns], NT)
        forward = value + dot(active[part, :], w_down[...])
        cotangent[part, :] = jnp.where(live, forward, 0.0).astype(BF)
        normal, rstd = norm_parts(value)
        middle_grad = out_grad + norm_back(normal, rstd, gain, back)
        middle[part, :] = middle_grad
        mixed[part, :] = dot(middle_grad.astype(BF), w_out[...], NT).astype(BF)
        for copy in stores(index):
            copy.start()
        return carry

    lax.fori_loop(0, tiles, down_tile, 0)
    down.wait_passed()
    for index in range(tiles):
        for copy in stores(index):
            copy.wait()


def gather_feed(axes, size_group, hidden, mixed, cotangent, gains, w_out, w_up, w_down, part_down):
    rows, width = hidden.shape
    planes = axes["wide"] // 2
    inner_width = w_up.shape[1]
    tiles = 3
    hbm = pl.BlockSpec(memory_space=pltpu.HBM)
    dma = pltpu.SemaphoreType.DMA
    count = Gather.semaphores(planes)
    return pl.pallas_call(
        functools.partial(gather_feed_kernel, planes, size_group.shape[0], 512),
        in_specs=[
            pl.BlockSpec(memory_space=pltpu.SMEM),
            pl.BlockSpec(memory_space=pltpu.VMEM),
        ]
        + [hbm] * 7,
        out_specs=[hbm] * 3,
        out_shape=[
            jax.ShapeDtypeStruct((rows, width), BF),
            jax.ShapeDtypeStruct((rows, width), F32),
            jax.ShapeDtypeStruct((rows, width), BF),
        ],
        scratch_shapes=[
            pltpu.VMEM((rows, width), F32),
            pltpu.VMEM((rows, width), BF),
            pltpu.VMEM((rows, width), BF),
            pltpu.VMEM(w_out.shape, BF),
            pltpu.VMEM(w_up.shape, BF),
            pltpu.VMEM((inner_width, width), BF),
            pltpu.VMEM((rows, inner_width), BF),
            pltpu.VMEM((rows, inner_width), F32),
            dma((1, count)),
            dma((1, count)),
            dma((3 + 2 * (planes - 1),)),
            dma((tiles, 3)),
            dma((tiles, 3)),
        ],
        compiler_params=pltpu.CompilerParams(
            collective_id=2, has_side_effects=True, vmem_limit_bytes=58 << 20
        ),
        name="gather_feed",
    )(size_group, gains, hidden, mixed, cotangent, w_out, w_up, w_down, part_down)


def finish_kernel(
    slots, groups, hidden, middle_grad, dq, dk, dv, gains, w_qkv, grad_ref, sums_ref, kept
):
    tile, width = hidden.shape
    step = pl.program_id(0)
    normed_grad = (
        dot(dq[...], w_qkv[:, :width], NT)
        + dot(dk[...], w_qkv[:, width : 2 * width], NT)
        + dot(dv[...], w_qkv[:, 2 * width :], NT)
    )
    normal, rstd = norm_parts(hidden[...])
    hidden_grad = middle_grad[...] + norm_back(normal, rstd, gains[0:1], normed_grad)
    prompt_slot, live = row_places(groups, slots, step * tile, tile)
    grad_ref[...] = jnp.where(live & (prompt_slot < 0), hidden_grad, 0.0).astype(BF)
    for column in range(width // LANES):
        kept[column, pl.ds(pl.multiple_of(step * tile, tile), tile), :] = hidden_grad[
            :, LANES * column : LANES * (column + 1)
        ]

    @pl.when(step == pl.num_programs(0) - 1)
    def _():
        total = total_length(groups, slots).astype(F32)
        slot_row = lax.broadcasted_iota(jnp.int32, (SLOT_ROWS, LANES), 0)
        for column in range(width // LANES):
            start = jnp.int32(0)
            sums = jnp.zeros((SLOT_ROWS, LANES), F32)
            for slot in range(slots):
                length = image_length(groups[slot])
                first = jnp.where(length > 0, start + 1, 0)
                taken = kept[column, pl.ds(first, SLOT_ROWS), :]
                sums = sums + jnp.where(length > 0, taken, 0.0)
                start = start + length
            sums_ref[:, LANES * column : LANES * (column + 1)] = jnp.where(
                slot_row < PROMPTS, sums, jnp.where(slot_row == PROMPTS, total, 0.0)
            )


def finish(size_group, hidden, middle_grad, dq, dk, dv, gains, w_qkv):
    rows, width = hidden.shape
    tile = 384
    keep = lambda i, g: (0, 0)
    whole = lambda a: pl.BlockSpec(a.shape, keep, pipeline_mode=pl.Buffered(1))
    by_row = pl.BlockSpec((tile, width), lambda i, g: (i, 0))
    return pl.pallas_call(
        functools.partial(finish_kernel, size_group.shape[0]),
        grid_spec=pltpu.PrefetchScalarGridSpec(
            num_scalar_prefetch=1,
            grid=(rows // tile,),
            in_specs=[by_row] * 5 + [whole(gains), whole(w_qkv)],
            out_specs=[by_row, pl.BlockSpec((SLOT_ROWS, width), keep)],
            scratch_shapes=[pltpu.VMEM((width // LANES, rows, LANES), F32)],
        ),
        out_shape=[
            jax.ShapeDtypeStruct((rows, width), BF),
            jax.ShapeDtypeStruct((SLOT_ROWS, width), F32),
        ],
        compiler_params=pltpu.CompilerParams(vmem_limit_bytes=50 << 20),
        name="finish",
    )(size_group, hidden, middle_grad, dq, dk, dv, gains, w_qkv)


def share_kernel(
    dp, wide, sums, prompts, grad_ref, penalty_ref, near, far, result, send, near_in, far_in, last_in
):
    members = 2 * dp
    planes = wide // 2
    slice_rows = SLOT_ROWS // members
    d = lax.axis_index("dp")
    w = lax.axis_index("wide")
    plane = w // 2
    member = d * 2 + lax.rem(w, 2)

    def peer(step):
        other = lax.rem(member + step, members)
        return other, (other // 2, plane * 2 + lax.rem(other, 2))

    def plane_peer(step):
        other = lax.rem(plane + step, planes)
        return other, (d, other * 2 + lax.rem(w, 2))

    barrier = pltpu.get_barrier_semaphore()
    for step in range(1, members):
        pl.semaphore_signal(barrier, inc=1, device_id=peer(step)[1], device_id_type=MESH)
    for step in range(1, planes):
        pl.semaphore_signal(barrier, inc=1, device_id=plane_peer(step)[1], device_id_type=MESH)
    pl.semaphore_wait(barrier, members + planes - 2)

    def part(ref, index):
        return ref.at[pl.ds(pl.multiple_of(index * slice_rows, slice_rows), slice_rows)]

    first = []
    for step in range(1, members):
        other, device = peer(step)
        first.append(
            pltpu.make_async_remote_copy(
                part(sums, other),
                near.at[step],
                send.at[0, step],
                near_in.at[step],
                device_id=device,
                device_id_type=MESH,
            )
        )
        first[-1].start()
    near[0] = part(sums, member)[...]
    for copy in first:
        copy.wait_recv()
    total = jnp.zeros(near.shape[1:], F32)
    for index in range(members):
        total = total + near[lax.rem(member - index + members, members)]
    far[plane] = total
    second = []
    for step in range(1, planes):
        other, device = plane_peer(step)
        second.append(
            pltpu.make_async_remote_copy(
                far.at[plane],
                far.at[plane],
                send.at[1, step],
                far_in.at[step],
                device_id=device,
                device_id_type=MESH,
            )
        )
        second[-1].start()
    for copy in second:
        copy.wait_recv()
    total = jnp.zeros(near.shape[1:], F32)
    for index in range(planes):
        total = total + far[index]
    part(result, member)[...] = total
    third = []
    for step in range(1, members):
        other, device = peer(step)
        third.append(
            pltpu.make_async_remote_copy(
                part(result, member),
                part(result, member),
                send.at[2, step],
                last_in.at[step],
                device_id=device,
                device_id_type=MESH,
            )
        )
        third[-1].start()
    for copy in third:
        copy.wait_recv()
    for copy in first + second + third:
        copy.wait_send()
    known = prompts[...]
    count = result[PROMPTS : PROMPTS + 1]
    size = known.shape[0] * known.shape[1]
    grad_ref[...] = result[:PROMPTS] + (2.0 * PENALTY_RATE / size) * count * known
    square = jnp.sum(jnp.sum(known * known, axis=1, keepdims=True), axis=0, keepdims=True)
    penalty_ref[...] = PENALTY_RATE * count[:, :1] * (square / size)


def share(axes, sums, prompts):
    dp, wide = axes["dp"], axes["wide"]
    members, planes = 2 * dp, wide // 2
    rows, width = sums.shape
    dma = pltpu.SemaphoreType.DMA
    grad, penalty = pl.pallas_call(
        functools.partial(share_kernel, dp, wide),
        in_specs=[pl.BlockSpec(memory_space=pltpu.VMEM)] * 2,
        out_specs=[pl.BlockSpec(memory_space=pltpu.VMEM)] * 2,
        out_shape=[
            jax.ShapeDtypeStruct(prompts.shape, F32),
            jax.ShapeDtypeStruct((1, 1), F32),
        ],
        scratch_shapes=[
            pltpu.VMEM((members, rows // members, width), F32),
            pltpu.VMEM((planes, rows // members, width), F32),
            pltpu.VMEM((rows, width), F32),
            dma((3, max(members, planes))),
            dma((members,)),
            dma((planes,)),
            dma((members,)),
        ],
        compiler_params=pltpu.CompilerParams(collective_id=1, has_side_effects=True),
        name="share",
    )(sums, prompts)
    return grad, penalty[0, 0]


def shards(
    axes,
    tokens,
    pos_index,
    size_group,
    pos_table,
    prompts,
    norm_gains,
    w_qkv,
    w_out,
    w_up,
    w_down,
    cotangent,
):
    if can_gather(axes, w_qkv, w_out, w_up, w_down):
        hidden, qkv, full_qkv, full_out, full_up, part_down = gather_embed(
            axes,
            size_group,
            tokens,
            pos_index,
            pos_table,
            prompts,
            norm_gains,
            w_qkv,
            w_out,
            w_up,
            w_down,
        )
        mixed, totals = attend(size_group, qkv)
        outputs, middle_grad, mixed_grad = gather_feed(
            axes,
            size_group,
            hidden,
            mixed,
            cotangent,
            norm_gains,
            full_out,
            full_up,
            w_down,
            part_down,
        )
    else:
        full_qkv = lax.all_gather(w_qkv, "wide", axis=0, tiled=True)
        full_out = lax.all_gather(w_out, "wide", axis=0, tiled=True)
        full_up = lax.all_gather(w_up, "wide", axis=0, tiled=True)
        full_down = lax.all_gather(w_down, "wide", axis=0, tiled=True)
        hidden, qkv = embed(size_group, tokens, pos_index, pos_table, prompts, norm_gains, full_qkv)
        mixed, totals = attend(size_group, qkv)
        outputs, middle_grad, mixed_grad = feed(
            size_group, hidden, mixed, cotangent, norm_gains, full_out, full_up, full_down
        )
    dq, dk, dv = attend_back(size_group, qkv, mixed_grad, mixed, totals)
    input_grad, sums = finish(size_group, hidden, middle_grad, dq, dk, dv, norm_gains, full_qkv)
    prompt_grad, penalty = share(axes, sums, prompts)
    return (outputs, input_grad, prompt_grad, penalty)


def solution(mesh):
    return jax.shard_map(
        functools.partial(shards, dict(mesh.shape)),
        mesh=mesh,
        in_specs=(
            P(("dp", "wide"), None),
            P(("dp", "wide"), None),
            P(("dp", "wide")),
            P(),
            P(),
            P(),
            P("wide", None),
            P("wide", None),
            P("wide", None),
            P("wide", None),
            P(("dp", "wide"), None),
        ),
        out_specs=(P(("dp", "wide"), None), P(("dp", "wide"), None), P(), P()),
        check_vma=False,
    )
```

```python
import functools

import jax
import jax.numpy as jnp
from jax import lax
from jax.experimental import pallas as pl
from jax.experimental.pallas import tpu as pltpu
from jax.sharding import PartitionSpec as P

HEADS = 12
HEAD_DIM = 64
PROMPTS = 50
PATCH_S = 100
PATCH_M = 196
PATCH_L = 576

EPSILON = 1e-06
PENALTY_RATE = 3e-05
SCALE = HEAD_DIM**-0.5
LOG2E = 1.4426950408889634
SCORE = SCALE * LOG2E

BF = jnp.bfloat16
F32 = jnp.float32
NN = (((1,), (0,)), ((), ()))
NT = (((1,), (1,)), ((), ()))
MESH = pl.DeviceIdType.MESH

LANES = 128
HEAD_COLS = 256
PAIRS = HEAD_COLS // LANES
GROUP_HEADS = HEAD_COLS // HEAD_DIM
SMALL = 256
LARGE = 640
CHUNKS = {SMAL: c for SMAL, c in ((SMALL, ((0, 256),)), (LARGE, ((0, 256), (256, 256), (512, 128))))}
POS_ROWS = 256
VMEM_LIMIT = 60 << 20
SLOT_ROWS = 64


def dot(a, b, dims=NN):
    return lax.dot_general(a, b, dims, preferred_element_type=F32)


def image_length(group):
    patches = jnp.where(group == 0, PATCH_S, jnp.where(group == 1, PATCH_M, PATCH_L))
    return jnp.where(group == 3, 0, 1 + PROMPTS + patches).astype(jnp.int32)


def total_length(groups, slots):
    total = jnp.int32(0)
    for slot in range(slots):
        total = total + image_length(groups[slot])
    return total


def row_places(groups, slots, first_row, count):
    rows = first_row + lax.broadcasted_iota(jnp.int32, (count, 1), 0)
    place = rows
    start = jnp.int32(0)
    for slot in range(slots):
        length = image_length(groups[slot])
        place = jnp.where((rows >= start) & (length > 0), rows - start, place)
        start = start + length
    live = rows < start
    prompt_slot = jnp.where(live & (place >= 1) & (place <= PROMPTS), place - 1, -1)
    return prompt_slot, live


def norm_parts(values):
    centered = values - jnp.mean(values, axis=-1, keepdims=True)
    rstd = lax.rsqrt(jnp.mean(centered * centered, axis=-1, keepdims=True) + EPSILON)
    return centered * rstd, rstd


def norm_back(normal, rstd, gain, grad):
    scaled = grad * gain
    return (
        scaled
        - jnp.mean(scaled, axis=-1, keepdims=True)
        - normal * jnp.mean(scaled * normal, axis=-1, keepdims=True)
    ) * rstd


def fill_table(table, pos_table, prompts):
    table[...] = jnp.zeros_like(table)
    table[: pos_table.shape[0]] = pos_table[...]
    rest = prompts[...]
    for piece in range(3):
        part = rest.astype(BF)
        first = POS_ROWS + piece * SLOT_ROWS
        table[first : first + PROMPTS] = part
        rest = rest - part.astype(F32)


def embedded(groups, slots, first_row, tokens, pos_index, table):
    prompt_slot, _ = row_places(groups, slots, first_row, tokens.shape[0])
    is_prompt = prompt_slot >= 0
    lane = lax.broadcasted_iota(jnp.int32, (1, POS_ROWS), 1)
    left = jnp.where(is_prompt, -1, pos_index[:, 0:1])
    right = jnp.where(is_prompt, -1, pos_index[:, 1:2])
    half_hot = jnp.where(lane == left, 0.5, 0.0) + jnp.where(lane == right, 0.5, 0.0)
    slot_lane = lax.broadcasted_iota(jnp.int32, (1, 3 * SLOT_ROWS), 1)
    slot_lane = lax.rem(slot_lane, SLOT_ROWS)
    slot_hot = jnp.where(slot_lane == prompt_slot, 1.0, 0.0)
    picked = dot(half_hot.astype(BF), table[:POS_ROWS]) + dot(
        slot_hot.astype(BF), table[POS_ROWS:]
    )
    return jnp.where(is_prompt, 0.0, tokens.astype(F32)) + picked


def embed_kernel(
    slots, groups, tokens, pos_index, pos_table, prompts, gains, w_qkv, hidden_out, qkv_out, table
):
    tile = tokens.shape[0]
    step = pl.program_id(0)

    @pl.when(step == 0)
    def _():
        fill_table(table, pos_table, prompts)

    hidden = embedded(groups, slots, step * tile, tokens[...], pos_index[...], table)
    hidden_out[...] = hidden
    normal, _ = norm_parts(hidden)
    normed = (normal * gains[0:1]).astype(BF)
    qkv_out[...] = dot(normed, w_qkv[...]).astype(BF)


def embed(size_group, tokens, pos_index, pos_table, prompts, gains, w_qkv):
    rows, width = tokens.shape
    tile = 384
    keep = lambda i, g: (0, 0)
    whole = lambda a: pl.BlockSpec(a.shape, keep, pipeline_mode=pl.Buffered(1))
    by_row = lambda columns: pl.BlockSpec((tile, columns), lambda i, g: (i, 0))
    return pl.pallas_call(
        functools.partial(embed_kernel, size_group.shape[0]),
        grid_spec=pltpu.PrefetchScalarGridSpec(
            num_scalar_prefetch=1,
            grid=(rows // tile,),
            in_specs=[
                by_row(width),
                by_row(2),
                whole(pos_table),
                whole(prompts),
                whole(gains),
                whole(w_qkv),
            ],
            out_specs=[by_row(width), by_row(3 * width)],
            scratch_shapes=[pltpu.VMEM((POS_ROWS + 3 * SLOT_ROWS, width), BF)],
        ),
        out_shape=[
            jax.ShapeDtypeStruct((rows, width), F32),
            jax.ShapeDtypeStruct((rows, 3 * width), BF),
        ],
        compiler_params=pltpu.CompilerParams(vmem_limit_bytes=VMEM_LIMIT),
        name="embed",
    )(size_group, tokens, pos_index, pos_table, prompts, gains, w_qkv)


ORDER = (
    ("own", 0, 0), ("own", 0, 1), ("own", 1, 0), ("bring", 0, 0, 0), ("bring", 0, 0, 1),
    ("own", 1, 1), ("embed",), ("pass_on", 0, 0, 0), ("bring", 1, 0, 0), ("bring", 0, 1, 0),
    ("embed",), ("pass_on", 0, 0, 1), ("bring", 0, 1, 1), ("bring", 1, 0, 1),
    ("bring", 0, 2, 0), ("give", 0), ("bring", 0, 2, 1), ("give", 1), ("pass_on", 0, 1, 1),
    ("embed",), ("pass_on", 0, 1, 0), ("bring", 1, 2, 1), ("close", 0, 0), ("bring", 1, 2, 0),
    ("embed",), ("own", 2, 1), ("pass_on", 0, 2, 0), ("pass_on", 0, 2, 1), ("bring", 1, 1, 0),
    ("pass_on", 1, 2, 1), ("own", 2, 0), ("embed",), ("pass_on", 1, 2, 0), ("close", 0, 1),
    ("fetch", 2, 0, 1), ("bring", 1, 1, 1), ("embed",), ("pass_on", 1, 0, 0), ("close", 0, 2),
    ("fetch", 2, 1, 0), ("pass_on", 1, 0, 1), ("fetch", 2, 0, 0), ("all", 0),
    ("pass_on", 1, 1, 0), ("fetch", 2, 1, 1), ("qkv",), ("qkv",), ("pass_on", 1, 1, 1),
    ("qkv",), ("close", 1, 2), ("fetch", 2, 2, 1), ("close", 1, 0), ("qkv",), ("qkv",),
    ("qkv",), ("close", 1, 1), ("fetch", 2, 2, 0), ("all", 1),
)


class Gather:
    def __init__(self, place, index, full, sems, by_rows=False):
        self.dp, self.wide, self.planes, self.plane, self.core = place
        self.index = index
        self.full = full
        self.send, self.recv = sems
        self.rows = full.shape[0] // (2 * self.planes)
        self.columns = full.shape[1] // 8
        self.by_rows = by_rows
        d = self.dp
        self.across = d + 1 - 2 * lax.rem(d, 2)
        self.beyond = lax.rem(d + 2, 4)

    def alpha(self, d):
        return d

    def beta(self, d):
        return 4 + 2 * lax.rem(d, 2) + d // 2

    def pair(self, slot):
        return slot - lax.rem(slot, 2)

    def shard(self, plane, core, slot=None, count=1, array=None):
        full = self.full if array is None else array
        first = pl.multiple_of((2 * plane + core) * self.rows, self.rows)
        if slot is None:
            return full.at[pl.ds(first, self.rows)]
        if self.by_rows:
            step = self.rows // 8
            return full.at[pl.ds(pl.multiple_of(first + slot * step, step), count * step)]
        column = pl.multiple_of(slot * self.columns, self.columns)
        return full.at[pl.ds(first, self.rows), pl.ds(column, count * self.columns)]

    def copy(self, ref, send, recv, device):
        return pltpu.make_async_remote_copy(
            ref,
            ref,
            self.send.at[self.index, send],
            self.recv.at[self.index, recv],
            device_id=device,
            device_id_type=MESH,
        )

    def device(self, plane):
        return (self.dp, 2 * plane + self.core)

    def nearest(self, k):
        n = self.planes
        low = 1 - self.plane // (n // 2)
        edge = low * self.plane + (1 - low) * (n - 1 - self.plane)
        other = k + 1 - (edge - k + n - 1) // n
        return low * other + (1 - low) * (n - 1 - other)

    def along_copies(self, plane, parts=(0, 1)):
        n = self.planes
        up = (plane <= self.plane) & (self.plane < n - 1)
        down = (plane >= self.plane) & (self.plane > 0)
        for part in parts:
            slot = (self.alpha(self.dp), self.beta(self.dp))[part]
            ref = self.shard(plane, self.core, slot)
            sem = 2 * plane + part
            for go, sent, target in (
                (up, sem, lax.rem(self.plane + 1, n)),
                (down, 2 * n + sem, lax.rem(self.plane + n - 1, n)),
            ):
                yield go, self.copy(ref, sent, sem, self.device(target))

    def along(self, plane, parts=(0, 1)):
        for go, copy in self.along_copies(plane, parts):
            pl.when(go)(copy.start)

    def wait_along(self, plane, parts=(0, 1)):
        for part in parts:
            slot = (self.alpha(self.dp), self.beta(self.dp))[part]
            ref = self.shard(plane, self.core, slot)
            sem = 2 * plane + part
            self.copy(ref, sem, sem, self.device(plane)).wait_recv()

    def exchange_copies(self, plane):
        for part, (slot, d) in enumerate(
            ((self.alpha(self.dp), self.across), (self.beta(self.dp), self.beyond))
        ):
            sem = 4 * self.planes + 2 * plane + part
            yield self.copy(self.shard(plane, self.core, slot), sem, sem, (d, self.wide))

    def exchange(self, plane):
        for copy in self.exchange_copies(plane):
            copy.start()

    def wait_one_exchange(self, plane, part):
        d = (self.across, self.beyond)[part]
        slot = (self.alpha, self.beta)[part](d)
        sem = 4 * self.planes + 2 * plane + part
        self.copy(self.shard(plane, self.core, slot), sem, sem, (d, self.wide)).wait_recv()

    def pair_copies(self, plane):
        for part, (slot, d) in enumerate(
            ((self.alpha(self.dp), self.beyond), (self.beta(self.dp), self.across))
        ):
            sem = 6 * self.planes + 2 * plane + part
            ref = self.shard(plane, self.core, self.pair(slot), 2)
            yield self.copy(ref, sem, sem, (d, self.wide))

    def wait_pairs(self, plane):
        for part, (slot, d) in enumerate(
            ((self.alpha(self.beyond), self.beyond), (self.beta(self.across), self.across))
        ):
            sem = 6 * self.planes + 2 * plane + part
            ref = self.shard(plane, self.core, self.pair(slot), 2)
            self.copy(ref, sem, sem, (d, self.wide)).wait_recv()

    def other_core(self):
        return (self.dp, 2 * self.plane + 1 - self.core)

    def give_copy(self, plane):
        sem = 8 * self.planes + plane
        return self.copy(self.shard(plane, self.core), sem, sem, self.other_core())

    def give(self, plane):
        self.give_copy(plane).start()

    def wait_given(self, plane):
        sem = 8 * self.planes + plane
        self.copy(self.shard(plane, 1 - self.core), sem, sem, self.other_core()).wait_recv()

    def wait_all_given(self):
        for plane in range(self.planes):
            self.wait_given(plane)

    def fetch(self, k, part):
        plane = self.nearest(k)
        self.wait_along(plane, (part,))
        self.along(plane, (part,))

    def bring(self, k, part):
        self.fetch(k, part)
        list(self.exchange_copies(self.nearest(k)))[part].start()

    def pass_on(self, k, part):
        plane = self.nearest(k)
        self.wait_one_exchange(plane, part)
        list(self.pair_copies(plane))[part].start()

    def close(self, k):
        plane = self.nearest(k)
        self.wait_pairs(plane)
        self.give(plane)

    def wait_fetched(self):
        for k in range(self.planes):
            plane = self.plane if k == self.planes - 1 else self.nearest(k)
            for go, copy in self.along_copies(plane):
                pl.when(go)(copy.wait_send)

    def wait_passed(self):
        self.give_copy(self.plane).wait_send()
        for k in range(self.planes - 1):
            plane = self.nearest(k)
            for copy in self.exchange_copies(plane):
                copy.wait_send()
            for copy in self.pair_copies(plane):
                copy.wait_send()
            self.give_copy(plane).wait_send()

    def greet(self, planes=True):
        barrier = pltpu.get_barrier_semaphore()
        peers = [(self.across, self.wide), (self.beyond, self.wide), self.other_core()]
        if planes:
            peers += [
                self.device(lax.rem(self.plane + step, self.planes))
                for step in range(1, self.planes)
            ]
        for device in peers:
            pl.semaphore_signal(barrier, inc=1, device_id=device, device_id_type=MESH)
        return barrier, len(peers)

    def fetched(self, k, part, array=None):
        slot = (self.alpha, self.beta)[part](self.dp)
        return self.shard(self.nearest(k), self.core, slot, 1, array)

    @staticmethod
    def semaphores(planes):
        return 9 * planes


def gather_embed_kernel(
    planes,
    slots,
    groups,
    pos_table,
    prompts,
    gains,
    pos_index_t,
    tokens_in,
    own_qkv,
    own_out,
    own_up,
    own_down,
    hidden_out,
    qkv_out,
    full_qkv,
    full_out,
    full_up,
    part_down,
    table,
    tokens,
    pos_index,
    hidden,
    normed,
    qkv,
    first_full,
    second_full,
    third_full,
    send,
    recv,
    local,
):
    d = lax.axis_index("dp")
    w = lax.axis_index("wide")
    place = (d, w, planes, w // 2, lax.rem(w, 2))
    first = Gather(place, 0, first_full, (send, recv))
    second = Gather(place, 1, second_full, (send, recv))
    third = Gather(place, 2, third_full, (send, recv), by_rows=True)
    others = planes - 1
    qkv_columns = own_qkv.shape[1]
    barrier, greeted = first.greet()
    mine = pl.ds(pl.multiple_of(w * first.rows, first.rows), first.rows)
    loads = [
        pltpu.make_async_copy(own_qkv, first_full.at[mine, :qkv_columns], local.at[0]),
        pltpu.make_async_copy(own_out, first_full.at[mine, qkv_columns:], local.at[1]),
        pltpu.make_async_copy(own_up, second_full.at[mine], local.at[2]),
        pltpu.make_async_copy(own_down, third.shard(third.plane, third.core), local.at[3]),
        pltpu.make_async_copy(tokens_in, tokens, local.at[4]),
    ]
    for copy in loads:
        copy.start()
    fill_table(table, pos_table, prompts)
    columns = jnp.concatenate([pos_index_t[...].astype(F32)] * 4, 0).T
    pos_index[...] = columns.astype(jnp.int32)
    for copy in loads[:4]:
        copy.wait()
    pl.semaphore_wait(barrier, greeted)

    rows = tokens.shape[0]
    tiles = ORDER.count(("embed",))
    tile = rows // tiles
    outgoing = []

    def leave(source, target):
        copy = pltpu.make_async_copy(source, target, local.at[7 + len(outgoing)])
        copy.start()
        outgoing.append(copy)

    def embed_tile(index):
        part = slice(index * tile, (index + 1) * tile)
        value = embedded(groups, slots, index * tile, tokens[part], pos_index[part], table)
        hidden[part] = value
        leave(hidden.at[part], hidden_out.at[part])
        normal, _ = norm_parts(value)
        normed[part] = (normal * gains[0:1]).astype(BF)

    def qkv_tile(index):
        part = slice(index * tile, (index + 1) * tile)
        qkv[part] = dot(normed[part], first_full[:, :qkv_columns]).astype(BF)
        leave(qkv.at[part], qkv_out.at[part])

    gathers = (first, second, third)
    embeds, qkvs = iter(range(tiles)), iter(range(tiles))
    leave(second.shard(second.plane, second.core), second.shard(second.plane, second.core, array=full_up))
    for name, *where in ORDER:
        if name == "embed":
            index = next(embeds)
            if index == 0:
                loads[4].wait()
            embed_tile(index)
            continue
        if name == "qkv":
            qkv_tile(next(qkvs))
            continue
        gather, place = gathers[where[0]], where[1:]
        if name == "own":
            gather.along(gather.plane, place)
        elif name == "give":
            gather.give(gather.plane)
        elif name == "bring":
            gather.bring(*place)
        elif name == "fetch":
            gather.fetch(*place)
            leave(gather.fetched(*place), gather.fetched(*place, part_down))
        elif name == "pass_on":
            gather.pass_on(*place)
        elif name == "close":
            gather.close(*place)
            if gather is second:
                plane = second.nearest(*place)
                leave(second.shard(plane, second.core), second.shard(plane, second.core, array=full_up))
        elif gather is first:
            first.wait_all_given()
            leave(first_full.at[:, :qkv_columns], full_qkv)
            leave(first_full.at[:, qkv_columns:], full_out)
        else:
            for k in range(planes):
                plane = second.plane if k == 0 else second.nearest(k - 1)
                second.wait_given(plane)
                core = 1 - second.core
                leave(second.shard(plane, core), second.shard(plane, core, array=full_up))
    first.wait_fetched()
    second.wait_fetched()
    third.wait_fetched()
    first.wait_passed()
    second.wait_passed()
    for copy in outgoing:
        copy.wait()


def can_gather(axes, w_qkv, w_out, w_up, w_down):
    return (
        axes["dp"] == 4
        and axes["wide"] == 8
        and w_qkv.shape[0] % 16 == 0
        and w_down.shape[0] % (8 * 16) == 0
        and w_up.shape[1] % (8 * LANES) == 0
        and (w_qkv.shape[1] + w_out.shape[1]) % (8 * LANES) == 0
    )


def gather_embed(
    axes, size_group, tokens, pos_index, pos_table, prompts, gains, w_qkv, w_out, w_up, w_down
):
    rows, width = tokens.shape
    wide = axes["wide"]
    planes = wide // 2
    depth = w_qkv.shape[0] * wide
    inner_width = w_up.shape[1]
    vmem = pl.BlockSpec(memory_space=pltpu.VMEM)
    hbm = pl.BlockSpec(memory_space=pltpu.HBM)
    dma = pltpu.SemaphoreType.DMA
    count = Gather.semaphores(planes)
    first_columns = w_qkv.shape[1] + w_out.shape[1]
    return pl.pallas_call(
        functools.partial(gather_embed_kernel, planes, size_group.shape[0]),
        in_specs=[pl.BlockSpec(memory_space=pltpu.SMEM)] + [vmem] * 4 + [hbm] * 5,
        out_specs=[hbm] * 6,
        out_shape=[
            jax.ShapeDtypeStruct((rows, width), F32),
            jax.ShapeDtypeStruct((rows, w_qkv.shape[1]), BF),
            jax.ShapeDtypeStruct((depth, w_qkv.shape[1]), BF),
            jax.ShapeDtypeStruct((depth, w_out.shape[1]), BF),
            jax.ShapeDtypeStruct((depth, inner_width), BF),
            jax.ShapeDtypeStruct((inner_width, width), BF),
        ],
        scratch_shapes=[
            pltpu.VMEM((POS_ROWS + 3 * SLOT_ROWS, width), BF),
            pltpu.VMEM((rows, width), BF),
            pltpu.VMEM((rows, 8), jnp.int32),
            pltpu.VMEM((rows, width), F32),
            pltpu.VMEM((rows, width), BF),
            pltpu.VMEM((rows, w_qkv.shape[1]), BF),
            pltpu.VMEM((depth, first_columns), BF),
            pltpu.VMEM((depth, inner_width), BF),
            pltpu.VMEM((inner_width, width), BF),
            dma((3, count)),
            dma((3, count)),
            dma((7 + 2 * ORDER.count(("embed",)) + 2 + 2 * planes + 2 * (planes - 1),)),
        ],
        compiler_params=pltpu.CompilerParams(
            collective_id=0, has_side_effects=True, vmem_limit_bytes=VMEM_LIMIT
        ),
        name="gather_embed",
    )(
        size_group, pos_table, prompts, gains, pos_index.T, tokens, w_qkv, w_out, w_up, w_down
    )


def half(values, which):
    lane = lax.broadcasted_iota(jnp.int32, values.shape, 1)
    inside = (lane < HEAD_DIM) if which == 0 else (lane >= HEAD_DIM)
    return jnp.where(inside, values, jnp.zeros_like(values))


def each_image(groups, slots, image):
    def body(slot, start):
        group = groups[slot]
        length = image_length(group)
        pl.when(group == 2)(functools.partial(image, LARGE, start, length, slot))
        pl.when(group < 2)(functools.partial(image, SMALL, start, length, slot))
        return start + length

    lax.fori_loop(0, slots, body, jnp.int32(0))


def spread(pairs):
    for spaced, block in pairs:
        for pair in range(PAIRS):
            columns = slice(LANES * pair, LANES * (pair + 1))
            spaced[pair, : block.shape[0]] = block[:, columns].astype(F32)


def collect(block, spaced):
    for pair in range(PAIRS):
        columns = slice(LANES * pair, LANES * (pair + 1))
        block[:, columns] = spaced[pair, : block.shape[0]].astype(BF)


def take(spaced, rows):
    return [spaced[pair, rows, :] for pair in range(PAIRS)]


def low(parts):
    return [part.astype(BF) for part in parts]


def head_rows(parts, head):
    return parts[head // 2][HEAD_DIM * (head % 2) : HEAD_DIM * (head % 2 + 1)]


def clear_first(*refs):
    @pl.when(pl.program_id(0) == 0)
    def _():
        for ref in refs:
            ref[...] = jnp.zeros_like(ref)


def attend_kernel(slots, groups, q_ref, k_ref, v_ref, out_ref, total_ref, qs, ks, vs, outs):
    clear_first(qs, ks, vs, outs)
    spread(((qs, q_ref), (ks, k_ref), (vs, v_ref)))
    heads = range(GROUP_HEADS)

    def image(span, start, length, slot):
        rows = pl.ds(start, span)
        query = low(take(qs, rows))
        key = low(take(ks, rows))
        value_t = low([x.T for x in take(vs, rows)])
        last = span - LANES
        tail = lax.broadcasted_iota(jnp.int32, (LANES, 1), 0) + last < length
        for first, count in CHUNKS[span]:
            scores = [
                dot(key[h // 2], half(query[h // 2][first : first + count], h % 2), NT)
                for h in heads
            ]
            scores = [
                jnp.concatenate([s[:last], jnp.where(tail, s[last:], -1e30)], 0) for s in scores
            ]
            peaks = [jnp.max(s, axis=0, keepdims=True) for s in scores]
            powers = [jnp.exp2((s - m) * SCORE) for s, m in zip(scores, peaks)]
            totals = [jnp.sum(e, axis=0, keepdims=True) for e in powers]
            mixed = [dot(head_rows(value_t, h), powers[h].astype(BF)) for h in heads]
            mixed = [o / t for o, t in zip(mixed, totals)]
            for h in heads:
                total_ref[0, GROUP_HEADS * slot + h, :, first : first + count] = peaks[
                    h
                ] * SCORE + jnp.log2(totals[h])
            for pair in range(PAIRS):
                outs[pair, pl.ds(start + first, count), :] = jnp.concatenate(
                    mixed[2 * pair : 2 * pair + 2], 0
                ).T

    each_image(groups, slots, image)
    collect(out_ref, outs)


def attend(size_group, qkv):
    rows = qkv.shape[0]
    width = qkv.shape[1] // 3
    steps = width // HEAD_COLS
    slots = size_group.shape[0]
    block = lambda shift: pl.BlockSpec((rows, HEAD_COLS), lambda i, g: (0, shift * steps + i))
    spaced = pltpu.VMEM((PAIRS, rows + LANES, LANES), F32)
    return pl.pallas_call(
        functools.partial(attend_kernel, slots),
        grid_spec=pltpu.PrefetchScalarGridSpec(
            num_scalar_prefetch=1,
            grid=(steps,),
            in_specs=[block(0), block(1), block(2)],
            out_specs=[
                block(0),
                pl.BlockSpec((1, GROUP_HEADS * slots, 1, LARGE), lambda i, g: (i, 0, 0, 0)),
            ],
            scratch_shapes=[spaced] * 4,
        ),
        out_shape=[
            jax.ShapeDtypeStruct((rows, width), BF),
            jax.ShapeDtypeStruct((steps, GROUP_HEADS * slots, 1, LARGE), F32),
        ],
        compiler_params=pltpu.CompilerParams(vmem_limit_bytes=VMEM_LIMIT),
        name="attend",
    )(size_group, qkv, qkv, qkv)


def attend_back_kernel(
    slots,
    groups,
    q_ref,
    k_ref,
    v_ref,
    grad_ref,
    mixed_ref,
    total_ref,
    middle_left,
    middle_right,
    passed_in,
    dq_ref,
    dk_ref,
    dv_ref,
    dq_sum,
    dk_sum,
    dv_sum,
    middle_sum,
    passed_out,
    qs,
    ks,
    vs,
    grads,
    mixes,
    dqs,
    dks,
    dvs,
):
    clear_first(qs, ks, vs, grads, mixes, dqs, dks, dvs)
    passed_out[...] = passed_in[...]
    for ref in (dq_sum, dk_sum, dv_sum, middle_sum):
        ref[...] = jnp.zeros_like(ref)
    spread(((qs, q_ref), (ks, k_ref), (vs, v_ref), (grads, grad_ref), (mixes, mixed_ref)))
    heads = range(GROUP_HEADS)

    def image(span, start, length, slot):
        rows = pl.ds(start, span)
        query = low(take(qs, rows))
        key = low(take(ks, rows))
        key_t = low([x.T for x in take(ks, rows)])
        value = low(take(vs, rows))
        inside = lax.broadcasted_iota(jnp.int32, (span, 1), 0) < length
        grad32 = [jnp.where(inside, x, 0.0) for x in take(grads, rows)]
        products = [(x * y).T for x, y in zip(grad32, take(mixes, rows))]
        grad = low(grad32)
        last = span - LANES
        tail = inside[last:]
        dk = [jnp.zeros((span, LANES), F32)] * PAIRS
        dv = [jnp.zeros((span, LANES), F32)] * PAIRS
        for first, count in CHUNKS[span]:
            part = slice(first, first + count)
            query_h = [half(query[h // 2][part], h % 2) for h in heads]
            grad_h = [half(grad[h // 2][part], h % 2) for h in heads]
            scores = [dot(key[h // 2], query_h[h], NT) for h in heads]
            prob_grads = [dot(value[h // 2], grad_h[h], NT) for h in heads]
            probs = [
                jnp.exp2(scores[h] * SCORE - total_ref[0, GROUP_HEADS * slot + h, :, part])
                for h in heads
            ]
            probs = [
                jnp.concatenate([p[:last], jnp.where(tail, p[last:], 0.0)], 0) for p in probs
            ]
            deltas = [
                jnp.sum(head_rows(products, h)[:, part], axis=0, keepdims=True) for h in heads
            ]
            score_grads = [(probs[h] * (prob_grads[h] - deltas[h])).astype(BF) for h in heads]
            for h in heads:
                dv[h // 2] += dot(probs[h].astype(BF), grad_h[h])
                dk[h // 2] += dot(score_grads[h], query_h[h])
            dq = [dot(head_rows(key_t, h), score_grads[h]) for h in heads]
            for pair in range(PAIRS):
                dqs[pair, pl.ds(start + first, count), :] = (
                    jnp.concatenate(dq[2 * pair : 2 * pair + 2], 0).T * SCALE
                )
        for pair in range(PAIRS):
            dks[pair, rows, :] = dk[pair] * SCALE
            dvs[pair, rows, :] = dv[pair]
        prompt_rows = pl.ds(start + 1, SLOT_ROWS)
        for pair, middle_ref in enumerate((middle_left, middle_right)):
            columns = slice(LANES * pair, LANES * (pair + 1))
            for total, spaced in ((dq_sum, dqs), (dk_sum, dks), (dv_sum, dvs)):
                total[:, columns] += spaced[pair, prompt_rows, :].astype(BF).astype(F32)
            middle_sum[:, columns] += middle_ref[prompt_rows, :]

    each_image(groups, slots, image)
    collect(dq_ref, dqs)
    collect(dk_ref, dks)
    collect(dv_ref, dvs)


def attend_back(size_group, qkv, mixed_grad, mixed, totals, middle_grad, passed):
    rows = qkv.shape[0]
    width = qkv.shape[1] // 3
    steps = width // HEAD_COLS
    slots = size_group.shape[0]
    block = lambda shift: pl.BlockSpec((rows, HEAD_COLS), lambda i, g: (0, shift * steps + i))
    spaced = pltpu.VMEM((PAIRS, rows + LANES, LANES), F32)
    return pl.pallas_call(
        functools.partial(attend_back_kernel, slots),
        grid_spec=pltpu.PrefetchScalarGridSpec(
            num_scalar_prefetch=1,
            grid=(steps,),
            in_specs=[
                block(0),
                block(1),
                block(2),
                block(0),
                block(0),
                pl.BlockSpec((1, GROUP_HEADS * slots, 1, LARGE), lambda i, g: (i, 0, 0, 0)),
                pl.BlockSpec((rows, LANES), lambda i, g: (0, PAIRS * i)),
                pl.BlockSpec((rows, LANES), lambda i, g: (0, PAIRS * i + 1)),
                block(0),
            ],
            out_specs=[block(0)] * 3
            + [pl.BlockSpec((SLOT_ROWS, HEAD_COLS), lambda i, g: (0, i))] * 4
            + [block(0)],
            scratch_shapes=[spaced] * 8,
        ),
        out_shape=[jax.ShapeDtypeStruct((rows, width), BF)] * 3
        + [jax.ShapeDtypeStruct((SLOT_ROWS, width), F32)] * 4
        + [jax.ShapeDtypeStruct((rows, width), BF)],
        compiler_params=pltpu.CompilerParams(vmem_limit_bytes=VMEM_LIMIT),
        name="attend_back",
    )(
        size_group,
        qkv,
        qkv,
        qkv,
        mixed_grad,
        mixed,
        totals,
        middle_grad,
        middle_grad,
        passed,
    )


def feed_kernel(
    slots,
    chunk,
    groups,
    hidden,
    mixed,
    cotangent,
    gains,
    w_out,
    w_up,
    w_down,
    out_ref,
    middle_grad_ref,
    mixed_grad_ref,
):
    tile = hidden.shape[0]
    inner_width = w_up.shape[1]
    rows = pl.program_id(0) * tile + lax.broadcasted_iota(jnp.int32, (tile, 1), 0)
    live = rows < total_length(groups, slots)
    out_grad = jnp.where(live, cotangent[...].astype(F32), 0.0)
    out_grad_low = out_grad.astype(BF)
    middle = hidden[...] + dot(mixed[...], w_out[...])
    normal, rstd = norm_parts(middle)
    gain = gains[1:2]
    second = (normal * gain).astype(BF)
    forward = middle
    back = jnp.zeros_like(middle)
    for first in range(0, inner_width, chunk):
        part = slice(first, first + chunk)
        inner = dot(second, w_up[:, part])
        act_grad = dot(out_grad_low, w_down[part], NT)
        phi = 0.5 + 0.5 * lax.erf(inner * (0.5**0.5))
        density = jnp.exp2(inner * inner * (-0.5 * LOG2E)) * 0.3989422804014327
        activated = (inner * phi).astype(BF)
        inner_grad = (act_grad * (phi + inner * density)).astype(BF)
        forward = forward + dot(activated, w_down[part])
        back = back + dot(inner_grad, w_up[:, part], NT)
    out_ref[...] = jnp.where(live, forward, 0.0).astype(BF)
    middle_grad = out_grad + norm_back(normal, rstd, gain, back)
    middle_grad_ref[...] = middle_grad
    mixed_grad_ref[...] = dot(middle_grad.astype(BF), w_out[...], NT).astype(BF)


def feed(size_group, hidden, mixed, cotangent, gains, w_out, w_up, w_down):
    rows, width = hidden.shape
    tile = 384
    chunk = 512
    keep = lambda i, g: (0, 0)
    whole = lambda a: pl.BlockSpec(a.shape, keep, pipeline_mode=pl.Buffered(1))
    by_row = pl.BlockSpec((tile, width), lambda i, g: (i, 0))
    return pl.pallas_call(
        functools.partial(feed_kernel, size_group.shape[0], chunk),
        grid_spec=pltpu.PrefetchScalarGridSpec(
            num_scalar_prefetch=1,
            grid=(rows // tile,),
            in_specs=[by_row, by_row, by_row, whole(gains), whole(w_out), whole(w_up), whole(w_down)],
            out_specs=[by_row, by_row, by_row],
        ),
        out_shape=[
            jax.ShapeDtypeStruct((rows, width), BF),
            jax.ShapeDtypeStruct((rows, width), F32),
            jax.ShapeDtypeStruct((rows, width), BF),
        ],
        compiler_params=pltpu.CompilerParams(vmem_limit_bytes=VMEM_LIMIT),
        name="feed",
    )(size_group, hidden, mixed, cotangent, gains, w_out, w_up, w_down)


def gather_feed_kernel(
    planes,
    slots,
    chunk,
    groups,
    gains,
    hidden_in,
    mixed_in,
    cotangent_in,
    full_out,
    full_up,
    own_down,
    part_down,
    out_ref,
    middle_grad_ref,
    mixed_grad_ref,
    middle,
    mixed,
    cotangent,
    w_out,
    w_up,
    w_down,
    active,
    slope,
    send,
    recv,
    weights_in,
    rows_in,
    rows_out,
):
    d = lax.axis_index("dp")
    w = lax.axis_index("wide")
    down = Gather((d, w, planes, w // 2, lax.rem(w, 2)), 0, w_down, (send, recv), by_rows=True)
    barrier, greeted = down.greet(planes=False)
    others = planes - 1
    tiles = rows_in.shape[0]
    tile = middle.shape[0] // tiles
    inner_width = w_up.shape[1]

    def tile_rows(index):
        return pl.ds(pl.multiple_of(index * tile, tile), tile)

    def loads(index):
        part = tile_rows(index)
        return [
            pltpu.make_async_copy(hidden_in.at[part], middle.at[part], rows_in.at[index, 0]),
            pltpu.make_async_copy(mixed_in.at[part], mixed.at[part], rows_in.at[index, 1]),
            pltpu.make_async_copy(cotangent_in.at[part], cotangent.at[part], rows_in.at[index, 2]),
        ]

    def stores(index):
        part = tile_rows(index)
        return [
            pltpu.make_async_copy(middle.at[part], middle_grad_ref.at[part], rows_out.at[index, 0]),
            pltpu.make_async_copy(mixed.at[part], mixed_grad_ref.at[part], rows_out.at[index, 1]),
            pltpu.make_async_copy(cotangent.at[part], out_ref.at[part], rows_out.at[index, 2]),
        ]

    down_loads = [(own_down, down.shard(down.plane, down.core))]
    for k in range(others):
        for part in (0, 1):
            down_loads.append((down.fetched(k, part, part_down), down.fetched(k, part)))
    down_loads = [
        pltpu.make_async_copy(source, target, weights_in.at[2 + index])
        for index, (source, target) in enumerate(down_loads)
    ]
    out_load = pltpu.make_async_copy(full_out, w_out, weights_in.at[0])
    up_load = pltpu.make_async_copy(full_up, w_up, weights_in.at[1])
    for copy in down_loads:
        copy.start()
    out_load.start()
    for copy in loads(0):
        copy.start()
    up_load.start()
    for index in range(1, tiles):
        for copy in loads(index):
            copy.start()
    for copy in down_loads:
        copy.wait()
    pl.semaphore_wait(barrier, greeted)
    for k in range(others):
        down.exchange(down.nearest(k))
    down.give(down.plane)
    out_load.wait()
    up_load.wait()
    gain = gains[1:2]

    def pump(step):
        @pl.when((step >= 0) & (step < others))
        def _():
            down.pass_on(step, 0)
            down.pass_on(step, 1)

        @pl.when((step >= 2) & (step < others + 2))
        def _():
            down.close(step - 2)

    def up_tile(index, carry):
        for copy in loads(index):
            copy.wait()
        part = tile_rows(index)
        value = middle[part, :] + dot(mixed[part, :], w_out[...])
        middle[part, :] = value
        normal, _ = norm_parts(value)
        second = (normal * gain).astype(BF)
        for first in range(0, inner_width, chunk):
            columns = slice(first, first + chunk)
            inner = dot(second, w_up[:, columns])
            phi = 0.5 + 0.5 * lax.erf(inner * (0.5**0.5))
            density = jnp.exp2(inner * inner * (-0.5 * LOG2E)) * 0.3989422804014327
            active[part, columns] = (inner * phi).astype(BF)
            slope[part, columns] = phi + inner * density
            if first + chunk == inner_width // 2:
                pump(2 * index)
        pump(2 * index + 1)
        return carry

    lax.fori_loop(0, tiles, up_tile, 0)
    for step in range(2 * tiles, others + 2):
        pump(step)
    down.wait_all_given()
    total = total_length(groups, slots)

    def down_tile(index, carry):
        part = tile_rows(index)
        rows = index * tile + lax.broadcasted_iota(jnp.int32, (tile, 1), 0)
        live = rows < total
        out_grad = jnp.where(live, cotangent[part, :].astype(F32), 0.0)
        out_grad_low = out_grad.astype(BF)
        value = middle[part, :]
        back = jnp.zeros_like(value)
        for first in range(0, inner_width, chunk):
            columns = slice(first, first + chunk)
            act_grad = dot(out_grad_low, w_down[columns], NT)
            inner_grad = (act_grad * slope[part, columns]).astype(BF)
            back = back + dot(inner_grad, w_up[:, columns], NT)
        forward = value + dot(active[part, :], w_down[...])
        cotangent[part, :] = jnp.where(live, forward, 0.0).astype(BF)
        normal, rstd = norm_parts(value)
        middle_grad = out_grad + norm_back(normal, rstd, gain, back)
        middle[part, :] = middle_grad
        mixed[part, :] = dot(middle_grad.astype(BF), w_out[...], NT).astype(BF)
        for copy in stores(index):
            copy.start()
        return carry

    lax.fori_loop(0, tiles, down_tile, 0)
    down.wait_passed()
    for index in range(tiles):
        for copy in stores(index):
            copy.wait()


def gather_feed(axes, size_group, hidden, mixed, cotangent, gains, w_out, w_up, w_down, part_down):
    rows, width = hidden.shape
    planes = axes["wide"] // 2
    inner_width = w_up.shape[1]
    tiles = 3
    hbm = pl.BlockSpec(memory_space=pltpu.HBM)
    dma = pltpu.SemaphoreType.DMA
    count = Gather.semaphores(planes)
    return pl.pallas_call(
        functools.partial(gather_feed_kernel, planes, size_group.shape[0], 512),
        in_specs=[
            pl.BlockSpec(memory_space=pltpu.SMEM),
            pl.BlockSpec(memory_space=pltpu.VMEM),
        ]
        + [hbm] * 7,
        out_specs=[hbm] * 3,
        out_shape=[
            jax.ShapeDtypeStruct((rows, width), BF),
            jax.ShapeDtypeStruct((rows, width), F32),
            jax.ShapeDtypeStruct((rows, width), BF),
        ],
        scratch_shapes=[
            pltpu.VMEM((rows, width), F32),
            pltpu.VMEM((rows, width), BF),
            pltpu.VMEM((rows, width), BF),
            pltpu.VMEM(w_out.shape, BF),
            pltpu.VMEM(w_up.shape, BF),
            pltpu.VMEM((inner_width, width), BF),
            pltpu.VMEM((rows, inner_width), BF),
            pltpu.VMEM((rows, inner_width), F32),
            dma((1, count)),
            dma((1, count)),
            dma((3 + 2 * (planes - 1),)),
            dma((tiles, 3)),
            dma((tiles, 3)),
        ],
        compiler_params=pltpu.CompilerParams(
            collective_id=2, has_side_effects=True, vmem_limit_bytes=VMEM_LIMIT
        ),
        name="gather_feed",
    )(size_group, gains, hidden, mixed, cotangent, w_out, w_up, w_down, part_down)


class Shared:
    def __init__(self, dp, wide, mine, near, far, result, sems):
        self.members = 2 * dp
        self.planes = wide // 2
        self.rows = mine.shape[0] // self.members
        self.d = lax.axis_index("dp")
        w = lax.axis_index("wide")
        self.plane = w // 2
        self.core = lax.rem(w, 2)
        self.member = self.d * 2 + self.core
        self.mine, self.near, self.far, self.result = mine, near, far, result
        self.send, self.near_in, self.far_in, self.last_in = sems

    def peer(self, step):
        other = lax.rem(self.member + step, self.members)
        return other, (other // 2, self.plane * 2 + lax.rem(other, 2))

    def plane_peer(self, step):
        other = lax.rem(self.plane + step, self.planes)
        return other, (self.d, other * 2 + self.core)

    def greet(self):
        barrier = pltpu.get_barrier_semaphore()
        for step in range(1, self.members):
            pl.semaphore_signal(barrier, inc=1, device_id=self.peer(step)[1], device_id_type=MESH)
        for step in range(1, self.planes):
            pl.semaphore_signal(
                barrier, inc=1, device_id=self.plane_peer(step)[1], device_id_type=MESH
            )
        return barrier, self.members + self.planes - 2

    def part(self, ref, index):
        return ref.at[pl.ds(pl.multiple_of(index * self.rows, self.rows), self.rows)]

    def copy(self, source, target, send, recv, device):
        return pltpu.make_async_remote_copy(
            source, target, send, recv, device_id=device, device_id_type=MESH
        )

    def first(self, step):
        other, device = self.peer(step)
        return self.copy(
            self.part(self.mine, other),
            self.near.at[step],
            self.send.at[0, step],
            self.near_in.at[step],
            device,
        )

    def second(self, step):
        mine = self.far.at[self.plane]
        device = self.plane_peer(step)[1]
        return self.copy(mine, mine, self.send.at[1, step], self.far_in.at[step], device)

    def third(self, step):
        mine = self.part(self.result, self.member)
        device = self.peer(step)[1]
        return self.copy(mine, mine, self.send.at[2, step], self.last_in.at[step], device)

    def start_first(self):
        for step in range(1, self.members):
            self.first(step).start()
        self.near[0] = self.part(self.mine, self.member)[...]

    def start_second(self):
        for step in range(1, self.members):
            self.first(step).wait_recv()
        total = jnp.zeros(self.near.shape[1:], F32)
        for index in range(self.members):
            total = total + self.near[lax.rem(self.member - index + self.members, self.members)]
        self.far[self.plane] = total
        for step in range(1, self.planes):
            self.second(step).start()

    def start_third(self):
        for step in range(1, self.planes):
            self.second(step).wait_recv()
        total = jnp.zeros(self.near.shape[1:], F32)
        for index in range(self.planes):
            total = total + self.far[index]
        self.part(self.result, self.member)[...] = total
        for step in range(1, self.members):
            self.third(step).start()

    def end(self):
        for step in range(1, self.members):
            self.third(step).wait_recv()
        for step in range(1, self.members):
            self.first(step).wait_send()
            self.third(step).wait_send()
        for step in range(1, self.planes):
            self.second(step).wait_send()


def finish_kernel(
    dp,
    wide,
    slots,
    groups,
    prompts,
    gains,
    dq_sum,
    dk_sum,
    dv_sum,
    middle_sum,
    hidden_in,
    middle_grad_in,
    dq_in,
    dk_in,
    dv_in,
    w_qkv_in,
    input_grad_out,
    prompt_grad,
    penalty,
    hidden,
    middle_grad,
    dq,
    dk,
    dv,
    w_qkv,
    input_grad,
    known,
    mine,
    near,
    far,
    result,
    send,
    near_in,
    far_in,
    last_in,
    weight_in,
    rows_in,
    rows_out,
):
    shared = Shared(dp, wide, mine, near, far, result, (send, near_in, far_in, last_in))
    barrier, greeted = shared.greet()
    tiles = rows_in.shape[0]
    width = hidden.shape[1]
    tile = hidden.shape[0] // tiles
    weight_load = pltpu.make_async_copy(w_qkv_in, w_qkv, weight_in)
    weight_load.start()

    def loads(index):
        part = pl.ds(index * tile, tile)
        pairs = (
            (dq_in, dq),
            (dk_in, dk),
            (dv_in, dv),
            (hidden_in, hidden),
            (middle_grad_in, middle_grad),
        )
        return [
            pltpu.make_async_copy(source.at[part], target.at[part], rows_in.at[index, number])
            for number, (source, target) in enumerate(pairs)
        ]

    for index in range(tiles):
        for copy in loads(index):
            copy.start()

    def back(q, k, v):
        return (
            dot(q, w_qkv[:, :width], NT)
            + dot(k, w_qkv[:, width : 2 * width], NT)
            + dot(v, w_qkv[:, 2 * width :], NT)
        )

    known[...] = jnp.zeros_like(known)
    known[: prompts.shape[0]] = prompts[...]
    pieces = []
    for ref in (dq_sum, dk_sum, dv_sum):
        rest = ref[...]
        terms = []
        for _ in range(3):
            terms.append(rest.astype(BF))
            rest = rest - terms[-1].astype(F32)
        pieces.append(jnp.concatenate(terms, 0))
    weight_load.wait()
    terms = back(*pieces)
    normed_grad = terms[:SLOT_ROWS] + terms[SLOT_ROWS : 2 * SLOT_ROWS] + terms[2 * SLOT_ROWS :]
    normal, rstd = norm_parts(known[...])
    local = middle_sum[...] + norm_back(normal, rstd, gains[0:1], normed_grad)
    slot_row = lax.broadcasted_iota(jnp.int32, (SLOT_ROWS, 1), 0)
    count = total_length(groups, slots).astype(F32)
    mine[...] = jnp.where(slot_row < PROMPTS, local, jnp.where(slot_row == PROMPTS, count, 0.0))
    pl.semaphore_wait(barrier, greeted)
    shared.start_first()

    def store(index):
        part = pl.ds(index * tile, tile)
        return pltpu.make_async_copy(
            input_grad.at[part], input_grad_out.at[part], rows_out.at[index]
        )

    for index in range(tiles):
        for copy in loads(index):
            copy.wait()
        part = slice(index * tile, (index + 1) * tile)
        normal, rstd = norm_parts(hidden[part])
        normed_grad = back(dq[part], dk[part], dv[part])
        hidden_grad = middle_grad[part] + norm_back(normal, rstd, gains[0:1], normed_grad)
        prompt_slot, live = row_places(groups, slots, index * tile, tile)
        input_grad[part] = jnp.where(live & (prompt_slot < 0), hidden_grad, 0.0).astype(BF)
        store(index).start()
        if index == 0:
            shared.start_second()
        if index == 1:
            shared.start_third()
    shared.end()
    given = prompts[...]
    size = given.shape[0] * given.shape[1]
    count = result[PROMPTS : PROMPTS + 1]
    prompt_grad[...] = result[:PROMPTS] + (2.0 * PENALTY_RATE / size) * count * given
    square = jnp.sum(jnp.sum(given * given, axis=1, keepdims=True), axis=0, keepdims=True)
    penalty[...] = PENALTY_RATE * count[:, :1] * (square / size)
    for index in range(tiles):
        store(index).wait()


def finish(axes, size_group, prompts, gains, sums, hidden, middle_grad, dq, dk, dv, w_qkv):
    rows, width = hidden.shape
    dp, wide = axes["dp"], axes["wide"]
    members, planes = 2 * dp, wide // 2
    tiles = 3
    dma = pltpu.SemaphoreType.DMA
    vmem = pl.BlockSpec(memory_space=pltpu.VMEM)
    hbm = pl.BlockSpec(memory_space=pltpu.HBM)
    input_grad, prompt_grad, penalty = pl.pallas_call(
        functools.partial(finish_kernel, dp, wide, size_group.shape[0]),
        in_specs=[pl.BlockSpec(memory_space=pltpu.SMEM)] + [vmem] * 6 + [hbm] * 6,
        out_specs=[hbm, vmem, vmem],
        out_shape=[
            jax.ShapeDtypeStruct((rows, width), BF),
            jax.ShapeDtypeStruct(prompts.shape, F32),
            jax.ShapeDtypeStruct((1, 1), F32),
        ],
        scratch_shapes=[
            pltpu.VMEM((rows, width), F32),
            pltpu.VMEM((rows, width), F32),
            pltpu.VMEM((rows, width), BF),
            pltpu.VMEM((rows, width), BF),
            pltpu.VMEM((rows, width), BF),
            pltpu.VMEM(w_qkv.shape, BF),
            pltpu.VMEM((rows, width), BF),
            pltpu.VMEM((SLOT_ROWS, width), F32),
            pltpu.VMEM((SLOT_ROWS, width), F32),
            pltpu.VMEM((members, SLOT_ROWS // members, width), F32),
            pltpu.VMEM((planes, SLOT_ROWS // members, width), F32),
            pltpu.VMEM((SLOT_ROWS, width), F32),
            dma((3, max(members, planes))),
            dma((members,)),
            dma((planes,)),
            dma((members,)),
            dma,
            dma((tiles, 5)),
            dma((tiles,)),
        ],
        compiler_params=pltpu.CompilerParams(
            collective_id=1, has_side_effects=True, vmem_limit_bytes=VMEM_LIMIT
        ),
        name="finish",
    )(size_group, prompts, gains, *sums, hidden, middle_grad, dq, dk, dv, w_qkv)
    return input_grad, prompt_grad, penalty[0, 0]


def shards(
    axes,
    tokens,
    pos_index,
    size_group,
    pos_table,
    prompts,
    norm_gains,
    w_qkv,
    w_out,
    w_up,
    w_down,
    cotangent,
):
    if can_gather(axes, w_qkv, w_out, w_up, w_down):
        hidden, qkv, full_qkv, full_out, full_up, part_down = gather_embed(
            axes,
            size_group,
            tokens,
            pos_index,
            pos_table,
            prompts,
            norm_gains,
            w_qkv,
            w_out,
            w_up,
            w_down,
        )
        mixed, totals = attend(size_group, qkv)
        outputs, middle_grad, mixed_grad = gather_feed(
            axes,
            size_group,
            hidden,
            mixed,
            cotangent,
            norm_gains,
            full_out,
            full_up,
            w_down,
            part_down,
        )
    else:
        full_qkv = lax.all_gather(w_qkv, "wide", axis=0, tiled=True)
        full_out = lax.all_gather(w_out, "wide", axis=0, tiled=True)
        full_up = lax.all_gather(w_up, "wide", axis=0, tiled=True)
        full_down = lax.all_gather(w_down, "wide", axis=0, tiled=True)
        hidden, qkv = embed(size_group, tokens, pos_index, pos_table, prompts, norm_gains, full_qkv)
        mixed, totals = attend(size_group, qkv)
        outputs, middle_grad, mixed_grad = feed(
            size_group, hidden, mixed, cotangent, norm_gains, full_out, full_up, full_down
        )
    dq, dk, dv, *sums, outputs = attend_back(
        size_group, qkv, mixed_grad, mixed, totals, middle_grad, outputs
    )
    input_grad, prompt_grad, penalty = finish(
        axes, size_group, prompts, norm_gains, sums, hidden, middle_grad, dq, dk, dv, full_qkv
    )
    return (outputs, input_grad, prompt_grad, penalty)


def solution(mesh):
    return jax.shard_map(
        functools.partial(shards, dict(mesh.shape)),
        mesh=mesh,
        in_specs=(
            P(("dp", "wide"), None),
            P(("dp", "wide"), None),
            P(("dp", "wide")),
            P(),
            P(),
            P(),
            P("wide", None),
            P("wide", None),
            P("wide", None),
            P("wide", None),
            P(("dp", "wide"), None),
        ),
        out_specs=(P(("dp", "wide"), None), P(("dp", "wide"), None), P(), P()),
        check_vma=False,
    )
```

```python
import functools

import jax
import jax.numpy as jnp
from jax import lax
from jax.experimental import pallas as pl
from jax.experimental.pallas import tpu as pltpu
from jax.sharding import PartitionSpec as P

HEADS = 12
HEAD_DIM = 64
PROMPTS = 50
PATCH_S = 100
PATCH_M = 196
PATCH_L = 576

EPSILON = 1e-06
PENALTY_RATE = 3e-05
SCALE = HEAD_DIM**-0.5
LOG2E = 1.4426950408889634
SCORE = SCALE * LOG2E

BF = jnp.bfloat16
F32 = jnp.float32
NN = (((1,), (0,)), ((), ()))
NT = (((1,), (1,)), ((), ()))
MESH = pl.DeviceIdType.MESH

LANES = 128
HEAD_COLS = 384
PAIRS = HEAD_COLS // LANES
GROUP_HEADS = HEAD_COLS // HEAD_DIM
LARGE = 640
KEY_ROWS = (160, 256, LARGE)
QUERY_CHUNKS = (((0, 256),), ((0, 256),), ((0, 256), (256, 256), (512, 128)))
MASKED = -1e30
POS_ROWS = 256
VMEM_LIMIT = 60 << 20
SLOT_ROWS = 64


def dot(a, b, dims=NN):
    return lax.dot_general(a, b, dims, preferred_element_type=F32)


def image_length(group):
    patches = jnp.where(group == 0, PATCH_S, jnp.where(group == 1, PATCH_M, PATCH_L))
    return jnp.where(group == 3, 0, 1 + PROMPTS + patches).astype(jnp.int32)


def total_length(groups, slots):
    total = jnp.int32(0)
    for slot in range(slots):
        total = total + image_length(groups[slot])
    return total


def row_places(groups, slots, first_row, count):
    rows = first_row + lax.broadcasted_iota(jnp.int32, (count, 1), 0)
    place = rows
    start = jnp.int32(0)
    for slot in range(slots):
        length = image_length(groups[slot])
        place = jnp.where((rows >= start) & (length > 0), rows - start, place)
        start = start + length
    live = rows < start
    prompt_slot = jnp.where(live & (place >= 1) & (place <= PROMPTS), place - 1, -1)
    return prompt_slot, live


def norm_parts(values):
    centered = values - jnp.mean(values, axis=-1, keepdims=True)
    rstd = lax.rsqrt(jnp.mean(centered * centered, axis=-1, keepdims=True) + EPSILON)
    return centered * rstd, rstd


def norm_back(normal, rstd, gain, grad):
    scaled = grad * gain
    return (
        scaled
        - jnp.mean(scaled, axis=-1, keepdims=True)
        - normal * jnp.mean(scaled * normal, axis=-1, keepdims=True)
    ) * rstd


def fill_table(table, pos_table, prompts):
    table[...] = jnp.zeros_like(table)
    table[: pos_table.shape[0]] = pos_table[...]
    rest = prompts[...]
    for piece in range(3):
        part = rest.astype(BF)
        first = POS_ROWS + piece * SLOT_ROWS
        table[first : first + PROMPTS] = part
        rest = rest - part.astype(F32)


def embedded(groups, slots, first_row, tokens, pos_index, table):
    prompt_slot, _ = row_places(groups, slots, first_row, tokens.shape[0])
    is_prompt = prompt_slot >= 0
    lane = lax.broadcasted_iota(jnp.int32, (1, POS_ROWS), 1)
    left = jnp.where(is_prompt, -1, pos_index[:, 0:1])
    right = jnp.where(is_prompt, -1, pos_index[:, 1:2])
    half_hot = jnp.where(lane == left, 0.5, 0.0) + jnp.where(lane == right, 0.5, 0.0)
    slot_lane = lax.broadcasted_iota(jnp.int32, (1, 3 * SLOT_ROWS), 1)
    slot_lane = lax.rem(slot_lane, SLOT_ROWS)
    slot_hot = jnp.where(slot_lane == prompt_slot, 1.0, 0.0)
    picked = dot(half_hot.astype(BF), table[:POS_ROWS]) + dot(
        slot_hot.astype(BF), table[POS_ROWS:]
    )
    return jnp.where(is_prompt, 0.0, tokens.astype(F32)) + picked


def embed_kernel(
    slots, groups, tokens, pos_index, pos_table, prompts, gains, w_qkv, hidden_out, qkv_out, table
):
    tile = tokens.shape[0]
    step = pl.program_id(0)

    @pl.when(step == 0)
    def _():
        fill_table(table, pos_table, prompts)

    hidden = embedded(groups, slots, step * tile, tokens[...], pos_index[...], table)
    hidden_out[...] = hidden
    normal, _ = norm_parts(hidden)
    normed = (normal * gains[0:1]).astype(BF)
    qkv_out[...] = dot(normed, w_qkv[...]).astype(BF)


def embed(size_group, tokens, pos_index, pos_table, prompts, gains, w_qkv):
    rows, width = tokens.shape
    tile = 384
    keep = lambda i, g: (0, 0)
    whole = lambda a: pl.BlockSpec(a.shape, keep, pipeline_mode=pl.Buffered(1))
    by_row = lambda columns: pl.BlockSpec((tile, columns), lambda i, g: (i, 0))
    return pl.pallas_call(
        functools.partial(embed_kernel, size_group.shape[0]),
        grid_spec=pltpu.PrefetchScalarGridSpec(
            num_scalar_prefetch=1,
            grid=(rows // tile,),
            in_specs=[
                by_row(width),
                by_row(2),
                whole(pos_table),
                whole(prompts),
                whole(gains),
                whole(w_qkv),
            ],
            out_specs=[by_row(width), by_row(3 * width)],
            scratch_shapes=[pltpu.VMEM((POS_ROWS + 3 * SLOT_ROWS, width), BF)],
        ),
        out_shape=[
            jax.ShapeDtypeStruct((rows, width), F32),
            jax.ShapeDtypeStruct((rows, 3 * width), BF),
        ],
        compiler_params=pltpu.CompilerParams(vmem_limit_bytes=VMEM_LIMIT),
        name="embed",
    )(size_group, tokens, pos_index, pos_table, prompts, gains, w_qkv)


ORDER = (
    ("own", 0, 0), ("own", 0, 1), ("own", 1, 0), ("bring", 0, 0, 0), ("bring", 0, 0, 1),
    ("own", 1, 1), ("embed",), ("pass_on", 0, 0, 0), ("bring", 1, 0, 0), ("bring", 0, 1, 0),
    ("embed",), ("pass_on", 0, 0, 1), ("bring", 0, 1, 1), ("bring", 1, 0, 1),
    ("bring", 0, 2, 0), ("give", 0), ("bring", 0, 2, 1), ("give", 1), ("pass_on", 0, 1, 1),
    ("embed",), ("pass_on", 0, 1, 0), ("bring", 1, 2, 1), ("close", 0, 0), ("bring", 1, 2, 0),
    ("embed",), ("own", 2, 1), ("pass_on", 0, 2, 0), ("pass_on", 0, 2, 1), ("bring", 1, 1, 0),
    ("pass_on", 1, 2, 1), ("own", 2, 0), ("embed",), ("pass_on", 1, 2, 0), ("close", 0, 1),
    ("fetch", 2, 0, 1), ("bring", 1, 1, 1), ("embed",), ("pass_on", 1, 0, 0), ("close", 0, 2),
    ("fetch", 2, 1, 0), ("pass_on", 1, 0, 1), ("fetch", 2, 0, 0), ("all", 0),
    ("pass_on", 1, 1, 0), ("fetch", 2, 1, 1), ("qkv",), ("qkv",), ("pass_on", 1, 1, 1),
    ("qkv",), ("close", 1, 2), ("fetch", 2, 2, 1), ("close", 1, 0), ("qkv",), ("qkv",),
    ("qkv",), ("close", 1, 1), ("fetch", 2, 2, 0), ("all", 1),
)


class Gather:
    def __init__(self, place, index, full, sems, by_rows=False):
        self.dp, self.wide, self.planes, self.plane, self.core = place
        self.index = index
        self.full = full
        self.send, self.recv = sems
        self.rows = full.shape[0] // (2 * self.planes)
        self.columns = full.shape[1] // 8
        self.by_rows = by_rows
        d = self.dp
        self.across = d + 1 - 2 * lax.rem(d, 2)
        self.beyond = lax.rem(d + 2, 4)

    def alpha(self, d):
        return d

    def beta(self, d):
        return 4 + 2 * lax.rem(d, 2) + d // 2

    def pair(self, slot):
        return slot - lax.rem(slot, 2)

    def shard(self, plane, core, slot=None, count=1, array=None):
        full = self.full if array is None else array
        first = pl.multiple_of((2 * plane + core) * self.rows, self.rows)
        if slot is None:
            return full.at[pl.ds(first, self.rows)]
        if self.by_rows:
            step = self.rows // 8
            return full.at[pl.ds(pl.multiple_of(first + slot * step, step), count * step)]
        column = pl.multiple_of(slot * self.columns, self.columns)
        return full.at[pl.ds(first, self.rows), pl.ds(column, count * self.columns)]

    def copy(self, ref, send, recv, device):
        return pltpu.make_async_remote_copy(
            ref,
            ref,
            self.send.at[self.index, send],
            self.recv.at[self.index, recv],
            device_id=device,
            device_id_type=MESH,
        )

    def device(self, plane):
        return (self.dp, 2 * plane + self.core)

    def nearest(self, k):
        n = self.planes
        low = 1 - self.plane // (n // 2)
        edge = low * self.plane + (1 - low) * (n - 1 - self.plane)
        other = k + 1 - (edge - k + n - 1) // n
        return low * other + (1 - low) * (n - 1 - other)

    def along_copies(self, plane, parts=(0, 1)):
        n = self.planes
        up = (plane <= self.plane) & (self.plane < n - 1)
        down = (plane >= self.plane) & (self.plane > 0)
        for part in parts:
            slot = (self.alpha(self.dp), self.beta(self.dp))[part]
            ref = self.shard(plane, self.core, slot)
            sem = 2 * plane + part
            for go, sent, target in (
                (up, sem, lax.rem(self.plane + 1, n)),
                (down, 2 * n + sem, lax.rem(self.plane + n - 1, n)),
            ):
                yield go, self.copy(ref, sent, sem, self.device(target))

    def along(self, plane, parts=(0, 1)):
        for go, copy in self.along_copies(plane, parts):
            pl.when(go)(copy.start)

    def wait_along(self, plane, parts=(0, 1)):
        for part in parts:
            slot = (self.alpha(self.dp), self.beta(self.dp))[part]
            ref = self.shard(plane, self.core, slot)
            sem = 2 * plane + part
            self.copy(ref, sem, sem, self.device(plane)).wait_recv()

    def exchange_copies(self, plane):
        for part, (slot, d) in enumerate(
            ((self.alpha(self.dp), self.across), (self.beta(self.dp), self.beyond))
        ):
            sem = 4 * self.planes + 2 * plane + part
            yield self.copy(self.shard(plane, self.core, slot), sem, sem, (d, self.wide))

    def exchange(self, plane):
        for copy in self.exchange_copies(plane):
            copy.start()

    def wait_one_exchange(self, plane, part):
        d = (self.across, self.beyond)[part]
        slot = (self.alpha, self.beta)[part](d)
        sem = 4 * self.planes + 2 * plane + part
        self.copy(self.shard(plane, self.core, slot), sem, sem, (d, self.wide)).wait_recv()

    def pair_copies(self, plane):
        for part, (slot, d) in enumerate(
            ((self.alpha(self.dp), self.beyond), (self.beta(self.dp), self.across))
        ):
            sem = 6 * self.planes + 2 * plane + part
            ref = self.shard(plane, self.core, self.pair(slot), 2)
            yield self.copy(ref, sem, sem, (d, self.wide))

    def wait_pairs(self, plane):
        for part, (slot, d) in enumerate(
            ((self.alpha(self.beyond), self.beyond), (self.beta(self.across), self.across))
        ):
            sem = 6 * self.planes + 2 * plane + part
            ref = self.shard(plane, self.core, self.pair(slot), 2)
            self.copy(ref, sem, sem, (d, self.wide)).wait_recv()

    def other_core(self):
        return (self.dp, 2 * self.plane + 1 - self.core)

    def give_copy(self, plane):
        sem = 8 * self.planes + plane
        return self.copy(self.shard(plane, self.core), sem, sem, self.other_core())

    def give(self, plane):
        self.give_copy(plane).start()

    def wait_given(self, plane):
        sem = 8 * self.planes + plane
        self.copy(self.shard(plane, 1 - self.core), sem, sem, self.other_core()).wait_recv()

    def wait_all_given(self):
        for plane in range(self.planes):
            self.wait_given(plane)

    def fetch(self, k, part):
        plane = self.nearest(k)
        self.wait_along(plane, (part,))
        self.along(plane, (part,))

    def bring(self, k, part):
        self.fetch(k, part)
        list(self.exchange_copies(self.nearest(k)))[part].start()

    def pass_on(self, k, part):
        plane = self.nearest(k)
        self.wait_one_exchange(plane, part)
        list(self.pair_copies(plane))[part].start()

    def close(self, k):
        plane = self.nearest(k)
        self.wait_pairs(plane)
        self.give(plane)

    def wait_fetched(self):
        for k in range(self.planes):
            plane = self.plane if k == self.planes - 1 else self.nearest(k)
            for go, copy in self.along_copies(plane):
                pl.when(go)(copy.wait_send)

    def wait_passed(self):
        self.give_copy(self.plane).wait_send()
        for k in range(self.planes - 1):
            plane = self.nearest(k)
            for copy in self.exchange_copies(plane):
                copy.wait_send()
            for copy in self.pair_copies(plane):
                copy.wait_send()
            self.give_copy(plane).wait_send()

    def greet(self, planes=True):
        barrier = pltpu.get_barrier_semaphore()
        peers = [(self.across, self.wide), (self.beyond, self.wide), self.other_core()]
        if planes:
            peers += [
                self.device(lax.rem(self.plane + step, self.planes))
                for step in range(1, self.planes)
            ]
        for device in peers:
            pl.semaphore_signal(barrier, inc=1, device_id=device, device_id_type=MESH)
        return barrier, len(peers)

    def fetched(self, k, part, array=None):
        slot = (self.alpha, self.beta)[part](self.dp)
        return self.shard(self.nearest(k), self.core, slot, 1, array)

    @staticmethod
    def semaphores(planes):
        return 9 * planes


def gather_embed_kernel(
    planes,
    slots,
    groups,
    pos_table,
    prompts,
    gains,
    pos_index_t,
    tokens_in,
    own_qkv,
    own_out,
    own_up,
    own_down,
    hidden_out,
    qkv_out,
    full_qkv,
    full_out,
    full_up,
    part_down,
    table,
    tokens,
    pos_index,
    hidden,
    normed,
    qkv,
    first_full,
    second_full,
    third_full,
    send,
    recv,
    local,
):
    d = lax.axis_index("dp")
    w = lax.axis_index("wide")
    place = (d, w, planes, w // 2, lax.rem(w, 2))
    first = Gather(place, 0, first_full, (send, recv))
    second = Gather(place, 1, second_full, (send, recv))
    third = Gather(place, 2, third_full, (send, recv), by_rows=True)
    others = planes - 1
    qkv_columns = own_qkv.shape[1]
    barrier, greeted = first.greet()
    mine = pl.ds(pl.multiple_of(w * first.rows, first.rows), first.rows)
    loads = [
        pltpu.make_async_copy(own_qkv, first_full.at[mine, :qkv_columns], local.at[0]),
        pltpu.make_async_copy(own_out, first_full.at[mine, qkv_columns:], local.at[1]),
        pltpu.make_async_copy(own_up, second_full.at[mine], local.at[2]),
        pltpu.make_async_copy(own_down, third.shard(third.plane, third.core), local.at[3]),
        pltpu.make_async_copy(tokens_in, tokens, local.at[4]),
    ]
    for copy in loads:
        copy.start()
    fill_table(table, pos_table, prompts)
    columns = jnp.concatenate([pos_index_t[...].astype(F32)] * 4, 0).T
    pos_index[...] = columns.astype(jnp.int32)
    for copy in loads[:4]:
        copy.wait()
    pl.semaphore_wait(barrier, greeted)

    rows = tokens.shape[0]
    tiles = ORDER.count(("embed",))
    tile = rows // tiles
    outgoing = []

    def leave(source, target):
        copy = pltpu.make_async_copy(source, target, local.at[7 + len(outgoing)])
        copy.start()
        outgoing.append(copy)

    def embed_tile(index):
        part = slice(index * tile, (index + 1) * tile)
        value = embedded(groups, slots, index * tile, tokens[part], pos_index[part], table)
        hidden[part] = value
        leave(hidden.at[part], hidden_out.at[part])
        normal, _ = norm_parts(value)
        normed[part] = (normal * gains[0:1]).astype(BF)

    def qkv_tile(index):
        part = slice(index * tile, (index + 1) * tile)
        value = normed[part]

        def half(number, done):
            columns = pl.ds(pl.multiple_of(number * qkv_columns // 2, LANES), qkv_columns // 2)
            qkv[part, columns] = dot(value, first_full[:, columns]).astype(BF)
            return done

        lax.fori_loop(0, 2, half, 0)
        leave(qkv.at[part], qkv_out.at[part])

    gathers = (first, second, third)
    embeds, qkvs = iter(range(tiles)), iter(range(tiles))
    leave(second.shard(second.plane, second.core), second.shard(second.plane, second.core, array=full_up))
    for name, *where in ORDER:
        if name == "embed":
            index = next(embeds)
            if index == 0:
                loads[4].wait()
            embed_tile(index)
            continue
        if name == "qkv":
            qkv_tile(next(qkvs))
            continue
        gather, place = gathers[where[0]], where[1:]
        if name == "own":
            gather.along(gather.plane, place)
        elif name == "give":
            gather.give(gather.plane)
        elif name == "bring":
            gather.bring(*place)
        elif name == "fetch":
            gather.fetch(*place)
            leave(gather.fetched(*place), gather.fetched(*place, part_down))
        elif name == "pass_on":
            gather.pass_on(*place)
        elif name == "close":
            gather.close(*place)
            if gather is second:
                plane = second.nearest(*place)
                leave(second.shard(plane, second.core), second.shard(plane, second.core, array=full_up))
        elif gather is first:
            first.wait_all_given()
            leave(first_full.at[:, :qkv_columns], full_qkv)
            leave(first_full.at[:, qkv_columns:], full_out)
        else:
            for k in range(planes):
                plane = second.plane if k == 0 else second.nearest(k - 1)
                second.wait_given(plane)
                core = 1 - second.core
                leave(second.shard(plane, core), second.shard(plane, core, array=full_up))
    first.wait_fetched()
    second.wait_fetched()
    third.wait_fetched()
    first.wait_passed()
    second.wait_passed()
    for copy in outgoing:
        copy.wait()


def can_gather(axes, w_qkv, w_out, w_up, w_down):
    return (
        axes["dp"] == 4
        and axes["wide"] == 8
        and w_qkv.shape[0] % 16 == 0
        and w_down.shape[0] % (8 * 16) == 0
        and w_up.shape[1] % (8 * LANES) == 0
        and (w_qkv.shape[1] + w_out.shape[1]) % (8 * LANES) == 0
    )


def gather_embed(
    axes, size_group, tokens, pos_index, pos_table, prompts, gains, w_qkv, w_out, w_up, w_down
):
    rows, width = tokens.shape
    wide = axes["wide"]
    planes = wide // 2
    depth = w_qkv.shape[0] * wide
    inner_width = w_up.shape[1]
    vmem = pl.BlockSpec(memory_space=pltpu.VMEM)
    hbm = pl.BlockSpec(memory_space=pltpu.HBM)
    dma = pltpu.SemaphoreType.DMA
    count = Gather.semaphores(planes)
    first_columns = w_qkv.shape[1] + w_out.shape[1]
    return pl.pallas_call(
        functools.partial(gather_embed_kernel, planes, size_group.shape[0]),
        in_specs=[pl.BlockSpec(memory_space=pltpu.SMEM)] + [vmem] * 4 + [hbm] * 5,
        out_specs=[hbm] * 6,
        out_shape=[
            jax.ShapeDtypeStruct((rows, width), F32),
            jax.ShapeDtypeStruct((rows, w_qkv.shape[1]), BF),
            jax.ShapeDtypeStruct((depth, w_qkv.shape[1]), BF),
            jax.ShapeDtypeStruct((depth, w_out.shape[1]), BF),
            jax.ShapeDtypeStruct((depth, inner_width), BF),
            jax.ShapeDtypeStruct((inner_width, width), BF),
        ],
        scratch_shapes=[
            pltpu.VMEM((POS_ROWS + 3 * SLOT_ROWS, width), BF),
            pltpu.VMEM((rows, width), BF),
            pltpu.VMEM((rows, 8), jnp.int32),
            pltpu.VMEM((rows, width), F32),
            pltpu.VMEM((rows, width), BF),
            pltpu.VMEM((rows, w_qkv.shape[1]), BF),
            pltpu.VMEM((depth, first_columns), BF),
            pltpu.VMEM((depth, inner_width), BF),
            pltpu.VMEM((inner_width, width), BF),
            dma((3, count)),
            dma((3, count)),
            dma((7 + 2 * ORDER.count(("embed",)) + 2 + 2 * planes + 2 * (planes - 1),)),
        ],
        compiler_params=pltpu.CompilerParams(
            collective_id=0, has_side_effects=True, vmem_limit_bytes=VMEM_LIMIT
        ),
        name="gather_embed",
    )(
        size_group, pos_table, prompts, gains, pos_index.T, tokens, w_qkv, w_out, w_up, w_down
    )


def each_image(groups, slots, image):
    def body(slot, start):
        group = groups[slot]
        length = image_length(group)
        for size in range(3):
            pl.when(group == size)(functools.partial(image, size, start, length, slot))
        return start + length

    lax.fori_loop(0, slots, body, jnp.int32(0))


def window(count, rows, start, length):
    first = jnp.minimum((start // 8) * 8, rows - count)
    return pl.multiple_of(first, 8), start - first


def in_image(count, shift, length, first=0):
    row = lax.broadcasted_iota(jnp.int32, (count, LANES), 0) + first
    return (row >= shift) & (row < shift + length)


def head_lanes(head):
    lane = lax.broadcasted_iota(jnp.int32, (1, LANES), 1)
    return (lane < HEAD_DIM) if head % 2 == 0 else (lane >= HEAD_DIM)


def one_head(values, head, other):
    return jnp.where(head_lanes(head), values, other)


def marker(head):
    lane = lax.broadcasted_iota(jnp.int32, (1, LANES), 1)
    return jnp.where(lane == HEAD_DIM * (1 - head % 2), 1.0, 0.0).astype(BF)


def take(ref, rows):
    return [ref[rows, LANES * pair : LANES * (pair + 1)] for pair in range(PAIRS)]


def put(ref, rows, pair, new, inside):
    columns = slice(LANES * pair, LANES * (pair + 1))
    old = ref[rows, columns].astype(F32)
    ref[rows, columns] = jnp.where(inside, new, old).astype(BF)


def low(parts):
    return [part.astype(BF) for part in parts]


def head_rows(values, head):
    return values[HEAD_DIM * (head % 2) : HEAD_DIM * (head % 2 + 1)]


def own_quarters(values):
    count = values.shape[1] // 2
    return [values[:HEAD_DIM, :count], values[HEAD_DIM : 2 * HEAD_DIM, count:]]


def blocks_of(count):
    if count == LANES:
        return [(2 * pair, 2 * pair + 1) for pair in range(PAIRS)]
    return [(head,) for head in range(GROUP_HEADS)]


class Keys:
    def __init__(self, ref, rows, inside):
        self.pairs = take(ref, rows)
        bias = jnp.where(inside, 0.0, MASKED)
        self.bias = jnp.concatenate([bias, bias], 1)
        low_bias = bias.astype(BF)
        self.heads = [one_head(self.pairs[h // 2], h, low_bias) for h in range(GROUP_HEADS)]

    def scores(self, block, queries):
        if len(block) == 1:
            head = block[0]
            return dot(self.heads[head], one_head(queries[head // 2], head, marker(head)), NT)
        return dot(self.pairs[block[0] // 2], stacked(block, queries), NT) + self.bias


def stacked(block, parts):
    zero = jnp.zeros((1, LANES), BF)
    return jnp.concatenate([one_head(parts[h // 2], h, zero) for h in block], 0)


def attend_kernel(slots, groups, q_ref, k_ref, v_ref, out_ref, total_ref):
    out_ref[...] = jnp.zeros_like(out_ref)

    def image(size, start, length, slot):
        all_rows = out_ref.shape[0]
        span = KEY_ROWS[size]
        chunks = QUERY_CHUNKS[size]
        key_first, key_shift = window(span, all_rows, start, length)
        first, shift = window(max(span, 256), all_rows, start, length)
        key_rows = pl.ds(key_first, span)
        keys = Keys(k_ref, key_rows, in_image(span, key_shift, length))
        ones = jnp.ones((8, span), BF)
        value_t = [x.T for x in take(v_ref, key_rows)]

        def values_of(block):
            pair = value_t[block[0] // 2]
            rows = pair if len(block) == 2 else head_rows(pair, block[0])
            return jnp.concatenate([rows, ones], 0)

        for chunk, count in chunks:
            rows = pl.ds(pl.multiple_of(first + chunk, 8), count)
            query = take(q_ref, rows)
            blocks = blocks_of(count)
            scores = [keys.scores(block, query) for block in blocks]
            peaks = [jnp.max(s, axis=0, keepdims=True) * SCORE for s in scores]
            powers = [jnp.exp2(s * SCORE - m).astype(BF) for s, m in zip(scores, peaks)]
            mixed = [dot(values_of(block), e) for block, e in zip(blocks, powers)]
            parts = []
            for block, peak, value in zip(blocks, peaks, mixed):
                depth = HEAD_DIM * len(block)
                sums = value[depth : depth + 1]
                total = peak + jnp.log2(sums)
                for number, head in enumerate(block):
                    total_ref[0, GROUP_HEADS * slot + head, :, chunk : chunk + count] = total[
                        :, number * count : (number + 1) * count
                    ]
                value = value[:depth] / sums
                parts += [value] if len(block) == 1 else own_quarters(value)
            inside = in_image(count, shift, length, chunk)
            for pair in range(PAIRS):
                put(out_ref, rows, pair, jnp.concatenate(parts[2 * pair : 2 * pair + 2], 0).T, inside)

    each_image(groups, slots, image)


def attend(size_group, qkv):
    rows = qkv.shape[0]
    width = qkv.shape[1] // 3
    steps = width // HEAD_COLS
    slots = size_group.shape[0]
    block = lambda shift: pl.BlockSpec((rows, HEAD_COLS), lambda i, g: (0, shift * steps + i))
    return pl.pallas_call(
        functools.partial(attend_kernel, slots),
        grid_spec=pltpu.PrefetchScalarGridSpec(
            num_scalar_prefetch=1,
            grid=(steps,),
            in_specs=[block(0), block(1), block(2)],
            out_specs=[
                block(0),
                pl.BlockSpec((1, GROUP_HEADS * slots, 1, LARGE), lambda i, g: (i, 0, 0, 0)),
            ],
        ),
        out_shape=[
            jax.ShapeDtypeStruct((rows, width), BF),
            jax.ShapeDtypeStruct((steps, GROUP_HEADS * slots, 1, LARGE), F32),
        ],
        compiler_params=pltpu.CompilerParams(vmem_limit_bytes=VMEM_LIMIT),
        name="attend",
    )(size_group, qkv, qkv, qkv)


def attend_back_kernel(slots, groups, q_ref, k_ref, v_ref, grad_ref, mixed_ref, total_ref, *refs):
    middles, refs = refs[:PAIRS], refs[PAIRS:]
    passed_in, dq_ref, dk_ref, dv_ref, dq_sum, dk_sum, dv_sum, middle_sum, passed_out = refs
    passed_out[...] = passed_in[...]
    for ref in (dq_sum, dk_sum, dv_sum, middle_sum):
        ref[...] = jnp.zeros_like(ref)

    def image(size, start, length, slot):
        all_rows = dq_ref.shape[0]
        span = KEY_ROWS[size]
        chunks = QUERY_CHUNKS[size]
        key_first, key_shift = window(span, all_rows, start, length)
        first, shift = window(max(span, 256), all_rows, start, length)
        key_rows = pl.ds(key_first, span)
        key_inside = in_image(span, key_shift, length)
        keys = Keys(k_ref, key_rows, key_inside)
        key_t = [x.T for x in keys.pairs]
        value = take(v_ref, key_rows)
        dk = [jnp.zeros((span, LANES), F32)] * PAIRS
        dv = [jnp.zeros((span, LANES), F32)] * PAIRS

        def add_prompts(total, pair, values, before):
            count = min(values.shape[0], 256)
            slot_row = lax.broadcasted_iota(jnp.int32, (SLOT_ROWS, count), 0)
            row = lax.broadcasted_iota(jnp.int32, (SLOT_ROWS, count), 1)
            chosen = (row == slot_row + before + 1) & (slot_row < PROMPTS)
            chosen = jnp.where(chosen, 1.0, 0.0).astype(BF)
            columns = slice(LANES * pair, LANES * (pair + 1))
            total[:, columns] += dot(chosen, values[:count].astype(BF))

        for chunk, count in chunks:
            rows = pl.ds(pl.multiple_of(first + chunk, 8), count)
            inside = in_image(count, shift, length, chunk)
            query = take(q_ref, rows)
            grad32 = [jnp.where(inside, x.astype(F32), 0.0) for x in take(grad_ref, rows)]
            products = [(x * y.astype(F32)).T for x, y in zip(grad32, take(mixed_ref, rows))]
            grad = low(grad32)
            blocks = blocks_of(count)
            queries = [stacked(block, query) for block in blocks]
            grads = [stacked(block, grad) for block in blocks]
            scores = [keys.scores(block, query) for block in blocks]
            prob_grads = [dot(value[block[0] // 2], g, NT) for block, g in zip(blocks, grads)]

            def side_by_side(block, row_of):
                found = [row_of(head) for head in block]
                return found[0] if len(found) == 1 else jnp.concatenate(found, 1)

            totals = [
                side_by_side(
                    block, lambda h: total_ref[0, GROUP_HEADS * slot + h, :, chunk : chunk + count]
                )
                for block in blocks
            ]
            deltas = [
                side_by_side(
                    block,
                    lambda h: jnp.sum(head_rows(products[h // 2], h), axis=0, keepdims=True),
                )
                for block in blocks
            ]
            probs = [jnp.exp2(s * SCORE - t) for s, t in zip(scores, totals)]
            score_grads = [
                (p * (g - t)).astype(BF) for p, g, t in zip(probs, prob_grads, deltas)
            ]
            parts = []
            for block, prob, score_grad, q, g in zip(blocks, probs, score_grads, queries, grads):
                pair = block[0] // 2
                dv[pair] += dot(prob.astype(BF), g)
                dk[pair] += dot(score_grad, q)
                if len(block) == 1:
                    parts.append(dot(head_rows(key_t[pair], block[0]), score_grad))
                else:
                    parts += own_quarters(dot(key_t[pair], score_grad))
            for pair in range(PAIRS):
                dq = jnp.concatenate(parts[2 * pair : 2 * pair + 2], 0).T * SCALE
                put(dq_ref, rows, pair, dq, inside)
                if chunk == 0:
                    add_prompts(dq_sum, pair, dq, shift)
        for pair in range(PAIRS):
            put(dk_ref, key_rows, pair, dk[pair] * SCALE, key_inside)
            put(dv_ref, key_rows, pair, dv[pair], key_inside)
            add_prompts(dk_sum, pair, dk[pair] * SCALE, key_shift)
            add_prompts(dv_sum, pair, dv[pair], key_shift)
            columns = slice(LANES * pair, LANES * (pair + 1))
            middle_sum[:, columns] += middles[pair][pl.ds(start + 1, SLOT_ROWS), :]

    each_image(groups, slots, image)


def attend_back(size_group, qkv, mixed_grad, mixed, totals, middle_grad, passed):
    rows = qkv.shape[0]
    width = qkv.shape[1] // 3
    steps = width // HEAD_COLS
    slots = size_group.shape[0]
    block = lambda shift: pl.BlockSpec((rows, HEAD_COLS), lambda i, g: (0, shift * steps + i))
    middle = lambda pair: pl.BlockSpec((rows, LANES), lambda i, g: (0, PAIRS * i + pair))
    return pl.pallas_call(
        functools.partial(attend_back_kernel, slots),
        grid_spec=pltpu.PrefetchScalarGridSpec(
            num_scalar_prefetch=1,
            grid=(steps,),
            in_specs=[
                block(0),
                block(1),
                block(2),
                block(0),
                block(0),
                pl.BlockSpec((1, GROUP_HEADS * slots, 1, LARGE), lambda i, g: (i, 0, 0, 0)),
            ]
            + [middle(pair) for pair in range(PAIRS)]
            + [block(0)],
            out_specs=[block(0)] * 3
            + [pl.BlockSpec((SLOT_ROWS, HEAD_COLS), lambda i, g: (0, i))] * 4
            + [block(0)],
        ),
        out_shape=[jax.ShapeDtypeStruct((rows, width), BF)] * 3
        + [jax.ShapeDtypeStruct((SLOT_ROWS, width), F32)] * 4
        + [jax.ShapeDtypeStruct((rows, width), BF)],
        compiler_params=pltpu.CompilerParams(vmem_limit_bytes=VMEM_LIMIT),
        name="attend_back",
    )(
        size_group,
        qkv,
        qkv,
        qkv,
        mixed_grad,
        mixed,
        totals,
        *[middle_grad] * PAIRS,
        passed,
    )


def feed_kernel(
    slots,
    chunk,
    groups,
    hidden,
    mixed,
    cotangent,
    gains,
    w_out,
    w_up,
    w_down,
    out_ref,
    middle_grad_ref,
    mixed_grad_ref,
):
    tile = hidden.shape[0]
    inner_width = w_up.shape[1]
    rows = pl.program_id(0) * tile + lax.broadcasted_iota(jnp.int32, (tile, 1), 0)
    live = rows < total_length(groups, slots)
    out_grad = jnp.where(live, cotangent[...].astype(F32), 0.0)
    out_grad_low = out_grad.astype(BF)
    middle = hidden[...] + dot(mixed[...], w_out[...])
    normal, rstd = norm_parts(middle)
    gain = gains[1:2]
    second = (normal * gain).astype(BF)
    forward = middle
    back = jnp.zeros_like(middle)
    for first in range(0, inner_width, chunk):
        part = slice(first, first + chunk)
        inner = dot(second, w_up[:, part])
        act_grad = dot(out_grad_low, w_down[part], NT)
        phi = 0.5 + 0.5 * lax.erf(inner * (0.5**0.5))
        density = jnp.exp2(inner * inner * (-0.5 * LOG2E)) * 0.3989422804014327
        activated = (inner * phi).astype(BF)
        inner_grad = (act_grad * (phi + inner * density)).astype(BF)
        forward = forward + dot(activated, w_down[part])
        back = back + dot(inner_grad, w_up[:, part], NT)
    out_ref[...] = jnp.where(live, forward, 0.0).astype(BF)
    middle_grad = out_grad + norm_back(normal, rstd, gain, back)
    middle_grad_ref[...] = middle_grad
    mixed_grad_ref[...] = dot(middle_grad.astype(BF), w_out[...], NT).astype(BF)


def feed(size_group, hidden, mixed, cotangent, gains, w_out, w_up, w_down):
    rows, width = hidden.shape
    tile = 384
    chunk = 512
    keep = lambda i, g: (0, 0)
    whole = lambda a: pl.BlockSpec(a.shape, keep, pipeline_mode=pl.Buffered(1))
    by_row = pl.BlockSpec((tile, width), lambda i, g: (i, 0))
    return pl.pallas_call(
        functools.partial(feed_kernel, size_group.shape[0], chunk),
        grid_spec=pltpu.PrefetchScalarGridSpec(
            num_scalar_prefetch=1,
            grid=(rows // tile,),
            in_specs=[by_row, by_row, by_row, whole(gains), whole(w_out), whole(w_up), whole(w_down)],
            out_specs=[by_row, by_row, by_row],
        ),
        out_shape=[
            jax.ShapeDtypeStruct((rows, width), BF),
            jax.ShapeDtypeStruct((rows, width), F32),
            jax.ShapeDtypeStruct((rows, width), BF),
        ],
        compiler_params=pltpu.CompilerParams(vmem_limit_bytes=VMEM_LIMIT),
        name="feed",
    )(size_group, hidden, mixed, cotangent, gains, w_out, w_up, w_down)


def gather_feed_kernel(
    planes,
    slots,
    chunk,
    groups,
    gains,
    hidden_in,
    mixed_in,
    cotangent_in,
    full_out,
    full_up,
    own_down,
    part_down,
    out_ref,
    middle_grad_ref,
    mixed_grad_ref,
    middle,
    mixed,
    cotangent,
    w_out,
    w_up,
    w_down,
    active,
    slope,
    send,
    recv,
    weights_in,
    rows_in,
    rows_out,
):
    d = lax.axis_index("dp")
    w = lax.axis_index("wide")
    down = Gather((d, w, planes, w // 2, lax.rem(w, 2)), 0, w_down, (send, recv), by_rows=True)
    barrier, greeted = down.greet(planes=False)
    others = planes - 1
    tiles = rows_in.shape[0]
    tile = middle.shape[0] // tiles
    inner_width = w_up.shape[1]

    def tile_rows(index):
        return pl.ds(pl.multiple_of(index * tile, tile), tile)

    def loads(index):
        part = tile_rows(index)
        return [
            pltpu.make_async_copy(hidden_in.at[part], middle.at[part], rows_in.at[index, 0]),
            pltpu.make_async_copy(mixed_in.at[part], mixed.at[part], rows_in.at[index, 1]),
            pltpu.make_async_copy(cotangent_in.at[part], cotangent.at[part], rows_in.at[index, 2]),
        ]

    def stores(index):
        part = tile_rows(index)
        return [
            pltpu.make_async_copy(middle.at[part], middle_grad_ref.at[part], rows_out.at[index, 0]),
            pltpu.make_async_copy(mixed.at[part], mixed_grad_ref.at[part], rows_out.at[index, 1]),
            pltpu.make_async_copy(cotangent.at[part], out_ref.at[part], rows_out.at[index, 2]),
        ]

    down_loads = [(own_down, down.shard(down.plane, down.core))]
    for k in range(others):
        for part in (0, 1):
            down_loads.append((down.fetched(k, part, part_down), down.fetched(k, part)))
    down_loads = [
        pltpu.make_async_copy(source, target, weights_in.at[2 + index])
        for index, (source, target) in enumerate(down_loads)
    ]
    out_load = pltpu.make_async_copy(full_out, w_out, weights_in.at[0])
    up_load = pltpu.make_async_copy(full_up, w_up, weights_in.at[1])
    for copy in down_loads:
        copy.start()
    out_load.start()
    for copy in loads(0):
        copy.start()
    up_load.start()
    for index in range(1, tiles):
        for copy in loads(index):
            copy.start()
    for copy in down_loads:
        copy.wait()
    pl.semaphore_wait(barrier, greeted)
    for k in range(others):
        down.exchange(down.nearest(k))
    down.give(down.plane)
    out_load.wait()
    up_load.wait()
    gain = gains[1:2]

    def pump(step):
        @pl.when((step >= 0) & (step < others))
        def _():
            down.pass_on(step, 0)
            down.pass_on(step, 1)

        @pl.when((step >= 2) & (step < others + 2))
        def _():
            down.close(step - 2)

    def up_tile(index, carry):
        for copy in loads(index):
            copy.wait()
        part = tile_rows(index)
        value = middle[part, :] + dot(mixed[part, :], w_out[...])
        middle[part, :] = value
        normal, _ = norm_parts(value)
        second = (normal * gain).astype(BF)
        for first in range(0, inner_width, chunk):
            columns = slice(first, first + chunk)
            inner = dot(second, w_up[:, columns])
            phi = 0.5 + 0.5 * lax.erf(inner * (0.5**0.5))
            density = jnp.exp2(inner * inner * (-0.5 * LOG2E)) * 0.3989422804014327
            active[part, columns] = (inner * phi).astype(BF)
            slope[part, columns] = phi + inner * density
            if first + chunk == inner_width // 2:
                pump(2 * index)
        pump(2 * index + 1)
        return carry

    lax.fori_loop(0, tiles, up_tile, 0)
    for step in range(2 * tiles, others + 2):
        pump(step)
    down.wait_all_given()
    total = total_length(groups, slots)

    def down_tile(index, carry):
        part = tile_rows(index)
        rows = index * tile + lax.broadcasted_iota(jnp.int32, (tile, 1), 0)
        live = rows < total
        out_grad = jnp.where(live, cotangent[part, :].astype(F32), 0.0)
        out_grad_low = out_grad.astype(BF)
        value = middle[part, :]
        back = jnp.zeros_like(value)
        for first in range(0, inner_width, chunk):
            columns = slice(first, first + chunk)
            act_grad = dot(out_grad_low, w_down[columns], NT)
            inner_grad = (act_grad * slope[part, columns]).astype(BF)
            back = back + dot(inner_grad, w_up[:, columns], NT)
        forward = value + dot(active[part, :], w_down[...])
        cotangent[part, :] = jnp.where(live, forward, 0.0).astype(BF)
        normal, rstd = norm_parts(value)
        middle_grad = out_grad + norm_back(normal, rstd, gain, back)
        middle[part, :] = middle_grad
        mixed[part, :] = dot(middle_grad.astype(BF), w_out[...], NT).astype(BF)
        for copy in stores(index):
            copy.start()
        return carry

    lax.fori_loop(0, tiles, down_tile, 0)
    down.wait_passed()
    for index in range(tiles):
        for copy in stores(index):
            copy.wait()


def gather_feed(axes, size_group, hidden, mixed, cotangent, gains, w_out, w_up, w_down, part_down):
    rows, width = hidden.shape
    planes = axes["wide"] // 2
    inner_width = w_up.shape[1]
    tiles = 3
    hbm = pl.BlockSpec(memory_space=pltpu.HBM)
    dma = pltpu.SemaphoreType.DMA
    count = Gather.semaphores(planes)
    return pl.pallas_call(
        functools.partial(gather_feed_kernel, planes, size_group.shape[0], 512),
        in_specs=[
            pl.BlockSpec(memory_space=pltpu.SMEM),
            pl.BlockSpec(memory_space=pltpu.VMEM),
        ]
        + [hbm] * 7,
        out_specs=[hbm] * 3,
        out_shape=[
            jax.ShapeDtypeStruct((rows, width), BF),
            jax.ShapeDtypeStruct((rows, width), F32),
            jax.ShapeDtypeStruct((rows, width), BF),
        ],
        scratch_shapes=[
            pltpu.VMEM((rows, width), F32),
            pltpu.VMEM((rows, width), BF),
            pltpu.VMEM((rows, width), BF),
            pltpu.VMEM(w_out.shape, BF),
            pltpu.VMEM(w_up.shape, BF),
            pltpu.VMEM((inner_width, width), BF),
            pltpu.VMEM((rows, inner_width), BF),
            pltpu.VMEM((rows, inner_width), F32),
            dma((1, count)),
            dma((1, count)),
            dma((3 + 2 * (planes - 1),)),
            dma((tiles, 3)),
            dma((tiles, 3)),
        ],
        compiler_params=pltpu.CompilerParams(
            collective_id=2, has_side_effects=True, vmem_limit_bytes=VMEM_LIMIT
        ),
        name="gather_feed",
    )(size_group, gains, hidden, mixed, cotangent, w_out, w_up, w_down, part_down)


class Shared:
    def __init__(self, dp, wide, mine, near, far, result, sems):
        self.members = 2 * dp
        self.planes = wide // 2
        self.rows = mine.shape[0] // self.members
        self.d = lax.axis_index("dp")
        w = lax.axis_index("wide")
        self.plane = w // 2
        self.core = lax.rem(w, 2)
        self.member = self.d * 2 + self.core
        self.mine, self.near, self.far, self.result = mine, near, far, result
        self.send, self.near_in, self.far_in, self.last_in = sems

    def peer(self, step):
        other = lax.rem(self.member + step, self.members)
        return other, (other // 2, self.plane * 2 + lax.rem(other, 2))

    def plane_peer(self, step):
        other = lax.rem(self.plane + step, self.planes)
        return other, (self.d, other * 2 + self.core)

    def greet(self):
        barrier = pltpu.get_barrier_semaphore()
        for step in range(1, self.members):
            pl.semaphore_signal(barrier, inc=1, device_id=self.peer(step)[1], device_id_type=MESH)
        for step in range(1, self.planes):
            pl.semaphore_signal(
                barrier, inc=1, device_id=self.plane_peer(step)[1], device_id_type=MESH
            )
        return barrier, self.members + self.planes - 2

    def part(self, ref, index):
        return ref.at[pl.ds(pl.multiple_of(index * self.rows, self.rows), self.rows)]

    def copy(self, source, target, send, recv, device):
        return pltpu.make_async_remote_copy(
            source, target, send, recv, device_id=device, device_id_type=MESH
        )

    def first(self, step):
        other, device = self.peer(step)
        return self.copy(
            self.part(self.mine, other),
            self.near.at[step],
            self.send.at[0, step],
            self.near_in.at[step],
            device,
        )

    def second(self, step):
        mine = self.far.at[self.plane]
        device = self.plane_peer(step)[1]
        return self.copy(mine, mine, self.send.at[1, step], self.far_in.at[step], device)

    def third(self, step):
        mine = self.part(self.result, self.member)
        device = self.peer(step)[1]
        return self.copy(mine, mine, self.send.at[2, step], self.last_in.at[step], device)

    def start_first(self):
        for step in range(1, self.members):
            self.first(step).start()
        self.near[0] = self.part(self.mine, self.member)[...]

    def start_second(self):
        for step in range(1, self.members):
            self.first(step).wait_recv()
        total = jnp.zeros(self.near.shape[1:], F32)
        for index in range(self.members):
            total = total + self.near[lax.rem(self.member - index + self.members, self.members)]
        self.far[self.plane] = total
        for step in range(1, self.planes):
            self.second(step).start()

    def start_third(self):
        for step in range(1, self.planes):
            self.second(step).wait_recv()
        total = jnp.zeros(self.near.shape[1:], F32)
        for index in range(self.planes):
            total = total + self.far[index]
        self.part(self.result, self.member)[...] = total
        for step in range(1, self.members):
            self.third(step).start()

    def end(self):
        for step in range(1, self.members):
            self.third(step).wait_recv()
        for step in range(1, self.members):
            self.first(step).wait_send()
            self.third(step).wait_send()
        for step in range(1, self.planes):
            self.second(step).wait_send()


def finish_kernel(
    dp,
    wide,
    slots,
    groups,
    prompts,
    gains,
    dq_sum,
    dk_sum,
    dv_sum,
    middle_sum,
    hidden_in,
    middle_grad_in,
    dq_in,
    dk_in,
    dv_in,
    w_qkv_in,
    input_grad_out,
    prompt_grad,
    penalty,
    hidden,
    middle_grad,
    dq,
    dk,
    dv,
    w_qkv,
    input_grad,
    known,
    mine,
    near,
    far,
    result,
    send,
    near_in,
    far_in,
    last_in,
    weight_in,
    rows_in,
    rows_out,
):
    shared = Shared(dp, wide, mine, near, far, result, (send, near_in, far_in, last_in))
    barrier, greeted = shared.greet()
    tiles = rows_in.shape[0]
    width = hidden.shape[1]
    tile = hidden.shape[0] // tiles
    weight_load = pltpu.make_async_copy(w_qkv_in, w_qkv, weight_in)
    weight_load.start()

    def tile_rows(index):
        return pl.ds(pl.multiple_of(index * tile, tile), tile)

    def loads(index):
        part = tile_rows(index)
        pairs = (
            (dq_in, dq),
            (dk_in, dk),
            (dv_in, dv),
            (hidden_in, hidden),
            (middle_grad_in, middle_grad),
        )
        return [
            pltpu.make_async_copy(source.at[part], target.at[part], rows_in.at[index, number])
            for number, (source, target) in enumerate(pairs)
        ]

    for index in range(tiles):
        for copy in loads(index):
            copy.start()

    def back(q, k, v):
        return (
            dot(q, w_qkv[:, :width], NT)
            + dot(k, w_qkv[:, width : 2 * width], NT)
            + dot(v, w_qkv[:, 2 * width :], NT)
        )

    known[...] = jnp.zeros_like(known)
    known[: prompts.shape[0]] = prompts[...]
    pieces = []
    for ref in (dq_sum, dk_sum, dv_sum):
        rest = ref[...]
        terms = []
        for _ in range(2):
            terms.append(rest.astype(BF))
            rest = rest - terms[-1].astype(F32)
        pieces.append(jnp.concatenate(terms, 0))
    weight_load.wait()
    terms = back(*pieces)
    normed_grad = terms[:SLOT_ROWS] + terms[SLOT_ROWS:]
    normal, rstd = norm_parts(known[...])
    local = middle_sum[...] + norm_back(normal, rstd, gains[0:1], normed_grad)
    slot_row = lax.broadcasted_iota(jnp.int32, (SLOT_ROWS, 1), 0)
    count = total_length(groups, slots).astype(F32)
    mine[...] = jnp.where(slot_row < PROMPTS, local, jnp.where(slot_row == PROMPTS, count, 0.0))
    pl.semaphore_wait(barrier, greeted)
    shared.start_first()

    def store(index):
        part = tile_rows(index)
        return pltpu.make_async_copy(
            input_grad.at[part], input_grad_out.at[part], rows_out.at[index]
        )

    def row_tile(index, carry):
        for copy in loads(index):
            copy.wait()
        part = tile_rows(index)
        normal, rstd = norm_parts(hidden[part, :])
        normed_grad = back(dq[part, :], dk[part, :], dv[part, :])
        hidden_grad = middle_grad[part, :] + norm_back(normal, rstd, gains[0:1], normed_grad)
        prompt_slot, live = row_places(groups, slots, index * tile, tile)
        input_grad[part, :] = jnp.where(live & (prompt_slot < 0), hidden_grad, 0.0).astype(BF)
        store(index).start()
        pl.when(index == 0)(shared.start_second)
        pl.when(index == 1)(shared.start_third)
        return carry

    lax.fori_loop(0, tiles, row_tile, 0)
    shared.end()
    given = prompts[...]
    size = given.shape[0] * given.shape[1]
    count = result[PROMPTS : PROMPTS + 1]
    prompt_grad[...] = result[:PROMPTS] + (2.0 * PENALTY_RATE / size) * count * given
    square = jnp.sum(jnp.sum(given * given, axis=1, keepdims=True), axis=0, keepdims=True)
    penalty[...] = PENALTY_RATE * count[:, :1] * (square / size)
    for index in range(tiles):
        store(index).wait()


def finish(axes, size_group, prompts, gains, sums, hidden, middle_grad, dq, dk, dv, w_qkv):
    rows, width = hidden.shape
    dp, wide = axes["dp"], axes["wide"]
    members, planes = 2 * dp, wide // 2
    tiles = 3
    dma = pltpu.SemaphoreType.DMA
    vmem = pl.BlockSpec(memory_space=pltpu.VMEM)
    hbm = pl.BlockSpec(memory_space=pltpu.HBM)
    input_grad, prompt_grad, penalty = pl.pallas_call(
        functools.partial(finish_kernel, dp, wide, size_group.shape[0]),
        in_specs=[pl.BlockSpec(memory_space=pltpu.SMEM)] + [vmem] * 6 + [hbm] * 6,
        out_specs=[hbm, vmem, vmem],
        out_shape=[
            jax.ShapeDtypeStruct((rows, width), BF),
            jax.ShapeDtypeStruct(prompts.shape, F32),
            jax.ShapeDtypeStruct((1, 1), F32),
        ],
        scratch_shapes=[
            pltpu.VMEM((rows, width), F32),
            pltpu.VMEM((rows, width), F32),
            pltpu.VMEM((rows, width), BF),
            pltpu.VMEM((rows, width), BF),
            pltpu.VMEM((rows, width), BF),
            pltpu.VMEM(w_qkv.shape, BF),
            pltpu.VMEM((rows, width), BF),
            pltpu.VMEM((SLOT_ROWS, width), F32),
            pltpu.VMEM((SLOT_ROWS, width), F32),
            pltpu.VMEM((members, SLOT_ROWS // members, width), F32),
            pltpu.VMEM((planes, SLOT_ROWS // members, width), F32),
            pltpu.VMEM((SLOT_ROWS, width), F32),
            dma((3, max(members, planes))),
            dma((members,)),
            dma((planes,)),
            dma((members,)),
            dma,
            dma((tiles, 5)),
            dma((tiles,)),
        ],
        compiler_params=pltpu.CompilerParams(
            collective_id=1, has_side_effects=True, vmem_limit_bytes=VMEM_LIMIT
        ),
        name="finish",
    )(size_group, prompts, gains, *sums, hidden, middle_grad, dq, dk, dv, w_qkv)
    return input_grad, prompt_grad, penalty[0, 0]


def shards(
    axes,
    tokens,
    pos_index,
    size_group,
    pos_table,
    prompts,
    norm_gains,
    w_qkv,
    w_out,
    w_up,
    w_down,
    cotangent,
):
    if can_gather(axes, w_qkv, w_out, w_up, w_down):
        hidden, qkv, full_qkv, full_out, full_up, part_down = gather_embed(
            axes,
            size_group,
            tokens,
            pos_index,
            pos_table,
            prompts,
            norm_gains,
            w_qkv,
            w_out,
            w_up,
            w_down,
        )
        mixed, totals = attend(size_group, qkv)
        outputs, middle_grad, mixed_grad = gather_feed(
            axes,
            size_group,
            hidden,
            mixed,
            cotangent,
            norm_gains,
            full_out,
            full_up,
            w_down,
            part_down,
        )
    else:
        full_qkv = lax.all_gather(w_qkv, "wide", axis=0, tiled=True)
        full_out = lax.all_gather(w_out, "wide", axis=0, tiled=True)
        full_up = lax.all_gather(w_up, "wide", axis=0, tiled=True)
        full_down = lax.all_gather(w_down, "wide", axis=0, tiled=True)
        hidden, qkv = embed(size_group, tokens, pos_index, pos_table, prompts, norm_gains, full_qkv)
        mixed, totals = attend(size_group, qkv)
        outputs, middle_grad, mixed_grad = feed(
            size_group, hidden, mixed, cotangent, norm_gains, full_out, full_up, full_down
        )
    dq, dk, dv, *sums, outputs = attend_back(
        size_group, qkv, mixed_grad, mixed, totals, middle_grad, outputs
    )
    input_grad, prompt_grad, penalty = finish(
        axes, size_group, prompts, norm_gains, sums, hidden, middle_grad, dq, dk, dv, full_qkv
    )
    return (outputs, input_grad, prompt_grad, penalty)


def solution(mesh):
    return jax.shard_map(
        functools.partial(shards, dict(mesh.shape)),
        mesh=mesh,
        in_specs=(
            P(("dp", "wide"), None),
            P(("dp", "wide"), None),
            P(("dp", "wide")),
            P(),
            P(),
            P(),
            P("wide", None),
            P("wide", None),
            P("wide", None),
            P("wide", None),
            P(("dp", "wide"), None),
        ),
        out_specs=(P(("dp", "wide"), None), P(("dp", "wide"), None), P(), P()),
        check_vma=False,
    )
```

```python
import functools

import jax
import jax.numpy as jnp
from jax import lax
from jax.experimental import pallas as pl
from jax.experimental.pallas import tpu as pltpu
from jax.sharding import PartitionSpec as P

HEADS = 12
HEAD_DIM = 64
PROMPTS = 50
PATCH_S = 100
PATCH_M = 196
PATCH_L = 576

EPSILON = 1e-06
PENALTY_RATE = 3e-05
SCALE = HEAD_DIM**-0.5
LOG2E = 1.4426950408889634
SCORE = SCALE * LOG2E

BF = jnp.bfloat16
F32 = jnp.float32
NN = (((1,), (0,)), ((), ()))
NT = (((1,), (1,)), ((), ()))
MESH = pl.DeviceIdType.MESH

LANES = 128
HEAD_COLS = 384
PAIRS = HEAD_COLS // LANES
GROUP_HEADS = HEAD_COLS // HEAD_DIM
LARGE = 640
KEY_ROWS = (160, 256, LARGE)
QUERY_CHUNKS = (((0, 256),), ((0, 256),), ((0, 256), (256, 256), (512, 128)))
MASKED = -1e30
POS_ROWS = 256
VMEM_LIMIT = 60 << 20
SLOT_ROWS = 64


def dot(a, b, dims=NN):
    return lax.dot_general(a, b, dims, preferred_element_type=F32)


def image_length(group):
    patches = jnp.where(group == 0, PATCH_S, jnp.where(group == 1, PATCH_M, PATCH_L))
    return jnp.where(group == 3, 0, 1 + PROMPTS + patches).astype(jnp.int32)


def total_length(groups, slots):
    total = jnp.int32(0)
    for slot in range(slots):
        total = total + image_length(groups[slot])
    return total


def row_places(groups, slots, first_row, count):
    rows = first_row + lax.broadcasted_iota(jnp.int32, (count, 1), 0)
    place = rows
    start = jnp.int32(0)
    for slot in range(slots):
        length = image_length(groups[slot])
        place = jnp.where((rows >= start) & (length > 0), rows - start, place)
        start = start + length
    live = rows < start
    prompt_slot = jnp.where(live & (place >= 1) & (place <= PROMPTS), place - 1, -1)
    return prompt_slot, live


def norm_parts(values):
    centered = values - jnp.mean(values, axis=-1, keepdims=True)
    rstd = lax.rsqrt(jnp.mean(centered * centered, axis=-1, keepdims=True) + EPSILON)
    return centered * rstd, rstd


def norm_back(normal, rstd, gain, grad):
    scaled = grad * gain
    return (
        scaled
        - jnp.mean(scaled, axis=-1, keepdims=True)
        - normal * jnp.mean(scaled * normal, axis=-1, keepdims=True)
    ) * rstd


def fill_table(table, pos_table, prompts):
    table[...] = jnp.zeros_like(table)
    table[: pos_table.shape[0]] = pos_table[...]
    rest = prompts[...]
    for piece in range(3):
        part = rest.astype(BF)
        first = POS_ROWS + piece * SLOT_ROWS
        table[first : first + PROMPTS] = part
        rest = rest - part.astype(F32)


def embedded(groups, slots, first_row, tokens, pos_index, table):
    prompt_slot, _ = row_places(groups, slots, first_row, tokens.shape[0])
    is_prompt = prompt_slot >= 0
    lane = lax.broadcasted_iota(jnp.int32, (1, POS_ROWS), 1)
    left = jnp.where(is_prompt, -1, pos_index[:, 0:1])
    right = jnp.where(is_prompt, -1, pos_index[:, 1:2])
    half_hot = jnp.where(lane == left, 0.5, 0.0) + jnp.where(lane == right, 0.5, 0.0)
    slot_lane = lax.broadcasted_iota(jnp.int32, (1, 3 * SLOT_ROWS), 1)
    slot_lane = lax.rem(slot_lane, SLOT_ROWS)
    slot_hot = jnp.where(slot_lane == prompt_slot, 1.0, 0.0)
    picked = dot(half_hot.astype(BF), table[:POS_ROWS]) + dot(
        slot_hot.astype(BF), table[POS_ROWS:]
    )
    return jnp.where(is_prompt, 0.0, tokens.astype(F32)) + picked


def embed_kernel(
    slots, groups, tokens, pos_index, pos_table, prompts, gains, w_qkv, hidden_out, qkv_out, table
):
    tile = tokens.shape[0]
    step = pl.program_id(0)

    @pl.when(step == 0)
    def _():
        fill_table(table, pos_table, prompts)

    hidden = embedded(groups, slots, step * tile, tokens[...], pos_index[...], table)
    hidden_out[...] = hidden
    normal, _ = norm_parts(hidden)
    normed = (normal * gains[0:1]).astype(BF)
    qkv_out[...] = dot(normed, w_qkv[...]).astype(BF)


def embed(size_group, tokens, pos_index, pos_table, prompts, gains, w_qkv):
    rows, width = tokens.shape
    tile = 384
    keep = lambda i, g: (0, 0)
    whole = lambda a: pl.BlockSpec(a.shape, keep, pipeline_mode=pl.Buffered(1))
    by_row = lambda columns: pl.BlockSpec((tile, columns), lambda i, g: (i, 0))
    return pl.pallas_call(
        functools.partial(embed_kernel, size_group.shape[0]),
        grid_spec=pltpu.PrefetchScalarGridSpec(
            num_scalar_prefetch=1,
            grid=(rows // tile,),
            in_specs=[
                by_row(width),
                by_row(2),
                whole(pos_table),
                whole(prompts),
                whole(gains),
                whole(w_qkv),
            ],
            out_specs=[by_row(width), by_row(3 * width)],
            scratch_shapes=[pltpu.VMEM((POS_ROWS + 3 * SLOT_ROWS, width), BF)],
        ),
        out_shape=[
            jax.ShapeDtypeStruct((rows, width), F32),
            jax.ShapeDtypeStruct((rows, 3 * width), BF),
        ],
        compiler_params=pltpu.CompilerParams(vmem_limit_bytes=VMEM_LIMIT),
        name="embed",
    )(size_group, tokens, pos_index, pos_table, prompts, gains, w_qkv)


ORDER = (
    ("own", 0, 0), ("own", 0, 1), ("own", 1, 0), ("bring", 0, 0, 0), ("bring", 0, 0, 1),
    ("own", 1, 1), ("embed",), ("pass_on", 0, 0, 0), ("bring", 1, 0, 0), ("bring", 0, 1, 0),
    ("embed",), ("pass_on", 0, 0, 1), ("bring", 0, 1, 1), ("bring", 1, 0, 1),
    ("bring", 0, 2, 0), ("give", 0), ("bring", 0, 2, 1), ("give", 1), ("pass_on", 0, 1, 1),
    ("embed",), ("pass_on", 0, 1, 0), ("bring", 1, 2, 1), ("close", 0, 0), ("bring", 1, 2, 0),
    ("embed",), ("own", 2, 1), ("pass_on", 0, 2, 0), ("pass_on", 0, 2, 1), ("bring", 1, 1, 0),
    ("pass_on", 1, 2, 1), ("own", 2, 0), ("embed",), ("pass_on", 1, 2, 0), ("close", 0, 1),
    ("fetch", 2, 0, 1), ("bring", 1, 1, 1), ("embed",), ("pass_on", 1, 0, 0), ("close", 0, 2),
    ("fetch", 2, 1, 0), ("pass_on", 1, 0, 1), ("fetch", 2, 0, 0), ("all", 0),
    ("pass_on", 1, 1, 0), ("fetch", 2, 1, 1), ("qkv",), ("qkv",), ("pass_on", 1, 1, 1),
    ("qkv",), ("close", 1, 2), ("fetch", 2, 2, 1), ("close", 1, 0), ("qkv",), ("qkv",),
    ("qkv",), ("close", 1, 1), ("fetch", 2, 2, 0), ("all", 1),
)


class Gather:
    def __init__(self, place, index, full, sems, by_rows=False):
        self.dp, self.wide, self.planes, self.plane, self.core = place
        self.index = index
        self.full = full
        self.send, self.recv = sems
        self.rows = full.shape[0] // (2 * self.planes)
        self.columns = full.shape[1] // 8
        self.by_rows = by_rows
        d = self.dp
        self.across = d + 1 - 2 * lax.rem(d, 2)
        self.beyond = lax.rem(d + 2, 4)

    def alpha(self, d):
        return d

    def beta(self, d):
        return 4 + 2 * lax.rem(d, 2) + d // 2

    def pair(self, slot):
        return slot - lax.rem(slot, 2)

    def shard(self, plane, core, slot=None, count=1, array=None):
        full = self.full if array is None else array
        first = pl.multiple_of((2 * plane + core) * self.rows, self.rows)
        if slot is None:
            return full.at[pl.ds(first, self.rows)]
        if self.by_rows:
            step = self.rows // 8
            return full.at[pl.ds(pl.multiple_of(first + slot * step, step), count * step)]
        column = pl.multiple_of(slot * self.columns, self.columns)
        return full.at[pl.ds(first, self.rows), pl.ds(column, count * self.columns)]

    def copy(self, ref, send, recv, device):
        return pltpu.make_async_remote_copy(
            ref,
            ref,
            self.send.at[self.index, send],
            self.recv.at[self.index, recv],
            device_id=device,
            device_id_type=MESH,
        )

    def device(self, plane):
        return (self.dp, 2 * plane + self.core)

    def nearest(self, k):
        n = self.planes
        low = 1 - self.plane // (n // 2)
        edge = low * self.plane + (1 - low) * (n - 1 - self.plane)
        other = k + 1 - (edge - k + n - 1) // n
        return low * other + (1 - low) * (n - 1 - other)

    def along_copies(self, plane, parts=(0, 1)):
        n = self.planes
        up = (plane <= self.plane) & (self.plane < n - 1)
        down = (plane >= self.plane) & (self.plane > 0)
        for part in parts:
            slot = (self.alpha(self.dp), self.beta(self.dp))[part]
            ref = self.shard(plane, self.core, slot)
            sem = 2 * plane + part
            for go, sent, target in (
                (up, sem, lax.rem(self.plane + 1, n)),
                (down, 2 * n + sem, lax.rem(self.plane + n - 1, n)),
            ):
                yield go, self.copy(ref, sent, sem, self.device(target))

    def along(self, plane, parts=(0, 1)):
        for go, copy in self.along_copies(plane, parts):
            pl.when(go)(copy.start)

    def wait_along(self, plane, parts=(0, 1)):
        for part in parts:
            slot = (self.alpha(self.dp), self.beta(self.dp))[part]
            ref = self.shard(plane, self.core, slot)
            sem = 2 * plane + part
            self.copy(ref, sem, sem, self.device(plane)).wait_recv()

    def exchange_copies(self, plane):
        for part, (slot, d) in enumerate(
            ((self.alpha(self.dp), self.across), (self.beta(self.dp), self.beyond))
        ):
            sem = 4 * self.planes + 2 * plane + part
            yield self.copy(self.shard(plane, self.core, slot), sem, sem, (d, self.wide))

    def exchange(self, plane):
        for copy in self.exchange_copies(plane):
            copy.start()

    def wait_one_exchange(self, plane, part):
        d = (self.across, self.beyond)[part]
        slot = (self.alpha, self.beta)[part](d)
        sem = 4 * self.planes + 2 * plane + part
        self.copy(self.shard(plane, self.core, slot), sem, sem, (d, self.wide)).wait_recv()

    def pair_copies(self, plane):
        for part, (slot, d) in enumerate(
            ((self.alpha(self.dp), self.beyond), (self.beta(self.dp), self.across))
        ):
            sem = 6 * self.planes + 2 * plane + part
            ref = self.shard(plane, self.core, self.pair(slot), 2)
            yield self.copy(ref, sem, sem, (d, self.wide))

    def wait_pairs(self, plane):
        for part, (slot, d) in enumerate(
            ((self.alpha(self.beyond), self.beyond), (self.beta(self.across), self.across))
        ):
            sem = 6 * self.planes + 2 * plane + part
            ref = self.shard(plane, self.core, self.pair(slot), 2)
            self.copy(ref, sem, sem, (d, self.wide)).wait_recv()

    def other_core(self):
        return (self.dp, 2 * self.plane + 1 - self.core)

    def give_copy(self, plane):
        sem = 8 * self.planes + plane
        return self.copy(self.shard(plane, self.core), sem, sem, self.other_core())

    def give(self, plane):
        self.give_copy(plane).start()

    def wait_given(self, plane):
        sem = 8 * self.planes + plane
        self.copy(self.shard(plane, 1 - self.core), sem, sem, self.other_core()).wait_recv()

    def wait_all_given(self):
        for plane in range(self.planes):
            self.wait_given(plane)

    def fetch(self, k, part):
        plane = self.nearest(k)
        self.wait_along(plane, (part,))
        self.along(plane, (part,))

    def bring(self, k, part):
        self.fetch(k, part)
        list(self.exchange_copies(self.nearest(k)))[part].start()

    def pass_on(self, k, part):
        plane = self.nearest(k)
        self.wait_one_exchange(plane, part)
        list(self.pair_copies(plane))[part].start()

    def close(self, k):
        plane = self.nearest(k)
        self.wait_pairs(plane)
        self.give(plane)

    def wait_fetched(self):
        for k in range(self.planes):
            plane = self.plane if k == self.planes - 1 else self.nearest(k)
            for go, copy in self.along_copies(plane):
                pl.when(go)(copy.wait_send)

    def wait_passed(self):
        self.give_copy(self.plane).wait_send()
        for k in range(self.planes - 1):
            plane = self.nearest(k)
            for copy in self.exchange_copies(plane):
                copy.wait_send()
            for copy in self.pair_copies(plane):
                copy.wait_send()
            self.give_copy(plane).wait_send()

    def greet(self, planes=True):
        barrier = pltpu.get_barrier_semaphore()
        peers = [(self.across, self.wide), (self.beyond, self.wide), self.other_core()]
        if planes:
            peers += [
                self.device(lax.rem(self.plane + step, self.planes))
                for step in range(1, self.planes)
            ]
        for device in peers:
            pl.semaphore_signal(barrier, inc=1, device_id=device, device_id_type=MESH)
        return barrier, len(peers)

    def fetched(self, k, part, array=None):
        slot = (self.alpha, self.beta)[part](self.dp)
        return self.shard(self.nearest(k), self.core, slot, 1, array)

    @staticmethod
    def semaphores(planes):
        return 9 * planes


def gather_embed_kernel(
    planes,
    slots,
    groups,
    pos_table,
    prompts,
    gains,
    pos_index_t,
    tokens_in,
    own_qkv,
    own_out,
    own_up,
    own_down,
    hidden_out,
    qkv_out,
    full_qkv,
    full_out,
    full_up,
    part_down,
    table,
    tokens,
    pos_index,
    hidden,
    normed,
    qkv,
    first_full,
    second_full,
    third_full,
    send,
    recv,
    local,
):
    d = lax.axis_index("dp")
    w = lax.axis_index("wide")
    place = (d, w, planes, w // 2, lax.rem(w, 2))
    first = Gather(place, 0, first_full, (send, recv))
    second = Gather(place, 1, second_full, (send, recv))
    third = Gather(place, 2, third_full, (send, recv), by_rows=True)
    others = planes - 1
    qkv_columns = own_qkv.shape[1]
    barrier, greeted = first.greet()
    mine = pl.ds(pl.multiple_of(w * first.rows, first.rows), first.rows)
    loads = [
        pltpu.make_async_copy(own_qkv, first_full.at[mine, :qkv_columns], local.at[0]),
        pltpu.make_async_copy(own_out, first_full.at[mine, qkv_columns:], local.at[1]),
        pltpu.make_async_copy(own_up, second_full.at[mine], local.at[2]),
        pltpu.make_async_copy(own_down, third.shard(third.plane, third.core), local.at[3]),
        pltpu.make_async_copy(tokens_in, tokens, local.at[4]),
    ]
    for copy in loads:
        copy.start()
    fill_table(table, pos_table, prompts)
    columns = jnp.concatenate([pos_index_t[...].astype(F32)] * 4, 0).T
    pos_index[...] = columns.astype(jnp.int32)
    for copy in loads[:4]:
        copy.wait()
    pl.semaphore_wait(barrier, greeted)

    rows = tokens.shape[0]
    tiles = ORDER.count(("embed",))
    tile = rows // tiles
    outgoing = []

    def leave(source, target):
        copy = pltpu.make_async_copy(source, target, local.at[7 + len(outgoing)])
        copy.start()
        outgoing.append(copy)

    def embed_tile(index):
        part = slice(index * tile, (index + 1) * tile)
        value = embedded(groups, slots, index * tile, tokens[part], pos_index[part], table)
        hidden[part] = value
        leave(hidden.at[part], hidden_out.at[part])
        normal, _ = norm_parts(value)
        normed[part] = (normal * gains[0:1]).astype(BF)

    def qkv_tile(index):
        part = slice(index * tile, (index + 1) * tile)
        value = normed[part]

        def half(number, done):
            columns = pl.ds(pl.multiple_of(number * qkv_columns // 2, LANES), qkv_columns // 2)
            qkv[part, columns] = dot(value, first_full[:, columns]).astype(BF)
            return done

        lax.fori_loop(0, 2, half, 0)
        leave(qkv.at[part], qkv_out.at[part])

    gathers = (first, second, third)
    embeds, qkvs = iter(range(tiles)), iter(range(tiles))
    leave(second.shard(second.plane, second.core), second.shard(second.plane, second.core, array=full_up))
    for name, *where in ORDER:
        if name == "embed":
            index = next(embeds)
            if index == 0:
                loads[4].wait()
            embed_tile(index)
            continue
        if name == "qkv":
            qkv_tile(next(qkvs))
            continue
        gather, place = gathers[where[0]], where[1:]
        if name == "own":
            gather.along(gather.plane, place)
        elif name == "give":
            gather.give(gather.plane)
        elif name == "bring":
            gather.bring(*place)
        elif name == "fetch":
            gather.fetch(*place)
            leave(gather.fetched(*place), gather.fetched(*place, part_down))
        elif name == "pass_on":
            gather.pass_on(*place)
        elif name == "close":
            gather.close(*place)
            if gather is second:
                plane = second.nearest(*place)
                leave(second.shard(plane, second.core), second.shard(plane, second.core, array=full_up))
        elif gather is first:
            first.wait_all_given()
            leave(first_full.at[:, :qkv_columns], full_qkv)
            leave(first_full.at[:, qkv_columns:], full_out)
        else:
            for k in range(planes):
                plane = second.plane if k == 0 else second.nearest(k - 1)
                second.wait_given(plane)
                core = 1 - second.core
                leave(second.shard(plane, core), second.shard(plane, core, array=full_up))
    first.wait_fetched()
    second.wait_fetched()
    third.wait_fetched()
    first.wait_passed()
    second.wait_passed()
    for copy in outgoing:
        copy.wait()


def can_gather(axes, w_qkv, w_out, w_up, w_down):
    return (
        axes["dp"] == 4
        and axes["wide"] == 8
        and w_qkv.shape[0] % 16 == 0
        and w_down.shape[0] % (8 * 16) == 0
        and w_up.shape[1] % (8 * LANES) == 0
        and (w_qkv.shape[1] + w_out.shape[1]) % (8 * LANES) == 0
    )


def gather_embed(
    axes, size_group, tokens, pos_index, pos_table, prompts, gains, w_qkv, w_out, w_up, w_down
):
    rows, width = tokens.shape
    wide = axes["wide"]
    planes = wide // 2
    depth = w_qkv.shape[0] * wide
    inner_width = w_up.shape[1]
    vmem = pl.BlockSpec(memory_space=pltpu.VMEM)
    hbm = pl.BlockSpec(memory_space=pltpu.HBM)
    dma = pltpu.SemaphoreType.DMA
    count = Gather.semaphores(planes)
    first_columns = w_qkv.shape[1] + w_out.shape[1]
    return pl.pallas_call(
        functools.partial(gather_embed_kernel, planes, size_group.shape[0]),
        in_specs=[pl.BlockSpec(memory_space=pltpu.SMEM)] + [vmem] * 4 + [hbm] * 5,
        out_specs=[hbm] * 6,
        out_shape=[
            jax.ShapeDtypeStruct((rows, width), F32),
            jax.ShapeDtypeStruct((rows, w_qkv.shape[1]), BF),
            jax.ShapeDtypeStruct((depth, w_qkv.shape[1]), BF),
            jax.ShapeDtypeStruct((depth, w_out.shape[1]), BF),
            jax.ShapeDtypeStruct((depth, inner_width), BF),
            jax.ShapeDtypeStruct((inner_width, width), BF),
        ],
        scratch_shapes=[
            pltpu.VMEM((POS_ROWS + 3 * SLOT_ROWS, width), BF),
            pltpu.VMEM((rows, width), BF),
            pltpu.VMEM((rows, 8), jnp.int32),
            pltpu.VMEM((rows, width), F32),
            pltpu.VMEM((rows, width), BF),
            pltpu.VMEM((rows, w_qkv.shape[1]), BF),
            pltpu.VMEM((depth, first_columns), BF),
            pltpu.VMEM((depth, inner_width), BF),
            pltpu.VMEM((inner_width, width), BF),
            dma((3, count)),
            dma((3, count)),
            dma((7 + 2 * ORDER.count(("embed",)) + 2 + 2 * planes + 2 * (planes - 1),)),
        ],
        compiler_params=pltpu.CompilerParams(
            collective_id=0, has_side_effects=True, vmem_limit_bytes=VMEM_LIMIT
        ),
        name="gather_embed",
    )(
        size_group, pos_table, prompts, gains, pos_index.T, tokens, w_qkv, w_out, w_up, w_down
    )


def each_image(groups, slots, image):
    def body(slot, start):
        group = groups[slot]
        length = image_length(group)
        for size in range(3):
            pl.when(group == size)(functools.partial(image, size, start, length, slot))
        return start + length

    lax.fori_loop(0, slots, body, jnp.int32(0))


def window(count, rows, start, length):
    first = jnp.minimum((start // 8) * 8, rows - count)
    return pl.multiple_of(first, 8), start - first


def in_image(count, shift, length, first=0):
    row = lax.broadcasted_iota(jnp.int32, (count, LANES), 0) + first
    return (row >= shift) & (row < shift + length)


def head_lanes(head):
    lane = lax.broadcasted_iota(jnp.int32, (1, LANES), 1)
    return (lane < HEAD_DIM) if head % 2 == 0 else (lane >= HEAD_DIM)


def one_head(values, head, other):
    return jnp.where(head_lanes(head), values, other)


def marker(head):
    lane = lax.broadcasted_iota(jnp.int32, (1, LANES), 1)
    return jnp.where(lane == HEAD_DIM * (1 - head % 2), 1.0, 0.0).astype(BF)


def take(ref, rows):
    return [ref[rows, LANES * pair : LANES * (pair + 1)] for pair in range(PAIRS)]


def put(ref, rows, pair, new, inside):
    columns = slice(LANES * pair, LANES * (pair + 1))
    old = ref[rows, columns].astype(F32)
    ref[rows, columns] = jnp.where(inside, new, old).astype(BF)


def low(parts):
    return [part.astype(BF) for part in parts]


def head_rows(values, head):
    return values[HEAD_DIM * (head % 2) : HEAD_DIM * (head % 2 + 1)]


def own_quarters(values):
    count = values.shape[1] // 2
    return [values[:HEAD_DIM, :count], values[HEAD_DIM : 2 * HEAD_DIM, count:]]


def blocks_of(count):
    if count == LANES:
        return [(2 * pair, 2 * pair + 1) for pair in range(PAIRS)]
    return [(head,) for head in range(GROUP_HEADS)]


class Keys:
    def __init__(self, ref, rows, inside):
        self.pairs = take(ref, rows)
        bias = jnp.where(inside, 0.0, MASKED)
        self.bias = jnp.concatenate([bias, bias], 1)
        low_bias = bias.astype(BF)
        self.heads = [one_head(self.pairs[h // 2], h, low_bias) for h in range(GROUP_HEADS)]

    def scores(self, block, queries):
        if len(block) == 1:
            head = block[0]
            return dot(self.heads[head], one_head(queries[head // 2], head, marker(head)), NT)
        return dot(self.pairs[block[0] // 2], stacked(block, queries), NT) + self.bias


def stacked(block, parts):
    zero = jnp.zeros((1, LANES), BF)
    return jnp.concatenate([one_head(parts[h // 2], h, zero) for h in block], 0)


def attend_kernel(slots, groups, q_ref, k_ref, v_ref, out_ref, total_ref):
    out_ref[...] = jnp.zeros_like(out_ref)

    def image(size, start, length, slot):
        all_rows = out_ref.shape[0]
        span = KEY_ROWS[size]
        chunks = QUERY_CHUNKS[size]
        key_first, key_shift = window(span, all_rows, start, length)
        first, shift = window(max(span, 256), all_rows, start, length)
        key_rows = pl.ds(key_first, span)
        keys = Keys(k_ref, key_rows, in_image(span, key_shift, length))
        ones = jnp.ones((8, span), BF)
        value_t = [x.T for x in take(v_ref, key_rows)]

        def values_of(block):
            pair = value_t[block[0] // 2]
            rows = pair if len(block) == 2 else head_rows(pair, block[0])
            return jnp.concatenate([rows, ones], 0)

        for chunk, count in chunks:
            rows = pl.ds(pl.multiple_of(first + chunk, 8), count)
            query = take(q_ref, rows)
            blocks = blocks_of(count)
            scores = [keys.scores(block, query) for block in blocks]
            peaks = [jnp.max(s, axis=0, keepdims=True) * SCORE for s in scores]
            powers = [jnp.exp2(s * SCORE - m).astype(BF) for s, m in zip(scores, peaks)]
            mixed = [dot(values_of(block), e) for block, e in zip(blocks, powers)]
            parts = []
            for block, peak, value in zip(blocks, peaks, mixed):
                depth = HEAD_DIM * len(block)
                sums = value[depth : depth + 1]
                total = peak + jnp.log2(sums)
                for number, head in enumerate(block):
                    total_ref[0, GROUP_HEADS * slot + head, :, chunk : chunk + count] = total[
                        :, number * count : (number + 1) * count
                    ]
                value = value[:depth] / sums
                parts += [value] if len(block) == 1 else own_quarters(value)
            inside = in_image(count, shift, length, chunk)
            for pair in range(PAIRS):
                put(out_ref, rows, pair, jnp.concatenate(parts[2 * pair : 2 * pair + 2], 0).T, inside)

    each_image(groups, slots, image)


def attend(size_group, qkv):
    rows = qkv.shape[0]
    width = qkv.shape[1] // 3
    steps = width // HEAD_COLS
    slots = size_group.shape[0]
    block = lambda shift: pl.BlockSpec((rows, HEAD_COLS), lambda i, g: (0, shift * steps + i))
    return pl.pallas_call(
        functools.partial(attend_kernel, slots),
        grid_spec=pltpu.PrefetchScalarGridSpec(
            num_scalar_prefetch=1,
            grid=(steps,),
            in_specs=[block(0), block(1), block(2)],
            out_specs=[
                block(0),
                pl.BlockSpec((1, GROUP_HEADS * slots, 1, LARGE), lambda i, g: (i, 0, 0, 0)),
            ],
        ),
        out_shape=[
            jax.ShapeDtypeStruct((rows, width), BF),
            jax.ShapeDtypeStruct((steps, GROUP_HEADS * slots, 1, LARGE), F32),
        ],
        compiler_params=pltpu.CompilerParams(vmem_limit_bytes=VMEM_LIMIT),
        name="attend",
    )(size_group, qkv, qkv, qkv)


def back_through_qkv(q, k, v, w_qkv):
    width = q.shape[1]
    return (
        dot(q, w_qkv[:, :width], NT)
        + dot(k, w_qkv[:, width : 2 * width], NT)
        + dot(v, w_qkv[:, 2 * width :], NT)
    )


def attend_back_kernel(
    slots,
    groups,
    prompts,
    gains,
    w_qkv_in,
    q_ref,
    k_ref,
    v_ref,
    grad_ref,
    mixed_ref,
    total_ref,
    *refs,
):
    middles, refs = refs[:PAIRS], refs[PAIRS:]
    passed_in, dq_ref, dk_ref, dv_ref, prompt_terms, passed_out = refs[:6]
    dq_sum, dk_sum, dv_sum, middle_sum, known, w_qkv, weight_in = refs[6:]
    step = pl.program_id(0)
    weight_load = pltpu.make_async_copy(w_qkv_in, w_qkv, weight_in)

    @pl.when(step == 0)
    def _():
        weight_load.start()
        for ref in (dq_sum, dk_sum, dv_sum, middle_sum, known):
            ref[...] = jnp.zeros_like(ref)
        known[: prompts.shape[0]] = prompts[...]

    passed_out[...] = passed_in[...]

    def sum_columns(pair):
        return pl.ds(pl.multiple_of(step * HEAD_COLS + LANES * pair, LANES), LANES)

    def image(size, start, length, slot):
        all_rows = dq_ref.shape[0]
        span = KEY_ROWS[size]
        chunks = QUERY_CHUNKS[size]
        key_first, key_shift = window(span, all_rows, start, length)
        first, shift = window(max(span, 256), all_rows, start, length)
        key_rows = pl.ds(key_first, span)
        key_inside = in_image(span, key_shift, length)
        keys = Keys(k_ref, key_rows, key_inside)
        key_t = [x.T for x in keys.pairs]
        value = take(v_ref, key_rows)
        dk = [jnp.zeros((span, LANES), F32)] * PAIRS
        dv = [jnp.zeros((span, LANES), F32)] * PAIRS

        def add_prompts(total, pair, values, before):
            count = min(values.shape[0], 256)
            slot_row = lax.broadcasted_iota(jnp.int32, (SLOT_ROWS, count), 0)
            row = lax.broadcasted_iota(jnp.int32, (SLOT_ROWS, count), 1)
            chosen = (row == slot_row + before + 1) & (slot_row < PROMPTS)
            chosen = jnp.where(chosen, 1.0, 0.0).astype(BF)
            total[:, sum_columns(pair)] += dot(chosen, values[:count].astype(BF))

        for chunk, count in chunks:
            rows = pl.ds(pl.multiple_of(first + chunk, 8), count)
            inside = in_image(count, shift, length, chunk)
            query = take(q_ref, rows)
            grad32 = [jnp.where(inside, x.astype(F32), 0.0) for x in take(grad_ref, rows)]
            products = [(x * y.astype(F32)).T for x, y in zip(grad32, take(mixed_ref, rows))]
            grad = low(grad32)
            blocks = blocks_of(count)
            queries = [stacked(block, query) for block in blocks]
            grads = [stacked(block, grad) for block in blocks]
            scores = [keys.scores(block, query) for block in blocks]
            prob_grads = [dot(value[block[0] // 2], g, NT) for block, g in zip(blocks, grads)]

            def side_by_side(block, row_of):
                found = [row_of(head) for head in block]
                return found[0] if len(found) == 1 else jnp.concatenate(found, 1)

            totals = [
                side_by_side(
                    block, lambda h: total_ref[0, GROUP_HEADS * slot + h, :, chunk : chunk + count]
                )
                for block in blocks
            ]
            deltas = [
                side_by_side(
                    block,
                    lambda h: jnp.sum(head_rows(products[h // 2], h), axis=0, keepdims=True),
                )
                for block in blocks
            ]
            probs = [jnp.exp2(s * SCORE - t) for s, t in zip(scores, totals)]
            score_grads = [
                (p * (g - t)).astype(BF) for p, g, t in zip(probs, prob_grads, deltas)
            ]
            parts = []
            for block, prob, score_grad, q, g in zip(blocks, probs, score_grads, queries, grads):
                pair = block[0] // 2
                dv[pair] += dot(prob.astype(BF), g)
                dk[pair] += dot(score_grad, q)
                if len(block) == 1:
                    parts.append(dot(head_rows(key_t[pair], block[0]), score_grad))
                else:
                    parts += own_quarters(dot(key_t[pair], score_grad))
            for pair in range(PAIRS):
                dq = jnp.concatenate(parts[2 * pair : 2 * pair + 2], 0).T * SCALE
                put(dq_ref, rows, pair, dq, inside)
                if chunk == 0:
                    add_prompts(dq_sum, pair, dq, shift)
        for pair in range(PAIRS):
            put(dk_ref, key_rows, pair, dk[pair] * SCALE, key_inside)
            put(dv_ref, key_rows, pair, dv[pair], key_inside)
            add_prompts(dk_sum, pair, dk[pair] * SCALE, key_shift)
            add_prompts(dv_sum, pair, dv[pair], key_shift)
            middle_sum[:, sum_columns(pair)] += middles[pair][pl.ds(start + 1, SLOT_ROWS), :]

    each_image(groups, slots, image)

    @pl.when(step == pl.num_programs(0) - 1)
    def _():
        weight_load.wait()
        pieces = []
        for ref in (dq_sum, dk_sum, dv_sum):
            high = ref[...].astype(BF)
            pieces.append(jnp.concatenate([high, (ref[...] - high.astype(F32)).astype(BF)], 0))
        terms = back_through_qkv(*pieces, w_qkv)
        normed_grad = terms[:SLOT_ROWS] + terms[SLOT_ROWS:]
        normal, rstd = norm_parts(known[...])
        prompt_terms[...] = middle_sum[...] + norm_back(normal, rstd, gains[0:1], normed_grad)


def attend_back(
    size_group, prompts, gains, w_qkv, qkv, mixed_grad, mixed, totals, middle_grad, passed
):
    rows = qkv.shape[0]
    width = qkv.shape[1] // 3
    steps = width // HEAD_COLS
    slots = size_group.shape[0]
    block = lambda shift: pl.BlockSpec((rows, HEAD_COLS), lambda i, g: (0, shift * steps + i))
    middle = lambda pair: pl.BlockSpec((rows, LANES), lambda i, g: (0, PAIRS * i + pair))
    return pl.pallas_call(
        functools.partial(attend_back_kernel, slots),
        grid_spec=pltpu.PrefetchScalarGridSpec(
            num_scalar_prefetch=1,
            grid=(steps,),
            in_specs=[
                pl.BlockSpec(prompts.shape, lambda i, g: (0, 0)),
                pl.BlockSpec(gains.shape, lambda i, g: (0, 0)),
                pl.BlockSpec(memory_space=pltpu.HBM),
                block(0),
                block(1),
                block(2),
                block(0),
                block(0),
                pl.BlockSpec((1, GROUP_HEADS * slots, 1, LARGE), lambda i, g: (i, 0, 0, 0)),
            ]
            + [middle(pair) for pair in range(PAIRS)]
            + [block(0)],
            out_specs=[block(0)] * 3
            + [pl.BlockSpec((SLOT_ROWS, width), lambda i, g: (0, 0)), block(0)],
            scratch_shapes=[pltpu.VMEM((SLOT_ROWS, width), F32)] * 5
            + [pltpu.VMEM(w_qkv.shape, BF), pltpu.SemaphoreType.DMA],
        ),
        out_shape=[jax.ShapeDtypeStruct((rows, width), BF)] * 3
        + [
            jax.ShapeDtypeStruct((SLOT_ROWS, width), F32),
            jax.ShapeDtypeStruct((rows, width), BF),
        ],
        compiler_params=pltpu.CompilerParams(vmem_limit_bytes=VMEM_LIMIT),
        name="attend_back",
    )(
        size_group,
        prompts,
        gains,
        w_qkv,
        qkv,
        qkv,
        qkv,
        mixed_grad,
        mixed,
        totals,
        *[middle_grad] * PAIRS,
        passed,
    )


def feed_kernel(
    slots,
    chunk,
    groups,
    hidden,
    mixed,
    cotangent,
    gains,
    w_out,
    w_up,
    w_down,
    out_ref,
    middle_grad_ref,
    mixed_grad_ref,
):
    tile = hidden.shape[0]
    inner_width = w_up.shape[1]
    rows = pl.program_id(0) * tile + lax.broadcasted_iota(jnp.int32, (tile, 1), 0)
    live = rows < total_length(groups, slots)
    out_grad = jnp.where(live, cotangent[...].astype(F32), 0.0)
    out_grad_low = out_grad.astype(BF)
    middle = hidden[...] + dot(mixed[...], w_out[...])
    normal, rstd = norm_parts(middle)
    gain = gains[1:2]
    second = (normal * gain).astype(BF)
    forward = middle
    back = jnp.zeros_like(middle)
    for first in range(0, inner_width, chunk):
        part = slice(first, first + chunk)
        inner = dot(second, w_up[:, part])
        act_grad = dot(out_grad_low, w_down[part], NT)
        phi = 0.5 + 0.5 * lax.erf(inner * (0.5**0.5))
        density = jnp.exp2(inner * inner * (-0.5 * LOG2E)) * 0.3989422804014327
        activated = (inner * phi).astype(BF)
        inner_grad = (act_grad * (phi + inner * density)).astype(BF)
        forward = forward + dot(activated, w_down[part])
        back = back + dot(inner_grad, w_up[:, part], NT)
    out_ref[...] = jnp.where(live, forward, 0.0).astype(BF)
    middle_grad = out_grad + norm_back(normal, rstd, gain, back)
    middle_grad_ref[...] = middle_grad
    mixed_grad_ref[...] = dot(middle_grad.astype(BF), w_out[...], NT).astype(BF)


def feed(size_group, hidden, mixed, cotangent, gains, w_out, w_up, w_down):
    rows, width = hidden.shape
    tile = 384
    chunk = 512
    keep = lambda i, g: (0, 0)
    whole = lambda a: pl.BlockSpec(a.shape, keep, pipeline_mode=pl.Buffered(1))
    by_row = pl.BlockSpec((tile, width), lambda i, g: (i, 0))
    return pl.pallas_call(
        functools.partial(feed_kernel, size_group.shape[0], chunk),
        grid_spec=pltpu.PrefetchScalarGridSpec(
            num_scalar_prefetch=1,
            grid=(rows // tile,),
            in_specs=[by_row, by_row, by_row, whole(gains), whole(w_out), whole(w_up), whole(w_down)],
            out_specs=[by_row, by_row, by_row],
        ),
        out_shape=[
            jax.ShapeDtypeStruct((rows, width), BF),
            jax.ShapeDtypeStruct((rows, width), F32),
            jax.ShapeDtypeStruct((rows, width), BF),
        ],
        compiler_params=pltpu.CompilerParams(vmem_limit_bytes=VMEM_LIMIT),
        name="feed",
    )(size_group, hidden, mixed, cotangent, gains, w_out, w_up, w_down)


def gather_feed_kernel(
    planes,
    slots,
    chunk,
    groups,
    gains,
    hidden_in,
    mixed_in,
    cotangent_in,
    full_out,
    full_up,
    own_down,
    part_down,
    out_ref,
    middle_grad_ref,
    mixed_grad_ref,
    middle,
    mixed,
    cotangent,
    w_out,
    w_up,
    w_down,
    active,
    slope,
    send,
    recv,
    weights_in,
    rows_in,
    rows_out,
):
    d = lax.axis_index("dp")
    w = lax.axis_index("wide")
    down = Gather((d, w, planes, w // 2, lax.rem(w, 2)), 0, w_down, (send, recv), by_rows=True)
    barrier, greeted = down.greet(planes=False)
    others = planes - 1
    tiles = rows_in.shape[0]
    tile = middle.shape[0] // tiles
    inner_width = w_up.shape[1]

    def tile_rows(index):
        return pl.ds(pl.multiple_of(index * tile, tile), tile)

    def loads(index):
        part = tile_rows(index)
        return [
            pltpu.make_async_copy(hidden_in.at[part], middle.at[part], rows_in.at[index, 0]),
            pltpu.make_async_copy(mixed_in.at[part], mixed.at[part], rows_in.at[index, 1]),
            pltpu.make_async_copy(cotangent_in.at[part], cotangent.at[part], rows_in.at[index, 2]),
        ]

    def stores(index):
        part = tile_rows(index)
        return [
            pltpu.make_async_copy(middle.at[part], middle_grad_ref.at[part], rows_out.at[index, 0]),
            pltpu.make_async_copy(mixed.at[part], mixed_grad_ref.at[part], rows_out.at[index, 1]),
            pltpu.make_async_copy(cotangent.at[part], out_ref.at[part], rows_out.at[index, 2]),
        ]

    down_loads = [(own_down, down.shard(down.plane, down.core))]
    for k in range(others):
        for part in (0, 1):
            down_loads.append((down.fetched(k, part, part_down), down.fetched(k, part)))
    down_loads = [
        pltpu.make_async_copy(source, target, weights_in.at[2 + index])
        for index, (source, target) in enumerate(down_loads)
    ]
    out_load = pltpu.make_async_copy(full_out, w_out, weights_in.at[0])
    up_load = pltpu.make_async_copy(full_up, w_up, weights_in.at[1])
    for copy in down_loads:
        copy.start()
    out_load.start()
    for copy in loads(0):
        copy.start()
    up_load.start()
    for index in range(1, tiles):
        for copy in loads(index):
            copy.start()
    for copy in down_loads:
        copy.wait()
    pl.semaphore_wait(barrier, greeted)
    for k in range(others):
        down.exchange(down.nearest(k))
    down.give(down.plane)
    out_load.wait()
    gain = gains[1:2]

    def pump(step):
        @pl.when((step >= 0) & (step < others))
        def _():
            down.pass_on(step, 0)
            down.pass_on(step, 1)

        @pl.when((step >= 2) & (step < others + 2))
        def _():
            down.close(step - 2)

    def up_tile(index, carry):
        for copy in loads(index):
            copy.wait()
        part = tile_rows(index)
        value = middle[part, :] + dot(mixed[part, :], w_out[...])
        middle[part, :] = value
        normal, _ = norm_parts(value)
        second = (normal * gain).astype(BF)
        pl.when(index == 0)(up_load.wait)
        for first in range(0, inner_width, chunk):
            columns = slice(first, first + chunk)
            inner = dot(second, w_up[:, columns])
            phi = 0.5 + 0.5 * lax.erf(inner * (0.5**0.5))
            density = jnp.exp2(inner * inner * (-0.5 * LOG2E)) * 0.3989422804014327
            active[part, columns] = (inner * phi).astype(BF)
            slope[part, columns] = phi + inner * density
            if first + chunk == inner_width // 2:
                pump(2 * index)
        pump(2 * index + 1)
        return carry

    lax.fori_loop(0, tiles, up_tile, 0)
    for step in range(2 * tiles, others + 2):
        pump(step)
    down.wait_all_given()
    total = total_length(groups, slots)

    def down_tile(index, carry):
        part = tile_rows(index)
        rows = index * tile + lax.broadcasted_iota(jnp.int32, (tile, 1), 0)
        live = rows < total
        out_grad = jnp.where(live, cotangent[part, :].astype(F32), 0.0)
        out_grad_low = out_grad.astype(BF)
        value = middle[part, :]
        back = jnp.zeros_like(value)
        for first in range(0, inner_width, chunk):
            columns = slice(first, first + chunk)
            act_grad = dot(out_grad_low, w_down[columns], NT)
            inner_grad = (act_grad * slope[part, columns]).astype(BF)
            back = back + dot(inner_grad, w_up[:, columns], NT)
        forward = value + dot(active[part, :], w_down[...])
        cotangent[part, :] = jnp.where(live, forward, 0.0).astype(BF)
        normal, rstd = norm_parts(value)
        middle_grad = out_grad + norm_back(normal, rstd, gain, back)
        middle[part, :] = middle_grad
        mixed[part, :] = dot(middle_grad.astype(BF), w_out[...], NT).astype(BF)
        for copy in stores(index):
            copy.start()
        return carry

    lax.fori_loop(0, tiles, down_tile, 0)
    down.wait_passed()
    for index in range(tiles):
        for copy in stores(index):
            copy.wait()


def gather_feed(axes, size_group, hidden, mixed, cotangent, gains, w_out, w_up, w_down, part_down):
    rows, width = hidden.shape
    planes = axes["wide"] // 2
    inner_width = w_up.shape[1]
    tiles = 3
    hbm = pl.BlockSpec(memory_space=pltpu.HBM)
    dma = pltpu.SemaphoreType.DMA
    count = Gather.semaphores(planes)
    return pl.pallas_call(
        functools.partial(gather_feed_kernel, planes, size_group.shape[0], 768),
        in_specs=[
            pl.BlockSpec(memory_space=pltpu.SMEM),
            pl.BlockSpec(memory_space=pltpu.VMEM),
        ]
        + [hbm] * 7,
        out_specs=[hbm] * 3,
        out_shape=[
            jax.ShapeDtypeStruct((rows, width), BF),
            jax.ShapeDtypeStruct((rows, width), F32),
            jax.ShapeDtypeStruct((rows, width), BF),
        ],
        scratch_shapes=[
            pltpu.VMEM((rows, width), F32),
            pltpu.VMEM((rows, width), BF),
            pltpu.VMEM((rows, width), BF),
            pltpu.VMEM(w_out.shape, BF),
            pltpu.VMEM(w_up.shape, BF),
            pltpu.VMEM((inner_width, width), BF),
            pltpu.VMEM((rows, inner_width), BF),
            pltpu.VMEM((rows, inner_width), F32),
            dma((1, count)),
            dma((1, count)),
            dma((3 + 2 * (planes - 1),)),
            dma((tiles, 3)),
            dma((tiles, 3)),
        ],
        compiler_params=pltpu.CompilerParams(
            collective_id=2, has_side_effects=True, vmem_limit_bytes=VMEM_LIMIT
        ),
        name="gather_feed",
    )(size_group, gains, hidden, mixed, cotangent, w_out, w_up, w_down, part_down)


class Shared:
    def __init__(self, dp, wide, mine, near, far, result, sems):
        self.members = 2 * dp
        self.planes = wide // 2
        self.rows = mine.shape[1]
        self.d = lax.axis_index("dp")
        w = lax.axis_index("wide")
        self.plane = w // 2
        self.core = lax.rem(w, 2)
        self.member = self.d * 2 + self.core
        self.mine, self.near, self.far, self.result = mine, near, far, result
        self.send, self.near_in, self.far_in, self.last_in = sems

    def peer(self, step):
        other = lax.rem(self.member + step, self.members)
        return other, (other // 2, self.plane * 2 + lax.rem(other, 2))

    def plane_peer(self, step):
        other = lax.rem(self.plane + step, self.planes)
        return other, (self.d, other * 2 + self.core)

    def greet(self):
        barrier = pltpu.get_barrier_semaphore()
        for step in range(1, self.members):
            pl.semaphore_signal(barrier, inc=1, device_id=self.peer(step)[1], device_id_type=MESH)
        for step in range(1, self.planes):
            pl.semaphore_signal(
                barrier, inc=1, device_id=self.plane_peer(step)[1], device_id_type=MESH
            )
        return barrier, self.members + self.planes - 2

    def part(self, ref, index):
        return ref.at[pl.ds(pl.multiple_of(index * self.rows, self.rows), self.rows)]

    def copy(self, source, target, send, recv, device):
        return pltpu.make_async_remote_copy(
            source, target, send, recv, device_id=device, device_id_type=MESH
        )

    def first(self, step):
        other, device = self.peer(step)
        return self.copy(
            self.mine.at[other],
            self.near.at[step],
            self.send.at[0, step],
            self.near_in.at[step],
            device,
        )

    def second(self, step):
        mine = self.far.at[self.plane]
        device = self.plane_peer(step)[1]
        return self.copy(mine, mine, self.send.at[1, step], self.far_in.at[step], device)

    def third(self, step):
        mine = self.part(self.result, self.member)
        device = self.peer(step)[1]
        return self.copy(mine, mine, self.send.at[2, step], self.last_in.at[step], device)

    def start_first(self):
        for step in range(1, self.members):
            self.first(step).start()
        self.near[0] = self.mine[self.member]

    def start_second(self):
        for step in range(1, self.members):
            self.first(step).wait_recv()
        total = jnp.zeros(self.near.shape[1:], F32)
        for index in range(self.members):
            place = lax.rem(self.member - index + self.members, self.members)
            total = total + self.near[place].astype(F32)
        self.far[self.plane] = total.astype(BF)
        for step in range(1, self.planes):
            self.second(step).start()

    def start_third(self):
        for step in range(1, self.planes):
            self.second(step).wait_recv()
        total = jnp.zeros(self.near.shape[1:], F32)
        for index in range(self.planes):
            total = total + self.far[index].astype(F32)
        self.part(self.result, self.member)[...] = total
        for step in range(1, self.members):
            self.third(step).start()

    def end(self):
        for step in range(1, self.members):
            self.third(step).wait_recv()
        for step in range(1, self.members):
            self.first(step).wait_send()
            self.third(step).wait_send()
        for step in range(1, self.planes):
            self.second(step).wait_send()


def finish_kernel(
    dp,
    wide,
    slots,
    groups,
    prompts,
    gains,
    prompt_terms,
    hidden_in,
    middle_grad_in,
    dq_in,
    dk_in,
    dv_in,
    w_qkv_in,
    input_grad_out,
    prompt_grad,
    penalty,
    hidden,
    middle_grad,
    dq,
    dk,
    dv,
    w_qkv,
    input_grad,
    mine,
    near,
    far,
    result,
    send,
    near_in,
    far_in,
    last_in,
    weight_in,
    rows_in,
    rows_out,
):
    shared = Shared(dp, wide, mine, near, far, result, (send, near_in, far_in, last_in))
    barrier, greeted = shared.greet()
    tiles = rows_in.shape[0]
    width = hidden.shape[1]
    tile = hidden.shape[0] // tiles
    weight_load = pltpu.make_async_copy(w_qkv_in, w_qkv, weight_in)
    weight_load.start()

    def tile_rows(index):
        return pl.ds(pl.multiple_of(index * tile, tile), tile)

    def loads(index):
        part = tile_rows(index)
        pairs = (
            (dq_in, dq),
            (dk_in, dk),
            (dv_in, dv),
            (hidden_in, hidden),
            (middle_grad_in, middle_grad),
        )
        return [
            pltpu.make_async_copy(source.at[part], target.at[part], rows_in.at[index, number])
            for number, (source, target) in enumerate(pairs)
        ]

    for index in range(tiles):
        for copy in loads(index):
            copy.start()

    slot_row = lax.broadcasted_iota(jnp.int32, (SLOT_ROWS, 1), 0)
    shifted = total_length(groups, slots) + lax.broadcasted_iota(jnp.int32, (1, width), 1)
    shares = jnp.zeros((1, width), F32)
    for least in range(width, hidden.shape[0] + width, width):
        shares = shares + jnp.where(shifted >= least, 1.0, 0.0)
    terms = jnp.where(slot_row < PROMPTS, prompt_terms[...], jnp.where(slot_row == PROMPTS, shares, 0.0))
    for member in range(mine.shape[0]):
        mine[member] = terms[member * mine.shape[1] : (member + 1) * mine.shape[1]].astype(BF)
    pl.semaphore_wait(barrier, greeted)
    shared.start_first()
    weight_load.wait()

    def store(index):
        part = tile_rows(index)
        return pltpu.make_async_copy(
            input_grad.at[part], input_grad_out.at[part], rows_out.at[index]
        )

    def row_tile(index, carry):
        for copy in loads(index):
            copy.wait()
        part = tile_rows(index)
        normal, rstd = norm_parts(hidden[part, :])
        normed_grad = back_through_qkv(dq[part, :], dk[part, :], dv[part, :], w_qkv)
        hidden_grad = middle_grad[part, :] + norm_back(normal, rstd, gains[0:1], normed_grad)
        prompt_slot, live = row_places(groups, slots, index * tile, tile)
        input_grad[part, :] = jnp.where(live & (prompt_slot < 0), hidden_grad, 0.0).astype(BF)
        store(index).start()
        pl.when(index == 0)(shared.start_second)
        pl.when(index == 1)(shared.start_third)
        return carry

    lax.fori_loop(0, tiles, row_tile, 0)
    shared.end()
    given = prompts[...]
    size = given.shape[0] * given.shape[1]
    count = jnp.sum(result[PROMPTS : PROMPTS + 1], axis=1, keepdims=True)
    prompt_grad[...] = result[:PROMPTS] + (2.0 * PENALTY_RATE / size) * count * given
    square = jnp.sum(jnp.sum(given * given, axis=1, keepdims=True), axis=0, keepdims=True)
    penalty[...] = PENALTY_RATE * count * (square / size)
    for index in range(tiles):
        store(index).wait()


def finish(axes, size_group, prompts, gains, terms, hidden, middle_grad, dq, dk, dv, w_qkv):
    rows, width = hidden.shape
    dp, wide = axes["dp"], axes["wide"]
    members, planes = 2 * dp, wide // 2
    tiles = 3
    dma = pltpu.SemaphoreType.DMA
    vmem = pl.BlockSpec(memory_space=pltpu.VMEM)
    hbm = pl.BlockSpec(memory_space=pltpu.HBM)
    input_grad, prompt_grad, penalty = pl.pallas_call(
        functools.partial(finish_kernel, dp, wide, size_group.shape[0]),
        in_specs=[pl.BlockSpec(memory_space=pltpu.SMEM)] + [vmem] * 3 + [hbm] * 6,
        out_specs=[hbm, vmem, vmem],
        out_shape=[
            jax.ShapeDtypeStruct((rows, width), BF),
            jax.ShapeDtypeStruct(prompts.shape, F32),
            jax.ShapeDtypeStruct((1, 1), F32),
        ],
        scratch_shapes=[
            pltpu.VMEM((rows, width), F32),
            pltpu.VMEM((rows, width), F32),
            pltpu.VMEM((rows, width), BF),
            pltpu.VMEM((rows, width), BF),
            pltpu.VMEM((rows, width), BF),
            pltpu.VMEM(w_qkv.shape, BF),
            pltpu.VMEM((rows, width), BF),
            pltpu.VMEM((members, SLOT_ROWS // members, width), BF),
            pltpu.VMEM((members, SLOT_ROWS // members, width), BF),
            pltpu.VMEM((planes, SLOT_ROWS // members, width), BF),
            pltpu.VMEM((SLOT_ROWS, width), F32),
            dma((3, max(members, planes))),
            dma((members,)),
            dma((planes,)),
            dma((members,)),
            dma,
            dma((tiles, 5)),
            dma((tiles,)),
        ],
        compiler_params=pltpu.CompilerParams(
            collective_id=1, has_side_effects=True, vmem_limit_bytes=VMEM_LIMIT
        ),
        name="finish",
    )(size_group, prompts, gains, terms, hidden, middle_grad, dq, dk, dv, w_qkv)
    return input_grad, prompt_grad, penalty[0, 0]


def shards(
    axes,
    tokens,
    pos_index,
    size_group,
    pos_table,
    prompts,
    norm_gains,
    w_qkv,
    w_out,
    w_up,
    w_down,
    cotangent,
):
    if can_gather(axes, w_qkv, w_out, w_up, w_down):
        hidden, qkv, full_qkv, full_out, full_up, part_down = gather_embed(
            axes,
            size_group,
            tokens,
            pos_index,
            pos_table,
            prompts,
            norm_gains,
            w_qkv,
            w_out,
            w_up,
            w_down,
        )
        mixed, totals = attend(size_group, qkv)
        outputs, middle_grad, mixed_grad = gather_feed(
            axes,
            size_group,
            hidden,
            mixed,
            cotangent,
            norm_gains,
            full_out,
            full_up,
            w_down,
            part_down,
        )
    else:
        full_qkv = lax.all_gather(w_qkv, "wide", axis=0, tiled=True)
        full_out = lax.all_gather(w_out, "wide", axis=0, tiled=True)
        full_up = lax.all_gather(w_up, "wide", axis=0, tiled=True)
        full_down = lax.all_gather(w_down, "wide", axis=0, tiled=True)
        hidden, qkv = embed(size_group, tokens, pos_index, pos_table, prompts, norm_gains, full_qkv)
        mixed, totals = attend(size_group, qkv)
        outputs, middle_grad, mixed_grad = feed(
            size_group, hidden, mixed, cotangent, norm_gains, full_out, full_up, full_down
        )
    dq, dk, dv, terms, outputs = attend_back(
        size_group,
        prompts,
        norm_gains,
        full_qkv,
        qkv,
        mixed_grad,
        mixed,
        totals,
        middle_grad,
        outputs,
    )
    input_grad, prompt_grad, penalty = finish(
        axes, size_group, prompts, norm_gains, terms, hidden, middle_grad, dq, dk, dv, full_qkv
    )
    return (outputs, input_grad, prompt_grad, penalty)


def solution(mesh):
    return jax.shard_map(
        functools.partial(shards, dict(mesh.shape)),
        mesh=mesh,
        in_specs=(
            P(("dp", "wide"), None),
            P(("dp", "wide"), None),
            P(("dp", "wide")),
            P(),
            P(),
            P(),
            P("wide", None),
            P("wide", None),
            P("wide", None),
            P("wide", None),
            P(("dp", "wide"), None),
        ),
        out_specs=(P(("dp", "wide"), None), P(("dp", "wide"), None), P(), P()),
        check_vma=False,
    )
```

```python
import functools

import jax
import jax.numpy as jnp
from jax import lax
from jax.experimental import pallas as pl
from jax.experimental.pallas import tpu as pltpu
from jax.sharding import PartitionSpec as P

HEADS = 12
HEAD_DIM = 64
PROMPTS = 50
PATCH_S = 100
PATCH_M = 196
PATCH_L = 576

EPSILON = 1e-06
PENALTY_RATE = 3e-05
SCALE = HEAD_DIM**-0.5
LOG2E = 1.4426950408889634
SCORE = SCALE * LOG2E

BF = jnp.bfloat16
F32 = jnp.float32
NN = (((1,), (0,)), ((), ()))
NT = (((1,), (1,)), ((), ()))
MESH = pl.DeviceIdType.MESH

LANES = 128
HEAD_COLS = 384
PAIRS = HEAD_COLS // LANES
GROUP_HEADS = HEAD_COLS // HEAD_DIM
LARGE = 640
KEY_ROWS = (160, 256, LARGE)
QUERY_CHUNKS = (((0, 256),), ((0, 256),), ((0, 256), (256, 256), (512, 128)))
MASKED = -1e30
POS_ROWS = 256
VMEM_LIMIT = 60 << 20
SLOT_ROWS = 64


def dot(a, b, dims=NN):
    return lax.dot_general(a, b, dims, preferred_element_type=F32)


def image_length(group):
    patches = jnp.where(group == 0, PATCH_S, jnp.where(group == 1, PATCH_M, PATCH_L))
    return jnp.where(group == 3, 0, 1 + PROMPTS + patches).astype(jnp.int32)


def total_length(groups, slots):
    total = jnp.int32(0)
    for slot in range(slots):
        total = total + image_length(groups[slot])
    return total


def row_places(groups, slots, first_row, count):
    rows = first_row + lax.broadcasted_iota(jnp.int32, (count, 1), 0)
    place = rows
    start = jnp.int32(0)
    for slot in range(slots):
        length = image_length(groups[slot])
        place = jnp.where((rows >= start) & (length > 0), rows - start, place)
        start = start + length
    live = rows < start
    prompt_slot = jnp.where(live & (place >= 1) & (place <= PROMPTS), place - 1, -1)
    return prompt_slot, live


def norm_parts(values):
    centered = values - jnp.mean(values, axis=-1, keepdims=True)
    rstd = lax.rsqrt(jnp.mean(centered * centered, axis=-1, keepdims=True) + EPSILON)
    return centered * rstd, rstd


def norm_back(normal, rstd, gain, grad):
    scaled = grad * gain
    return (
        scaled
        - jnp.mean(scaled, axis=-1, keepdims=True)
        - normal * jnp.mean(scaled * normal, axis=-1, keepdims=True)
    ) * rstd


def fill_table(table, pos_table, prompts):
    table[...] = jnp.zeros_like(table)
    table[: pos_table.shape[0]] = pos_table[...]
    rest = prompts[...]
    for piece in range(3):
        part = rest.astype(BF)
        first = POS_ROWS + piece * SLOT_ROWS
        table[first : first + PROMPTS] = part
        rest = rest - part.astype(F32)


def embedded(groups, slots, first_row, tokens, pos_index, table):
    prompt_slot, _ = row_places(groups, slots, first_row, tokens.shape[0])
    is_prompt = prompt_slot >= 0
    lane = lax.broadcasted_iota(jnp.int32, (1, POS_ROWS), 1)
    left = jnp.where(is_prompt, -1, pos_index[:, 0:1])
    right = jnp.where(is_prompt, -1, pos_index[:, 1:2])
    half_hot = jnp.where(lane == left, 0.5, 0.0) + jnp.where(lane == right, 0.5, 0.0)
    slot_lane = lax.broadcasted_iota(jnp.int32, (1, 3 * SLOT_ROWS), 1)
    slot_lane = lax.rem(slot_lane, SLOT_ROWS)
    slot_hot = jnp.where(slot_lane == prompt_slot, 1.0, 0.0)
    picked = dot(half_hot.astype(BF), table[:POS_ROWS]) + dot(
        slot_hot.astype(BF), table[POS_ROWS:]
    )
    return jnp.where(is_prompt, 0.0, tokens.astype(F32)) + picked


def embed_kernel(
    slots, groups, tokens, pos_index, pos_table, prompts, gains, w_qkv, hidden_out, qkv_out, table
):
    tile = tokens.shape[0]
    step = pl.program_id(0)

    @pl.when(step == 0)
    def _():
        fill_table(table, pos_table, prompts)

    hidden = embedded(groups, slots, step * tile, tokens[...], pos_index[...], table)
    hidden_out[...] = hidden
    normal, _ = norm_parts(hidden)
    normed = (normal * gains[0:1]).astype(BF)
    qkv_out[...] = dot(normed, w_qkv[...]).astype(BF)


def embed(size_group, tokens, pos_index, pos_table, prompts, gains, w_qkv):
    rows, width = tokens.shape
    tile = 384
    keep = lambda i, g: (0, 0)
    whole = lambda a: pl.BlockSpec(a.shape, keep, pipeline_mode=pl.Buffered(1))
    by_row = lambda columns: pl.BlockSpec((tile, columns), lambda i, g: (i, 0))
    return pl.pallas_call(
        functools.partial(embed_kernel, size_group.shape[0]),
        grid_spec=pltpu.PrefetchScalarGridSpec(
            num_scalar_prefetch=1,
            grid=(rows // tile,),
            in_specs=[
                by_row(width),
                by_row(2),
                whole(pos_table),
                whole(prompts),
                whole(gains),
                whole(w_qkv),
            ],
            out_specs=[by_row(width), by_row(3 * width)],
            scratch_shapes=[pltpu.VMEM((POS_ROWS + 3 * SLOT_ROWS, width), BF)],
        ),
        out_shape=[
            jax.ShapeDtypeStruct((rows, width), F32),
            jax.ShapeDtypeStruct((rows, 3 * width), BF),
        ],
        compiler_params=pltpu.CompilerParams(vmem_limit_bytes=VMEM_LIMIT),
        name="embed",
    )(size_group, tokens, pos_index, pos_table, prompts, gains, w_qkv)


ORDER = (
    ("own", 0, 0), ("own", 0, 1), ("own", 1, 0), ("bring", 0, 0, 0), ("bring", 0, 0, 1),
    ("own", 1, 1), ("embed",), ("pass_on", 0, 0, 0), ("bring", 1, 0, 0), ("bring", 0, 1, 0),
    ("embed",), ("pass_on", 0, 0, 1), ("bring", 0, 1, 1), ("bring", 1, 0, 1),
    ("bring", 0, 2, 0), ("give", 0), ("bring", 0, 2, 1), ("give", 1), ("pass_on", 0, 1, 1),
    ("embed",), ("pass_on", 0, 1, 0), ("bring", 1, 2, 1), ("close", 0, 0), ("bring", 1, 2, 0),
    ("embed",), ("own", 2, 1), ("pass_on", 0, 2, 0), ("pass_on", 0, 2, 1), ("bring", 1, 1, 0),
    ("pass_on", 1, 2, 1), ("own", 2, 0), ("embed",), ("pass_on", 1, 2, 0), ("close", 0, 1),
    ("fetch", 2, 0, 1), ("bring", 1, 1, 1), ("embed",), ("pass_on", 1, 0, 0), ("close", 0, 2),
    ("fetch", 2, 1, 0), ("pass_on", 1, 0, 1), ("fetch", 2, 0, 0), ("all", 0),
    ("pass_on", 1, 1, 0), ("fetch", 2, 1, 1), ("qkv",), ("qkv",), ("pass_on", 1, 1, 1),
    ("qkv",), ("close", 1, 2), ("fetch", 2, 2, 1), ("close", 1, 0), ("qkv",), ("qkv",),
    ("qkv",), ("close", 1, 1), ("fetch", 2, 2, 0), ("all", 1),
)


class Gather:
    def __init__(self, place, index, full, sems, by_rows=False):
        self.dp, self.wide, self.planes, self.plane, self.core = place
        self.index = index
        self.full = full
        self.send, self.recv = sems
        self.rows = full.shape[0] // (2 * self.planes)
        self.columns = full.shape[1] // 8
        self.by_rows = by_rows
        d = self.dp
        self.across = d + 1 - 2 * lax.rem(d, 2)
        self.beyond = lax.rem(d + 2, 4)

    def alpha(self, d):
        return d

    def beta(self, d):
        return 4 + 2 * lax.rem(d, 2) + d // 2

    def pair(self, slot):
        return slot - lax.rem(slot, 2)

    def shard(self, plane, core, slot=None, count=1, array=None):
        full = self.full if array is None else array
        first = pl.multiple_of((2 * plane + core) * self.rows, self.rows)
        if slot is None:
            return full.at[pl.ds(first, self.rows)]
        if self.by_rows:
            step = self.rows // 8
            return full.at[pl.ds(pl.multiple_of(first + slot * step, step), count * step)]
        column = pl.multiple_of(slot * self.columns, self.columns)
        return full.at[pl.ds(first, self.rows), pl.ds(column, count * self.columns)]

    def copy(self, ref, send, recv, device):
        return pltpu.make_async_remote_copy(
            ref,
            ref,
            self.send.at[self.index, send],
            self.recv.at[self.index, recv],
            device_id=device,
            device_id_type=MESH,
        )

    def device(self, plane):
        return (self.dp, 2 * plane + self.core)

    def nearest(self, k):
        n = self.planes
        low = 1 - self.plane // (n // 2)
        edge = low * self.plane + (1 - low) * (n - 1 - self.plane)
        other = k + 1 - (edge - k + n - 1) // n
        return low * other + (1 - low) * (n - 1 - other)

    def along_copies(self, plane, parts=(0, 1)):
        n = self.planes
        up = (plane <= self.plane) & (self.plane < n - 1)
        down = (plane >= self.plane) & (self.plane > 0)
        for part in parts:
            slot = (self.alpha(self.dp), self.beta(self.dp))[part]
            ref = self.shard(plane, self.core, slot)
            sem = 2 * plane + part
            for go, sent, target in (
                (up, sem, lax.rem(self.plane + 1, n)),
                (down, 2 * n + sem, lax.rem(self.plane + n - 1, n)),
            ):
                yield go, self.copy(ref, sent, sem, self.device(target))

    def along(self, plane, parts=(0, 1)):
        for go, copy in self.along_copies(plane, parts):
            pl.when(go)(copy.start)

    def wait_along(self, plane, parts=(0, 1)):
        for part in parts:
            slot = (self.alpha(self.dp), self.beta(self.dp))[part]
            ref = self.shard(plane, self.core, slot)
            sem = 2 * plane + part
            self.copy(ref, sem, sem, self.device(plane)).wait_recv()

    def exchange_copies(self, plane):
        for part, (slot, d) in enumerate(
            ((self.alpha(self.dp), self.across), (self.beta(self.dp), self.beyond))
        ):
            sem = 4 * self.planes + 2 * plane + part
            yield self.copy(self.shard(plane, self.core, slot), sem, sem, (d, self.wide))

    def exchange(self, plane):
        for copy in self.exchange_copies(plane):
            copy.start()

    def wait_one_exchange(self, plane, part):
        d = (self.across, self.beyond)[part]
        slot = (self.alpha, self.beta)[part](d)
        sem = 4 * self.planes + 2 * plane + part
        self.copy(self.shard(plane, self.core, slot), sem, sem, (d, self.wide)).wait_recv()

    def pair_copies(self, plane):
        for part, (slot, d) in enumerate(
            ((self.alpha(self.dp), self.beyond), (self.beta(self.dp), self.across))
        ):
            sem = 6 * self.planes + 2 * plane + part
            ref = self.shard(plane, self.core, self.pair(slot), 2)
            yield self.copy(ref, sem, sem, (d, self.wide))

    def wait_pairs(self, plane):
        for part, (slot, d) in enumerate(
            ((self.alpha(self.beyond), self.beyond), (self.beta(self.across), self.across))
        ):
            sem = 6 * self.planes + 2 * plane + part
            ref = self.shard(plane, self.core, self.pair(slot), 2)
            self.copy(ref, sem, sem, (d, self.wide)).wait_recv()

    def other_core(self):
        return (self.dp, 2 * self.plane + 1 - self.core)

    def give_copy(self, plane):
        sem = 8 * self.planes + plane
        return self.copy(self.shard(plane, self.core), sem, sem, self.other_core())

    def give(self, plane):
        self.give_copy(plane).start()

    def wait_given(self, plane):
        sem = 8 * self.planes + plane
        self.copy(self.shard(plane, 1 - self.core), sem, sem, self.other_core()).wait_recv()

    def wait_all_given(self):
        for plane in range(self.planes):
            self.wait_given(plane)

    def fetch(self, k, part):
        plane = self.nearest(k)
        self.wait_along(plane, (part,))
        self.along(plane, (part,))

    def bring(self, k, part):
        self.fetch(k, part)
        list(self.exchange_copies(self.nearest(k)))[part].start()

    def pass_on(self, k, part):
        plane = self.nearest(k)
        self.wait_one_exchange(plane, part)
        list(self.pair_copies(plane))[part].start()

    def close(self, k):
        plane = self.nearest(k)
        self.wait_pairs(plane)
        self.give(plane)

    def wait_fetched(self):
        for k in range(self.planes):
            plane = self.plane if k == self.planes - 1 else self.nearest(k)
            for go, copy in self.along_copies(plane):
                pl.when(go)(copy.wait_send)

    def wait_passed(self):
        self.give_copy(self.plane).wait_send()
        for k in range(self.planes - 1):
            plane = self.nearest(k)
            for copy in self.exchange_copies(plane):
                copy.wait_send()
            for copy in self.pair_copies(plane):
                copy.wait_send()
            self.give_copy(plane).wait_send()

    def greet(self, planes=True):
        barrier = pltpu.get_barrier_semaphore()
        peers = [(self.across, self.wide), (self.beyond, self.wide), self.other_core()]
        if planes:
            peers += [
                self.device(lax.rem(self.plane + step, self.planes))
                for step in range(1, self.planes)
            ]
        for device in peers:
            pl.semaphore_signal(barrier, inc=1, device_id=device, device_id_type=MESH)
        return barrier, len(peers)

    def fetched(self, k, part, array=None):
        slot = (self.alpha, self.beta)[part](self.dp)
        return self.shard(self.nearest(k), self.core, slot, 1, array)

    @staticmethod
    def semaphores(planes):
        return 9 * planes


def gather_embed_kernel(
    planes,
    slots,
    groups,
    pos_table,
    prompts,
    gains,
    pos_index_t,
    tokens_in,
    own_qkv,
    own_out,
    own_up,
    own_down,
    hidden_out,
    qkv_out,
    full_qkv,
    full_out,
    full_up,
    part_down,
    table,
    tokens,
    pos_index,
    hidden,
    normed,
    qkv,
    first_full,
    second_full,
    third_full,
    send,
    recv,
    local,
):
    d = lax.axis_index("dp")
    w = lax.axis_index("wide")
    place = (d, w, planes, w // 2, lax.rem(w, 2))
    first = Gather(place, 0, first_full, (send, recv))
    second = Gather(place, 1, second_full, (send, recv))
    third = Gather(place, 2, third_full, (send, recv), by_rows=True)
    others = planes - 1
    qkv_columns = own_qkv.shape[1]
    barrier, greeted = first.greet()
    mine = pl.ds(pl.multiple_of(w * first.rows, first.rows), first.rows)
    loads = [
        pltpu.make_async_copy(own_qkv, first_full.at[mine, :qkv_columns], local.at[0]),
        pltpu.make_async_copy(own_out, first_full.at[mine, qkv_columns:], local.at[1]),
        pltpu.make_async_copy(own_up, second_full.at[mine], local.at[2]),
        pltpu.make_async_copy(own_down, third.shard(third.plane, third.core), local.at[3]),
        pltpu.make_async_copy(tokens_in, tokens, local.at[4]),
    ]
    for copy in loads:
        copy.start()
    fill_table(table, pos_table, prompts)
    columns = jnp.concatenate([pos_index_t[...].astype(F32)] * 4, 0).T
    pos_index[...] = columns.astype(jnp.int32)
    for copy in loads[:4]:
        copy.wait()
    pl.semaphore_wait(barrier, greeted)

    rows = tokens.shape[0]
    tiles = ORDER.count(("embed",))
    tile = rows // tiles
    outgoing = []

    def leave(source, target):
        copy = pltpu.make_async_copy(source, target, local.at[7 + len(outgoing)])
        copy.start()
        outgoing.append(copy)

    def embed_tile(index):
        part = slice(index * tile, (index + 1) * tile)
        value = embedded(groups, slots, index * tile, tokens[part], pos_index[part], table)
        hidden[part] = value
        leave(hidden.at[part], hidden_out.at[part])
        normal, _ = norm_parts(value)
        normed[part] = (normal * gains[0:1]).astype(BF)

    def qkv_tile(index):
        part = slice(index * tile, (index + 1) * tile)
        value = normed[part]

        def half(number, done):
            columns = pl.ds(pl.multiple_of(number * qkv_columns // 2, LANES), qkv_columns // 2)
            qkv[part, columns] = dot(value, first_full[:, columns]).astype(BF)
            return done

        lax.fori_loop(0, 2, half, 0)
        leave(qkv.at[part], qkv_out.at[part])

    gathers = (first, second, third)
    embeds, qkvs = iter(range(tiles)), iter(range(tiles))
    leave(second.shard(second.plane, second.core), second.shard(second.plane, second.core, array=full_up))
    for name, *where in ORDER:
        if name == "embed":
            index = next(embeds)
            if index == 0:
                loads[4].wait()
            embed_tile(index)
            continue
        if name == "qkv":
            qkv_tile(next(qkvs))
            continue
        gather, place = gathers[where[0]], where[1:]
        if name == "own":
            gather.along(gather.plane, place)
        elif name == "give":
            gather.give(gather.plane)
        elif name == "bring":
            gather.bring(*place)
        elif name == "fetch":
            gather.fetch(*place)
            leave(gather.fetched(*place), gather.fetched(*place, part_down))
        elif name == "pass_on":
            gather.pass_on(*place)
        elif name == "close":
            gather.close(*place)
            if gather is second:
                plane = second.nearest(*place)
                leave(second.shard(plane, second.core), second.shard(plane, second.core, array=full_up))
        elif gather is first:
            first.wait_all_given()
            leave(first_full.at[:, :qkv_columns], full_qkv)
            leave(first_full.at[:, qkv_columns:], full_out)
        else:
            for k in range(planes):
                plane = second.plane if k == 0 else second.nearest(k - 1)
                second.wait_given(plane)
                core = 1 - second.core
                leave(second.shard(plane, core), second.shard(plane, core, array=full_up))
    first.wait_fetched()
    second.wait_fetched()
    third.wait_fetched()
    first.wait_passed()
    second.wait_passed()
    for copy in outgoing:
        copy.wait()


def can_gather(axes, w_qkv, w_out, w_up, w_down):
    return (
        axes["dp"] == 4
        and axes["wide"] == 8
        and w_qkv.shape[0] % 16 == 0
        and w_down.shape[0] % (8 * 16) == 0
        and w_up.shape[1] % (8 * LANES) == 0
        and (w_qkv.shape[1] + w_out.shape[1]) % (8 * LANES) == 0
    )


def gather_embed(
    axes, size_group, tokens, pos_index, pos_table, prompts, gains, w_qkv, w_out, w_up, w_down
):
    rows, width = tokens.shape
    wide = axes["wide"]
    planes = wide // 2
    depth = w_qkv.shape[0] * wide
    inner_width = w_up.shape[1]
    vmem = pl.BlockSpec(memory_space=pltpu.VMEM)
    hbm = pl.BlockSpec(memory_space=pltpu.HBM)
    dma = pltpu.SemaphoreType.DMA
    count = Gather.semaphores(planes)
    first_columns = w_qkv.shape[1] + w_out.shape[1]
    return pl.pallas_call(
        functools.partial(gather_embed_kernel, planes, size_group.shape[0]),
        in_specs=[pl.BlockSpec(memory_space=pltpu.SMEM)] + [vmem] * 4 + [hbm] * 5,
        out_specs=[hbm] * 6,
        out_shape=[
            jax.ShapeDtypeStruct((rows, width), F32),
            jax.ShapeDtypeStruct((rows, w_qkv.shape[1]), BF),
            jax.ShapeDtypeStruct((depth, w_qkv.shape[1]), BF),
            jax.ShapeDtypeStruct((depth, w_out.shape[1]), BF),
            jax.ShapeDtypeStruct((depth, inner_width), BF),
            jax.ShapeDtypeStruct((inner_width, width), BF),
        ],
        scratch_shapes=[
            pltpu.VMEM((POS_ROWS + 3 * SLOT_ROWS, width), BF),
            pltpu.VMEM((rows, width), BF),
            pltpu.VMEM((rows, 8), jnp.int32),
            pltpu.VMEM((rows, width), F32),
            pltpu.VMEM((rows, width), BF),
            pltpu.VMEM((rows, w_qkv.shape[1]), BF),
            pltpu.VMEM((depth, first_columns), BF),
            pltpu.VMEM((depth, inner_width), BF),
            pltpu.VMEM((inner_width, width), BF),
            dma((3, count)),
            dma((3, count)),
            dma((7 + 2 * ORDER.count(("embed",)) + 2 + 2 * planes + 2 * (planes - 1),)),
        ],
        compiler_params=pltpu.CompilerParams(
            collective_id=0, has_side_effects=True, vmem_limit_bytes=VMEM_LIMIT
        ),
        name="gather_embed",
    )(
        size_group, pos_table, prompts, gains, pos_index.T, tokens, w_qkv, w_out, w_up, w_down
    )


def each_image(groups, slots, image):
    def body(slot, start):
        group = groups[slot]
        length = image_length(group)
        for size in range(3):
            pl.when(group == size)(functools.partial(image, size, start, length, slot))
        return start + length

    lax.fori_loop(0, slots, body, jnp.int32(0))


def window(count, rows, start, length):
    first = jnp.minimum((start // 8) * 8, rows - count)
    return pl.multiple_of(first, 8), start - first


def in_image(count, shift, length, first=0):
    row = lax.broadcasted_iota(jnp.int32, (count, LANES), 0) + first
    return (row >= shift) & (row < shift + length)


def head_lanes(head):
    lane = lax.broadcasted_iota(jnp.int32, (1, LANES), 1)
    return (lane < HEAD_DIM) if head % 2 == 0 else (lane >= HEAD_DIM)


def one_head(values, head, other):
    return jnp.where(head_lanes(head), values, other)


def marker(head):
    lane = lax.broadcasted_iota(jnp.int32, (1, LANES), 1)
    return jnp.where(lane == HEAD_DIM * (1 - head % 2), 1.0, 0.0).astype(BF)


def take(ref, rows):
    return [ref[rows, LANES * pair : LANES * (pair + 1)] for pair in range(PAIRS)]


def put(ref, rows, pair, new, inside):
    columns = slice(LANES * pair, LANES * (pair + 1))
    old = ref[rows, columns].astype(F32)
    ref[rows, columns] = jnp.where(inside, new, old).astype(BF)


def low(parts):
    return [part.astype(BF) for part in parts]


def head_rows(values, head):
    return values[HEAD_DIM * (head % 2) : HEAD_DIM * (head % 2 + 1)]


def own_quarters(values):
    count = values.shape[1] // 2
    return [values[:HEAD_DIM, :count], values[HEAD_DIM : 2 * HEAD_DIM, count:]]


def blocks_of(count):
    if count == LANES:
        return [(2 * pair, 2 * pair + 1) for pair in range(PAIRS)]
    return [(head,) for head in range(GROUP_HEADS)]


class Keys:
    def __init__(self, ref, rows, inside):
        self.pairs = take(ref, rows)
        bias = jnp.where(inside, 0.0, MASKED)
        self.bias = jnp.concatenate([bias, bias], 1)
        low_bias = bias.astype(BF)
        self.heads = [one_head(self.pairs[h // 2], h, low_bias) for h in range(GROUP_HEADS)]

    def scores(self, block, queries):
        if len(block) == 1:
            head = block[0]
            return dot(self.heads[head], one_head(queries[head // 2], head, marker(head)), NT)
        return dot(self.pairs[block[0] // 2], stacked(block, queries), NT) + self.bias


def stacked(block, parts):
    zero = jnp.zeros((1, LANES), BF)
    return jnp.concatenate([one_head(parts[h // 2], h, zero) for h in block], 0)


def attend_kernel(slots, groups, q_ref, k_ref, v_ref, out_ref, total_ref):
    out_ref[...] = jnp.zeros_like(out_ref)

    def image(size, start, length, slot):
        all_rows = out_ref.shape[0]
        span = KEY_ROWS[size]
        chunks = QUERY_CHUNKS[size]
        key_first, key_shift = window(span, all_rows, start, length)
        first, shift = window(max(span, 256), all_rows, start, length)
        key_rows = pl.ds(key_first, span)
        keys = Keys(k_ref, key_rows, in_image(span, key_shift, length))
        ones = jnp.ones((8, span), BF)
        value_t = [x.T for x in take(v_ref, key_rows)]

        def values_of(block):
            pair = value_t[block[0] // 2]
            rows = pair if len(block) == 2 else head_rows(pair, block[0])
            return jnp.concatenate([rows, ones], 0)

        def scores_of(chunk, count):
            rows = pl.ds(pl.multiple_of(first + chunk, 8), count)
            query = take(q_ref, rows)
            blocks = blocks_of(count)
            return rows, blocks, [keys.scores(block, query) for block in blocks]

        ahead = scores_of(*chunks[0])
        for number, (chunk, count) in enumerate(chunks):
            rows, blocks, scores = ahead
            if number + 1 < len(chunks):
                ahead = scores_of(*chunks[number + 1])
            peaks = [jnp.max(s, axis=0, keepdims=True) * SCORE for s in scores]
            powers = [jnp.exp2(s * SCORE - m).astype(BF) for s, m in zip(scores, peaks)]
            mixed = [dot(values_of(block), e) for block, e in zip(blocks, powers)]
            parts = []
            for block, peak, value in zip(blocks, peaks, mixed):
                depth = HEAD_DIM * len(block)
                sums = value[depth : depth + 1]
                total = peak + jnp.log2(sums)
                for place, head in enumerate(block):
                    total_ref[0, GROUP_HEADS * slot + head, :, chunk : chunk + count] = total[
                        :, place * count : (place + 1) * count
                    ]
                value = value[:depth] / sums
                parts += [value] if len(block) == 1 else own_quarters(value)
            inside = in_image(count, shift, length, chunk)
            for pair in range(PAIRS):
                put(out_ref, rows, pair, jnp.concatenate(parts[2 * pair : 2 * pair + 2], 0).T, inside)

    each_image(groups, slots, image)


def attend(size_group, qkv):
    rows = qkv.shape[0]
    width = qkv.shape[1] // 3
    steps = width // HEAD_COLS
    slots = size_group.shape[0]
    block = lambda shift: pl.BlockSpec((rows, HEAD_COLS), lambda i, g: (0, shift * steps + i))
    return pl.pallas_call(
        functools.partial(attend_kernel, slots),
        grid_spec=pltpu.PrefetchScalarGridSpec(
            num_scalar_prefetch=1,
            grid=(steps,),
            in_specs=[block(0), block(1), block(2)],
            out_specs=[
                block(0),
                pl.BlockSpec((1, GROUP_HEADS * slots, 1, LARGE), lambda i, g: (i, 0, 0, 0)),
            ],
        ),
        out_shape=[
            jax.ShapeDtypeStruct((rows, width), BF),
            jax.ShapeDtypeStruct((steps, GROUP_HEADS * slots, 1, LARGE), F32),
        ],
        compiler_params=pltpu.CompilerParams(vmem_limit_bytes=VMEM_LIMIT),
        name="attend",
    )(size_group, qkv, qkv, qkv)


def back_through_qkv(q, k, v, w_qkv):
    width = q.shape[1]
    return (
        dot(q, w_qkv[:, :width], NT)
        + dot(k, w_qkv[:, width : 2 * width], NT)
        + dot(v, w_qkv[:, 2 * width :], NT)
    )


def attend_back_kernel(
    slots,
    groups,
    prompts,
    gains,
    w_qkv_in,
    q_ref,
    k_ref,
    v_ref,
    grad_ref,
    mixed_ref,
    total_ref,
    *refs,
):
    middles, refs = refs[:PAIRS], refs[PAIRS:]
    passed_in, dq_ref, dk_ref, dv_ref, prompt_terms, passed_out = refs[:6]
    dq_sum, dk_sum, dv_sum, middle_sum, known, w_qkv, weight_in = refs[6:]
    step = pl.program_id(0)
    weight_load = pltpu.make_async_copy(w_qkv_in, w_qkv, weight_in)

    @pl.when(step == 0)
    def _():
        weight_load.start()
        for ref in (dq_sum, dk_sum, dv_sum, middle_sum, known):
            ref[...] = jnp.zeros_like(ref)
        known[: prompts.shape[0]] = prompts[...]

    passed_out[...] = passed_in[...]

    def sum_columns(pair):
        return pl.ds(pl.multiple_of(step * HEAD_COLS + LANES * pair, LANES), LANES)

    def image(size, start, length, slot):
        all_rows = dq_ref.shape[0]
        span = KEY_ROWS[size]
        chunks = QUERY_CHUNKS[size]
        key_first, key_shift = window(span, all_rows, start, length)
        first, shift = window(max(span, 256), all_rows, start, length)
        key_rows = pl.ds(key_first, span)
        key_inside = in_image(span, key_shift, length)
        keys = Keys(k_ref, key_rows, key_inside)
        key_t = [x.T for x in keys.pairs]
        value = take(v_ref, key_rows)
        dk = [jnp.zeros((span, LANES), F32)] * PAIRS
        dv = [jnp.zeros((span, LANES), F32)] * PAIRS

        def add_prompts(total, pair, values, before):
            count = min(values.shape[0], 256)
            slot_row = lax.broadcasted_iota(jnp.int32, (SLOT_ROWS, count), 0)
            row = lax.broadcasted_iota(jnp.int32, (SLOT_ROWS, count), 1)
            chosen = (row == slot_row + before + 1) & (slot_row < PROMPTS)
            chosen = jnp.where(chosen, 1.0, 0.0).astype(BF)
            total[:, sum_columns(pair)] += dot(chosen, values[:count].astype(BF))

        for chunk, count in chunks:
            rows = pl.ds(pl.multiple_of(first + chunk, 8), count)
            inside = in_image(count, shift, length, chunk)
            query = take(q_ref, rows)
            grad32 = [jnp.where(inside, x.astype(F32), 0.0) for x in take(grad_ref, rows)]
            products = [(x * y.astype(F32)).T for x, y in zip(grad32, take(mixed_ref, rows))]
            grad = low(grad32)
            blocks = blocks_of(count)
            queries = [stacked(block, query) for block in blocks]
            grads = [stacked(block, grad) for block in blocks]
            scores = [keys.scores(block, query) for block in blocks]
            prob_grads = [dot(value[block[0] // 2], g, NT) for block, g in zip(blocks, grads)]

            def side_by_side(block, row_of):
                found = [row_of(head) for head in block]
                return found[0] if len(found) == 1 else jnp.concatenate(found, 1)

            totals = [
                side_by_side(
                    block, lambda h: total_ref[0, GROUP_HEADS * slot + h, :, chunk : chunk + count]
                )
                for block in blocks
            ]
            deltas = [
                side_by_side(
                    block,
                    lambda h: jnp.sum(head_rows(products[h // 2], h), axis=0, keepdims=True),
                )
                for block in blocks
            ]
            probs = [jnp.exp2(s * SCORE - t) for s, t in zip(scores, totals)]
            score_grads = [
                (p * (g - t)).astype(BF) for p, g, t in zip(probs, prob_grads, deltas)
            ]
            parts = []
            for block, prob, score_grad, q, g in zip(blocks, probs, score_grads, queries, grads):
                pair = block[0] // 2
                dv[pair] += dot(prob.astype(BF), g)
                dk[pair] += dot(score_grad, q)
                if len(block) == 1:
                    parts.append(dot(head_rows(key_t[pair], block[0]), score_grad))
                else:
                    parts += own_quarters(dot(key_t[pair], score_grad))
            for pair in range(PAIRS):
                dq = jnp.concatenate(parts[2 * pair : 2 * pair + 2], 0).T * SCALE
                put(dq_ref, rows, pair, dq, inside)
                if chunk == 0:
                    add_prompts(dq_sum, pair, dq, shift)
        for pair in range(PAIRS):
            put(dk_ref, key_rows, pair, dk[pair] * SCALE, key_inside)
            put(dv_ref, key_rows, pair, dv[pair], key_inside)
            add_prompts(dk_sum, pair, dk[pair] * SCALE, key_shift)
            add_prompts(dv_sum, pair, dv[pair], key_shift)
            middle_sum[:, sum_columns(pair)] += middles[pair][pl.ds(start + 1, SLOT_ROWS), :]

    each_image(groups, slots, image)

    @pl.when(step == pl.num_programs(0) - 1)
    def _():
        weight_load.wait()
        pieces = []
        for ref in (dq_sum, dk_sum, dv_sum):
            high = ref[...].astype(BF)
            pieces.append(jnp.concatenate([high, (ref[...] - high.astype(F32)).astype(BF)], 0))
        terms = back_through_qkv(*pieces, w_qkv)
        normed_grad = terms[:SLOT_ROWS] + terms[SLOT_ROWS:]
        normal, rstd = norm_parts(known[...])
        prompt_terms[...] = middle_sum[...] + norm_back(normal, rstd, gains[0:1], normed_grad)


def attend_back(
    size_group, prompts, gains, w_qkv, qkv, mixed_grad, mixed, totals, middle_grad, passed
):
    rows = qkv.shape[0]
    width = qkv.shape[1] // 3
    steps = width // HEAD_COLS
    slots = size_group.shape[0]
    block = lambda shift: pl.BlockSpec((rows, HEAD_COLS), lambda i, g: (0, shift * steps + i))
    middle = lambda pair: pl.BlockSpec((rows, LANES), lambda i, g: (0, PAIRS * i + pair))
    return pl.pallas_call(
        functools.partial(attend_back_kernel, slots),
        grid_spec=pltpu.PrefetchScalarGridSpec(
            num_scalar_prefetch=1,
            grid=(steps,),
            in_specs=[
                pl.BlockSpec(prompts.shape, lambda i, g: (0, 0)),
                pl.BlockSpec(gains.shape, lambda i, g: (0, 0)),
                pl.BlockSpec(memory_space=pltpu.HBM),
                block(0),
                block(1),
                block(2),
                block(0),
                block(0),
                pl.BlockSpec((1, GROUP_HEADS * slots, 1, LARGE), lambda i, g: (i, 0, 0, 0)),
            ]
            + [middle(pair) for pair in range(PAIRS)]
            + [block(0)],
            out_specs=[block(0)] * 3
            + [pl.BlockSpec((SLOT_ROWS, width), lambda i, g: (0, 0)), block(0)],
            scratch_shapes=[pltpu.VMEM((SLOT_ROWS, width), F32)] * 5
            + [pltpu.VMEM(w_qkv.shape, BF), pltpu.SemaphoreType.DMA],
        ),
        out_shape=[jax.ShapeDtypeStruct((rows, width), BF)] * 3
        + [
            jax.ShapeDtypeStruct((SLOT_ROWS, width), F32),
            jax.ShapeDtypeStruct((rows, width), BF),
        ],
        compiler_params=pltpu.CompilerParams(vmem_limit_bytes=VMEM_LIMIT),
        name="attend_back",
    )(
        size_group,
        prompts,
        gains,
        w_qkv,
        qkv,
        qkv,
        qkv,
        mixed_grad,
        mixed,
        totals,
        *[middle_grad] * PAIRS,
        passed,
    )


def feed_kernel(
    slots,
    chunk,
    groups,
    hidden,
    mixed,
    cotangent,
    gains,
    w_out,
    w_up,
    w_down,
    out_ref,
    middle_grad_ref,
    mixed_grad_ref,
):
    tile = hidden.shape[0]
    inner_width = w_up.shape[1]
    rows = pl.program_id(0) * tile + lax.broadcasted_iota(jnp.int32, (tile, 1), 0)
    live = rows < total_length(groups, slots)
    out_grad = jnp.where(live, cotangent[...].astype(F32), 0.0)
    out_grad_low = out_grad.astype(BF)
    middle = hidden[...] + dot(mixed[...], w_out[...])
    normal, rstd = norm_parts(middle)
    gain = gains[1:2]
    second = (normal * gain).astype(BF)
    forward = middle
    back = jnp.zeros_like(middle)
    for first in range(0, inner_width, chunk):
        part = slice(first, first + chunk)
        inner = dot(second, w_up[:, part])
        act_grad = dot(out_grad_low, w_down[part], NT)
        phi = 0.5 + 0.5 * lax.erf(inner * (0.5**0.5))
        density = jnp.exp2(inner * inner * (-0.5 * LOG2E)) * 0.3989422804014327
        activated = (inner * phi).astype(BF)
        inner_grad = (act_grad * (phi + inner * density)).astype(BF)
        forward = forward + dot(activated, w_down[part])
        back = back + dot(inner_grad, w_up[:, part], NT)
    out_ref[...] = jnp.where(live, forward, 0.0).astype(BF)
    middle_grad = out_grad + norm_back(normal, rstd, gain, back)
    middle_grad_ref[...] = middle_grad
    mixed_grad_ref[...] = dot(middle_grad.astype(BF), w_out[...], NT).astype(BF)


def feed(size_group, hidden, mixed, cotangent, gains, w_out, w_up, w_down):
    rows, width = hidden.shape
    tile = 384
    chunk = 512
    keep = lambda i, g: (0, 0)
    whole = lambda a: pl.BlockSpec(a.shape, keep, pipeline_mode=pl.Buffered(1))
    by_row = pl.BlockSpec((tile, width), lambda i, g: (i, 0))
    return pl.pallas_call(
        functools.partial(feed_kernel, size_group.shape[0], chunk),
        grid_spec=pltpu.PrefetchScalarGridSpec(
            num_scalar_prefetch=1,
            grid=(rows // tile,),
            in_specs=[by_row, by_row, by_row, whole(gains), whole(w_out), whole(w_up), whole(w_down)],
            out_specs=[by_row, by_row, by_row],
        ),
        out_shape=[
            jax.ShapeDtypeStruct((rows, width), BF),
            jax.ShapeDtypeStruct((rows, width), F32),
            jax.ShapeDtypeStruct((rows, width), BF),
        ],
        compiler_params=pltpu.CompilerParams(vmem_limit_bytes=VMEM_LIMIT),
        name="feed",
    )(size_group, hidden, mixed, cotangent, gains, w_out, w_up, w_down)


def gather_feed_kernel(
    planes,
    slots,
    chunk,
    groups,
    gains,
    hidden_in,
    mixed_in,
    cotangent_in,
    full_out,
    full_up,
    own_down,
    part_down,
    out_ref,
    middle_grad_ref,
    mixed_grad_ref,
    middle,
    mixed,
    cotangent,
    w_out,
    w_up,
    w_down,
    active,
    slope,
    send,
    recv,
    weights_in,
    rows_in,
    rows_out,
):
    d = lax.axis_index("dp")
    w = lax.axis_index("wide")
    down = Gather((d, w, planes, w // 2, lax.rem(w, 2)), 0, w_down, (send, recv), by_rows=True)
    barrier, greeted = down.greet(planes=False)
    others = planes - 1
    tiles = rows_in.shape[0]
    tile = middle.shape[0] // tiles
    inner_width = w_up.shape[1]

    def tile_rows(index):
        return pl.ds(pl.multiple_of(index * tile, tile), tile)

    def loads(index):
        part = tile_rows(index)
        return [
            pltpu.make_async_copy(hidden_in.at[part], middle.at[part], rows_in.at[index, 0]),
            pltpu.make_async_copy(mixed_in.at[part], mixed.at[part], rows_in.at[index, 1]),
            pltpu.make_async_copy(cotangent_in.at[part], cotangent.at[part], rows_in.at[index, 2]),
        ]

    def stores(index):
        part = tile_rows(index)
        return [
            pltpu.make_async_copy(middle.at[part], middle_grad_ref.at[part], rows_out.at[index, 0]),
            pltpu.make_async_copy(mixed.at[part], mixed_grad_ref.at[part], rows_out.at[index, 1]),
            pltpu.make_async_copy(cotangent.at[part], out_ref.at[part], rows_out.at[index, 2]),
        ]

    down_loads = [(own_down, down.shard(down.plane, down.core))]
    for k in range(others):
        for part in (0, 1):
            down_loads.append((down.fetched(k, part, part_down), down.fetched(k, part)))
    down_loads = [
        pltpu.make_async_copy(source, target, weights_in.at[2 + index])
        for index, (source, target) in enumerate(down_loads)
    ]
    out_load = pltpu.make_async_copy(full_out, w_out, weights_in.at[0])
    up_load = pltpu.make_async_copy(full_up, w_up, weights_in.at[1])
    for copy in down_loads:
        copy.start()
    out_load.start()
    for copy in loads(0):
        copy.start()
    up_load.start()
    for index in range(1, tiles):
        for copy in loads(index):
            copy.start()
    for copy in down_loads:
        copy.wait()
    pl.semaphore_wait(barrier, greeted)
    for k in range(others):
        down.exchange(down.nearest(k))
    down.give(down.plane)
    out_load.wait()
    gain = gains[1:2]

    def pump(step):
        @pl.when((step >= 0) & (step < others))
        def _():
            down.pass_on(step, 0)
            down.pass_on(step, 1)

        @pl.when((step >= 2) & (step < others + 2))
        def _():
            down.close(step - 2)

    def up_tile(index, carry):
        for copy in loads(index):
            copy.wait()
        part = tile_rows(index)
        value = middle[part, :] + dot(mixed[part, :], w_out[...])
        middle[part, :] = value
        normal, _ = norm_parts(value)
        second = (normal * gain).astype(BF)
        pl.when(index == 0)(up_load.wait)
        for first in range(0, inner_width, chunk):
            columns = slice(first, first + chunk)
            inner = dot(second, w_up[:, columns])
            phi = 0.5 + 0.5 * lax.erf(inner * (0.5**0.5))
            density = jnp.exp2(inner * inner * (-0.5 * LOG2E)) * 0.3989422804014327
            active[part, columns] = (inner * phi).astype(BF)
            slope[part, columns] = phi + inner * density
            if first + chunk == inner_width // 2:
                pump(2 * index)
        pump(2 * index + 1)
        return carry

    lax.fori_loop(0, tiles, up_tile, 0)
    for step in range(2 * tiles, others + 2):
        pump(step)
    down.wait_all_given()
    total = total_length(groups, slots)

    def down_tile(index, carry):
        part = tile_rows(index)
        rows = index * tile + lax.broadcasted_iota(jnp.int32, (tile, 1), 0)
        live = rows < total
        out_grad = jnp.where(live, cotangent[part, :].astype(F32), 0.0)
        out_grad_low = out_grad.astype(BF)
        value = middle[part, :]
        back = jnp.zeros_like(value)
        for first in range(0, inner_width, chunk):
            columns = slice(first, first + chunk)
            act_grad = dot(out_grad_low, w_down[columns], NT)
            inner_grad = (act_grad * slope[part, columns]).astype(BF)
            back = back + dot(inner_grad, w_up[:, columns], NT)
        forward = value + dot(active[part, :], w_down[...])
        cotangent[part, :] = jnp.where(live, forward, 0.0).astype(BF)
        normal, rstd = norm_parts(value)
        middle_grad = out_grad + norm_back(normal, rstd, gain, back)
        middle[part, :] = middle_grad
        mixed[part, :] = dot(middle_grad.astype(BF), w_out[...], NT).astype(BF)
        for copy in stores(index):
            copy.start()
        return carry

    lax.fori_loop(0, tiles, down_tile, 0)
    down.wait_passed()
    for index in range(tiles):
        for copy in stores(index):
            copy.wait()


def gather_feed(axes, size_group, hidden, mixed, cotangent, gains, w_out, w_up, w_down, part_down):
    rows, width = hidden.shape
    planes = axes["wide"] // 2
    inner_width = w_up.shape[1]
    tiles = 3
    hbm = pl.BlockSpec(memory_space=pltpu.HBM)
    dma = pltpu.SemaphoreType.DMA
    count = Gather.semaphores(planes)
    return pl.pallas_call(
        functools.partial(gather_feed_kernel, planes, size_group.shape[0], 768),
        in_specs=[
            pl.BlockSpec(memory_space=pltpu.SMEM),
            pl.BlockSpec(memory_space=pltpu.VMEM),
        ]
        + [hbm] * 7,
        out_specs=[hbm] * 3,
        out_shape=[
            jax.ShapeDtypeStruct((rows, width), BF),
            jax.ShapeDtypeStruct((rows, width), F32),
            jax.ShapeDtypeStruct((rows, width), BF),
        ],
        scratch_shapes=[
            pltpu.VMEM((rows, width), F32),
            pltpu.VMEM((rows, width), BF),
            pltpu.VMEM((rows, width), BF),
            pltpu.VMEM(w_out.shape, BF),
            pltpu.VMEM(w_up.shape, BF),
            pltpu.VMEM((inner_width, width), BF),
            pltpu.VMEM((rows, inner_width), BF),
            pltpu.VMEM((rows, inner_width), F32),
            dma((1, count)),
            dma((1, count)),
            dma((3 + 2 * (planes - 1),)),
            dma((tiles, 3)),
            dma((tiles, 3)),
        ],
        compiler_params=pltpu.CompilerParams(
            collective_id=2, has_side_effects=True, vmem_limit_bytes=VMEM_LIMIT
        ),
        name="gather_feed",
    )(size_group, gains, hidden, mixed, cotangent, w_out, w_up, w_down, part_down)


class Shared:
    def __init__(self, dp, wide, mine, near, far, result, sems):
        self.members = 2 * dp
        self.planes = wide // 2
        self.rows = mine.shape[1]
        self.d = lax.axis_index("dp")
        w = lax.axis_index("wide")
        self.plane = w // 2
        self.core = lax.rem(w, 2)
        self.member = self.d * 2 + self.core
        self.mine, self.near, self.far, self.result = mine, near, far, result
        self.send, self.near_in, self.far_in, self.last_in = sems

    def peer(self, step):
        other = lax.rem(self.member + step, self.members)
        return other, (other // 2, self.plane * 2 + lax.rem(other, 2))

    def plane_peer(self, step):
        other = lax.rem(self.plane + step, self.planes)
        return other, (self.d, other * 2 + self.core)

    def greet(self):
        barrier = pltpu.get_barrier_semaphore()
        for step in range(1, self.members):
            pl.semaphore_signal(barrier, inc=1, device_id=self.peer(step)[1], device_id_type=MESH)
        for step in range(1, self.planes):
            pl.semaphore_signal(
                barrier, inc=1, device_id=self.plane_peer(step)[1], device_id_type=MESH
            )
        return barrier, self.members + self.planes - 2

    def part(self, ref, index):
        return ref.at[pl.ds(pl.multiple_of(index * self.rows, self.rows), self.rows)]

    def copy(self, source, target, send, recv, device):
        return pltpu.make_async_remote_copy(
            source, target, send, recv, device_id=device, device_id_type=MESH
        )

    def first(self, step):
        other, device = self.peer(step)
        return self.copy(
            self.mine.at[other],
            self.near.at[step],
            self.send.at[0, step],
            self.near_in.at[step],
            device,
        )

    def second(self, step):
        mine = self.far.at[self.plane]
        device = self.plane_peer(step)[1]
        return self.copy(mine, mine, self.send.at[1, step], self.far_in.at[step], device)

    def third(self, step):
        mine = self.part(self.result, self.member)
        device = self.peer(step)[1]
        return self.copy(mine, mine, self.send.at[2, step], self.last_in.at[step], device)

    def start_first(self):
        for step in range(1, self.members):
            self.first(step).start()
        self.near[0] = self.mine[self.member]

    def start_second(self):
        for step in range(1, self.members):
            self.first(step).wait_recv()
        total = jnp.zeros(self.near.shape[1:], F32)
        for index in range(self.members):
            place = lax.rem(self.member - index + self.members, self.members)
            total = total + self.near[place].astype(F32)
        self.far[self.plane] = total.astype(BF)
        for step in range(1, self.planes):
            self.second(step).start()

    def start_third(self):
        for step in range(1, self.planes):
            self.second(step).wait_recv()
        total = jnp.zeros(self.near.shape[1:], F32)
        for index in range(self.planes):
            total = total + self.far[index].astype(F32)
        self.part(self.result, self.member)[...] = total
        for step in range(1, self.members):
            self.third(step).start()

    def end(self):
        for step in range(1, self.members):
            self.third(step).wait_recv()
        for step in range(1, self.members):
            self.first(step).wait_send()
            self.third(step).wait_send()
        for step in range(1, self.planes):
            self.second(step).wait_send()


def finish_kernel(
    dp,
    wide,
    slots,
    groups,
    prompts,
    gains,
    prompt_terms,
    hidden_in,
    middle_grad_in,
    dq_in,
    dk_in,
    dv_in,
    w_qkv_in,
    input_grad,
    prompt_grad,
    penalty,
    hidden,
    middle_grad,
    dq,
    dk,
    dv,
    w_qkv,
    mine,
    near,
    far,
    result,
    send,
    near_in,
    far_in,
    last_in,
    weight_in,
    rows_in,
):
    shared = Shared(dp, wide, mine, near, far, result, (send, near_in, far_in, last_in))
    barrier, greeted = shared.greet()
    tiles = rows_in.shape[0]
    width = hidden.shape[1]
    tile = hidden.shape[0] // tiles
    weight_load = pltpu.make_async_copy(w_qkv_in, w_qkv, weight_in)
    weight_load.start()

    def tile_rows(index):
        return pl.ds(pl.multiple_of(index * tile, tile), tile)

    def loads(index):
        part = tile_rows(index)
        pairs = (
            (dq_in, dq),
            (dk_in, dk),
            (dv_in, dv),
            (hidden_in, hidden),
            (middle_grad_in, middle_grad),
        )
        return [
            pltpu.make_async_copy(source.at[part], target.at[part], rows_in.at[index, number])
            for number, (source, target) in enumerate(pairs)
        ]

    for index in range(tiles):
        for copy in loads(index):
            copy.start()

    slot_row = lax.broadcasted_iota(jnp.int32, (SLOT_ROWS, 1), 0)
    shifted = total_length(groups, slots) + lax.broadcasted_iota(jnp.int32, (1, width), 1)
    shares = jnp.zeros((1, width), F32)
    for least in range(width, hidden.shape[0] + width, width):
        shares = shares + jnp.where(shifted >= least, 1.0, 0.0)
    terms = jnp.where(slot_row < PROMPTS, prompt_terms[...], jnp.where(slot_row == PROMPTS, shares, 0.0))
    for member in range(mine.shape[0]):
        mine[member] = terms[member * mine.shape[1] : (member + 1) * mine.shape[1]].astype(BF)
    pl.semaphore_wait(barrier, greeted)
    shared.start_first()
    weight_load.wait()

    def row_tile(index, carry):
        for copy in loads(index):
            copy.wait()
        part = tile_rows(index)
        normal, rstd = norm_parts(hidden[part, :])
        normed_grad = back_through_qkv(dq[part, :], dk[part, :], dv[part, :], w_qkv)
        hidden_grad = middle_grad[part, :] + norm_back(normal, rstd, gains[0:1], normed_grad)
        prompt_slot, live = row_places(groups, slots, index * tile, tile)
        input_grad[part, :] = jnp.where(live & (prompt_slot < 0), hidden_grad, 0.0).astype(BF)
        pl.when(index == 0)(shared.start_second)
        pl.when(index == 1)(shared.start_third)
        return carry

    lax.fori_loop(0, tiles, row_tile, 0)
    shared.end()
    given = prompts[...]
    size = given.shape[0] * given.shape[1]
    count = jnp.sum(result[PROMPTS : PROMPTS + 1], axis=1, keepdims=True)
    prompt_grad[...] = result[:PROMPTS] + (2.0 * PENALTY_RATE / size) * count * given
    square = jnp.sum(jnp.sum(given * given, axis=1, keepdims=True), axis=0, keepdims=True)
    penalty[...] = PENALTY_RATE * count * (square / size)


def finish(axes, size_group, prompts, gains, terms, hidden, middle_grad, dq, dk, dv, w_qkv):
    rows, width = hidden.shape
    dp, wide = axes["dp"], axes["wide"]
    members, planes = 2 * dp, wide // 2
    tiles = 3
    dma = pltpu.SemaphoreType.DMA
    vmem = pl.BlockSpec(memory_space=pltpu.VMEM)
    hbm = pl.BlockSpec(memory_space=pltpu.HBM)
    input_grad, prompt_grad, penalty = pl.pallas_call(
        functools.partial(finish_kernel, dp, wide, size_group.shape[0]),
        in_specs=[pl.BlockSpec(memory_space=pltpu.SMEM)] + [vmem] * 3 + [hbm] * 6,
        out_specs=[vmem, vmem, vmem],
        out_shape=[
            pltpu.VMEM((rows, width), BF),
            pltpu.VMEM(prompts.shape, F32),
            jax.ShapeDtypeStruct((1, 1), F32),
        ],
        scratch_shapes=[
            pltpu.VMEM((rows, width), F32),
            pltpu.VMEM((rows, width), F32),
            pltpu.VMEM((rows, width), BF),
            pltpu.VMEM((rows, width), BF),
            pltpu.VMEM((rows, width), BF),
            pltpu.VMEM(w_qkv.shape, BF),
            pltpu.VMEM((members, SLOT_ROWS // members, width), BF),
            pltpu.VMEM((members, SLOT_ROWS // members, width), BF),
            pltpu.VMEM((planes, SLOT_ROWS // members, width), BF),
            pltpu.VMEM((SLOT_ROWS, width), F32),
            dma((3, max(members, planes))),
            dma((members,)),
            dma((planes,)),
            dma((members,)),
            dma,
            dma((tiles, 5)),
        ],
        compiler_params=pltpu.CompilerParams(
            collective_id=1, has_side_effects=True, vmem_limit_bytes=VMEM_LIMIT - (2 << 20)
        ),
        name="finish",
    )(size_group, prompts, gains, terms, hidden, middle_grad, dq, dk, dv, w_qkv)
    return input_grad, prompt_grad, penalty[0, 0]


def shards(
    axes,
    tokens,
    pos_index,
    size_group,
    pos_table,
    prompts,
    norm_gains,
    w_qkv,
    w_out,
    w_up,
    w_down,
    cotangent,
):
    if can_gather(axes, w_qkv, w_out, w_up, w_down):
        hidden, qkv, full_qkv, full_out, full_up, part_down = gather_embed(
            axes,
            size_group,
            tokens,
            pos_index,
            pos_table,
            prompts,
            norm_gains,
            w_qkv,
            w_out,
            w_up,
            w_down,
        )
        mixed, totals = attend(size_group, qkv)
        outputs, middle_grad, mixed_grad = gather_feed(
            axes,
            size_group,
            hidden,
            mixed,
            cotangent,
            norm_gains,
            full_out,
            full_up,
            w_down,
            part_down,
        )
    else:
        full_qkv = lax.all_gather(w_qkv, "wide", axis=0, tiled=True)
        full_out = lax.all_gather(w_out, "wide", axis=0, tiled=True)
        full_up = lax.all_gather(w_up, "wide", axis=0, tiled=True)
        full_down = lax.all_gather(w_down, "wide", axis=0, tiled=True)
        hidden, qkv = embed(size_group, tokens, pos_index, pos_table, prompts, norm_gains, full_qkv)
        mixed, totals = attend(size_group, qkv)
        outputs, middle_grad, mixed_grad = feed(
            size_group, hidden, mixed, cotangent, norm_gains, full_out, full_up, full_down
        )
    dq, dk, dv, terms, outputs = attend_back(
        size_group,
        prompts,
        norm_gains,
        full_qkv,
        qkv,
        mixed_grad,
        mixed,
        totals,
        middle_grad,
        outputs,
    )
    input_grad, prompt_grad, penalty = finish(
        axes, size_group, prompts, norm_gains, terms, hidden, middle_grad, dq, dk, dv, full_qkv
    )
    return (outputs, input_grad, prompt_grad, penalty)


def solution(mesh):
    return jax.shard_map(
        functools.partial(shards, dict(mesh.shape)),
        mesh=mesh,
        in_specs=(
            P(("dp", "wide"), None),
            P(("dp", "wide"), None),
            P(("dp", "wide")),
            P(),
            P(),
            P(),
            P("wide", None),
            P("wide", None),
            P("wide", None),
            P("wide", None),
            P(("dp", "wide"), None),
        ),
        out_specs=(P(("dp", "wide"), None), P(("dp", "wide"), None), P(), P()),
        check_vma=False,
    )
```
